128 devices in a mesh: outer: 16 (over y, x), inner: 8 (over z, core).
Axes of the slice: x: 4, y: 4, z: 4, core: 2. Of those that a mesh axis runs over, the one named last changes fastest.
Arguments:
- world_shocks: float32 [256, 2, 128], P('outer'), may hold values from -6 to 6
- short_rate: float32 [256, 2], P('outer'), may hold values from 0 to 0.06
- inner_shocks: float32 [2, 128, 16384], P(None, 'outer', 'inner'), may hold values from -12 to 12
- fund_volatility: float32 [128], P('outer'), may hold values from 0.08 to 0.25
- fund_index: int32 [256, 4], P('outer'), may hold values from 0 to 127
- allocation: float32 [256, 4], P('outer'), may hold values from 0.1 to 1
- guarantee_type: int32 [256], P('outer'), may hold values from 0 to 1
- maturity: int32 [256], P('outer'), may hold values from 1 to 64
- guarantee_ratio: float32 [256], P('outer'), may hold values from 0.7 to 1.4
- fee_rate: float32 [256], P('outer'), may hold values from 0.005 to 0.03
- mortality: float32 [256], P('outer'), may hold values from 0.004 to 0.05
- account: float32 [256], P('outer'), may hold values from 1 to 8
Outputs:
- reserve: float32 [256, 2, 256], P(('outer', 'inner'))
- reserve_rho: float32 [256, 2, 256], P(('outer', 'inner'))
- fund_delta: float32 [256, 2, 128], P(('outer', 'inner'))
The draws below stay inside these ranges and needn't reach their ends.
All inputs are finite; a program needn't handle non-finite values.
Results may differ from the reference program's by a relative error of at most 0.0025.
Values may be sent and summed in bfloat16 or wider, within the bound.
A program may use at most 64 MiB of HBM per device.

```python
import math
import jax
import jax.numpy as jnp
from jax import lax

FUNDS = 128
COHORTS = 256
PICKS = 4
STEPS = 64
INNER = 256
OUTER = 256


def draw_inner_shocks(key, part):
    key_steady, key_own, key_shared = jax.random.split(key, 3)
    steady = jax.random.normal(key_steady, (2, FUNDS, INNER, STEPS), jnp.float32)
    own_level = jax.random.normal(key_own, (2, FUNDS, INNER, STEPS + 1), jnp.float32)
    shared_level = jax.random.normal(key_shared, (2, FUNDS, 1, STEPS + 1), jnp.float32)
    combined = 0.6 * steady + 2.5 * (own_level[..., 1:] - own_level[..., :-1]) + 1.5 * (shared_level[..., 1:] - shared_level[..., :-1])
    clipped = jnp.clip(combined, -12.0, 12.0)
    return clipped.reshape(2, FUNDS, INNER * STEPS)


def touch_ends(entries, stream_key, low, largest):
    spot = [jax.random.randint(jax.random.fold_in(stream_key, axis), (), 0, length) for axis, length in enumerate(entries.shape)]
    longest = entries.shape.index(max(entries.shape))
    neighbour = spot[:longest] + [(spot[longest] + 1) % entries.shape[longest]] + spot[longest + 1:]
    return entries.at[tuple(spot)].set(low).at[tuple(neighbour)].set(largest)


def level_of(own_key, shape, cuts, low, high):
    gain = 1.0
    for position, parts in cuts:
        steps = jax.random.uniform(jax.random.fold_in(jax.random.fold_in(own_key, 6), position), (parts,), jnp.float32, low / len(cuts), high / len(cuts))
        gain = gain * jnp.repeat(jnp.exp(steps), shape[position] // parts).reshape((-1,) + (1,) * (len(shape) - 1 - position))
    return gain


def centred(own_key, dims, scale, bound, cuts=(), kind=jnp.bfloat16):
    values = scale * jax.random.normal(own_key, dims, jnp.float32)
    if cuts:
        values = values * level_of(own_key, dims, cuts, -0.22, 0.18)
    return jnp.clip(values, -bound, bound).astype(kind)


def setup_inputs(seed: int = 0) -> dict:
    streams_of = jax.random.split(jax.random.key(seed), 13)
    return {
        "world_shocks": centred(streams_of[0], (OUTER, 2, FUNDS), 1.0, 6.0, ((0, 16),), jnp.float32),
        "short_rate": jnp.clip(0.06 * jax.random.uniform(streams_of[1], (OUTER, 2), jnp.float32) ** level_of(streams_of[1], (OUTER, 2), ((0, 16),), -0.2, 0.2), 0.0, 0.06),
        "inner_shocks": draw_inner_shocks(jax.random.fold_in(streams_of[12], 71), 0),
        "fund_volatility": jnp.clip(jnp.exp(math.log(0.25) - 1.1394343 * jax.random.uniform(streams_of[3], (FUNDS,), jnp.float32) ** level_of(streams_of[3], (FUNDS,), ((0, 16),), -0.2, 0.2)), 0.08, 0.25),
        "fund_index": touch_ends(jax.random.randint(streams_of[4], (COHORTS, PICKS), 0, FUNDS), jax.random.fold_in(streams_of[4], 1), 0, FUNDS - 1).astype(jnp.int32),
        "allocation": jnp.clip(0.1 + 0.9 * jax.random.uniform(streams_of[5], (COHORTS, PICKS), jnp.float32) ** level_of(streams_of[5], (COHORTS, PICKS), ((0, 16),), -0.2, 0.2), 0.1, 1.0),
        "guarantee_type": touch_ends(jax.random.randint(streams_of[6], (COHORTS,), 0, 2), jax.random.fold_in(streams_of[6], 1), 0, 1).astype(jnp.int32),
        "maturity": touch_ends(jax.random.randint(streams_of[7], (COHORTS,), 1, STEPS + 1), jax.random.fold_in(streams_of[7], 1), 1, STEPS).astype(jnp.int32),
        "guarantee_ratio": jnp.clip(0.7 + 0.7 * jax.random.uniform(streams_of[8], (COHORTS,), jnp.float32) ** level_of(streams_of[8], (COHORTS,), ((0, 16),), -0.2, 0.2), 0.7, 1.4),
        "fee_rate": jnp.clip(0.005 + 0.024999999 * jax.random.uniform(streams_of[9], (COHORTS,), jnp.float32) ** level_of(streams_of[9], (COHORTS,), ((0, 16),), -0.2, 0.2), 0.005, 0.03),
        "mortality": jnp.clip(jnp.exp(math.log(0.05) - 2.5257286 * jax.random.uniform(streams_of[10], (COHORTS,), jnp.float32) ** level_of(streams_of[10], (COHORTS,), ((0, 16),), -0.2, 0.2)), 0.004, 0.05),
        "account": jnp.clip(jnp.exp(math.log(8.0) - 2.0794415 * jax.random.uniform(streams_of[11], (COHORTS,), jnp.float32) ** level_of(streams_of[11], (COHORTS,), ((0, 16),), -0.2, 0.2)), 1.0, 8.0),
    }


drift_rate = 0.06
smooth_width = 0.05

def make_factor(shocks, sigmas, horizon):
    month_count, fund_count, flat = shocks.shape
    step_count = horizon.shape[0]
    paths = flat // step_count
    running = jnp.cumsum(shocks.reshape(month_count, fund_count, paths, step_count), axis=3)
    spread = sigmas[None, :, None, None]
    exponent = -0.5 * spread * spread * horizon[None, None, None, :] + spread * running
    return jnp.exp(exponent).astype(jnp.bfloat16).reshape(month_count, fund_count, flat)

def weight_table(fund_index, allocation, fund_count):
    share = allocation / lax.optimization_barrier(jnp.sum(allocation, axis=1, keepdims=True))
    picks = (fund_index[:, :, None] == jnp.arange(fund_count, dtype=jnp.int32)[None, None, :]).astype(jnp.float32)
    return lax.optimization_barrier(jnp.sum(share[:, :, None] * picks, axis=1))

def decrements(mortality, maturity, guarantee_type, horizon_int, horizon):
    keep = 1.0 - mortality
    survive = jnp.power(keep[:, None], horizon[None, :] - 1.0)
    inside = (horizon_int[None, :] <= maturity[:, None]).astype(jnp.float32)
    death = mortality[:, None] * survive * inside
    at_end = (horizon_int[None, :] == maturity[:, None]).astype(jnp.float32)
    ending = jnp.power(keep, maturity.astype(jnp.float32))[:, None] * at_end
    return jnp.where(guarantee_type[:, None] == 0, death, ending)

def fund_levels(world_shocks, sigmas):
    spread = sigmas[None, None, :]
    monthly = (drift_rate - 0.5 * spread * spread) / 12.0 + spread * world_shocks / math.sqrt(12.0)
    return jnp.exp(jnp.cumsum(monthly, axis=1))

def reference(world_shocks, short_rate, inner_shocks, fund_volatility, fund_index, allocation, guarantee_type, maturity, guarantee_ratio, fee_rate, mortality, account):
    horizon_int = jnp.arange(1, STEPS + 1, dtype=jnp.int32)
    horizon = horizon_int.astype(jnp.float32)
    flat_factor = make_factor(inner_shocks, fund_volatility, horizon)
    weights = weight_table(fund_index, allocation, FUNDS)
    decay = decrements(mortality, maturity, guarantee_type, horizon_int, horizon)
    levels = fund_levels(world_shocks, fund_volatility)
    width = smooth_width * account[:, None, None]
    strike = (guarantee_ratio * account)[:, None, None]
    fee_decay = jnp.exp(-fee_rate[:, None] * horizon[None, :]) * decay
    delta_weights = weights * account[:, None]

    def one_path(item):
        path_levels, path_rates = item
        reserves, rhos, deltas = ([], [], [])
        for month_index in range(2):
            month_factor = flat_factor[month_index]
            rate = path_rates[month_index]
            weighted = (weights * path_levels[month_index][None, :]).astype(jnp.bfloat16)
            sums = jnp.dot(weighted, month_factor, preferred_element_type=jnp.float32).reshape(COHORTS, INNER, STEPS)
            growth = jnp.exp((rate - fee_rate)[:, None] * horizon[None, :])
            balance = account[:, None, None] * growth[:, None, :] * sums
            scaled = (strike - balance) / width
            payoff = width * jax.nn.softplus(scaled)
            slope = jax.nn.sigmoid(scaled)
            weight_t = decay * jnp.exp(-rate * horizon)[None, :]
            reserves.append(lax.optimization_barrier(jnp.sum(weight_t[:, None, :] * payoff, axis=(1, 2))) / INNER)
            rhos.append(-lax.optimization_barrier(jnp.sum((horizon[None, :] * weight_t)[:, None, :] * (payoff + slope * balance), axis=(1, 2))) / INNER)
            kernel = (fee_decay[:, None, :] * slope).astype(jnp.bfloat16).reshape(COHORTS, INNER * STEPS)
            sens = jnp.dot(kernel, month_factor.T, preferred_element_type=jnp.float32)
            deltas.append(-lax.optimization_barrier(jnp.sum(delta_weights * sens, axis=0)) / INNER)
        return (jnp.stack(reserves), jnp.stack(rhos), jnp.stack(deltas))
    reserve, reserve_rho, fund_delta = lax.map(one_path, (levels, short_rate))
    return (reserve, reserve_rho, fund_delta)
```

```python
import functools
import math

import jax
import jax.numpy as jnp
from jax import lax
from jax.experimental import pallas as pl
from jax.experimental.pallas import tpu as pltpu
from jax.sharding import PartitionSpec as P

MESH = pl.DeviceIdType.MESH
HIGHEST = lax.Precision.HIGHEST
F32, BF16 = jnp.float32, jnp.bfloat16

STEPS = 64
DRIFT = 0.06
SMOOTH = 0.05
NOUT = 16
NIN = 8
TILES = 32
GROUPS = 16
TYPE, MAT, RATIO, FEE, MORT, ACC, SIG, KEY = 8, 9, 10, 11, 12, 13, 14, 15
SLAB = 24


def dot(a, b, dims=((1,), (0,)), precision=None):
    return lax.dot_general(
        a, b, (dims, ((), ())), precision=precision, preferred_element_type=F32
    )


def iota(shape, dim):
    return lax.broadcasted_iota(jnp.int32, shape, dim)


def factor_kernel(shocks_ref, sigma_ref, out_ref):
    rows = jnp.concatenate(
        [shocks_ref[m, :, 128 * j : 128 * j + 128] for m in range(2) for j in range(16)],
        axis=0,
    )
    src, dst = iota((128, 128), 0), iota((128, 128), 1)
    upper = ((src // 64 == dst // 64) & (src <= dst)).astype(F32)
    running = dot(rows, upper, precision=HIGHEST)
    sigma = sigma_ref[...]
    sigma = jnp.broadcast_to(sigma[None], (32, 8, 1)).reshape(256, 1)
    horizon = (iota((1, 128), 1) % 64 + 1).astype(F32)
    factor = jnp.exp(-0.5 * sigma * sigma * horizon + sigma * running)
    lane = iota((8, 128), 1)
    months = []
    for m in range(2):
        regs = [factor[(m * 16 + j) * 8 : (m * 16 + j) * 8 + 8] for j in range(16)]
        for bit in range(4):
            low = (lane // (4 << bit)) % 2 == 0
            step = 4 << bit
            fresh = list(regs)
            for j in range(16):
                if j >> bit & 1:
                    continue
                k = j | 1 << bit
                a, b = regs[j], regs[k]
                fresh[j] = jnp.where(low, a, pltpu.roll(b, step, 1))
                fresh[k] = jnp.where(low, pltpu.roll(a, 128 - step, 1), b)
            regs = fresh
        months.append(regs)
    for g in range(16):
        both = jnp.concatenate([months[0][g], months[1][g]], axis=0)
        out_ref[:, 128 * g : 128 * g + 128] = both.astype(BF16)


def own_factor(shocks, sigma):
    return pl.pallas_call(
        factor_kernel,
        out_shape=jax.ShapeDtypeStruct((16, 2048), BF16),
        name="own_factor",
    )(shocks, sigma)


def gather_kernel(block_ref, table_ref, blocks_ref, tables_ref, send, recv, own):
    me = lax.axis_index("outer")
    barrier = pltpu.get_barrier_semaphore()
    for d in range(1, NOUT):
        pl.semaphore_signal(
            barrier, inc=1, device_id={"outer": lax.rem(me + d, NOUT)}, device_id_type=MESH
        )
    pl.semaphore_wait(barrier, NOUT - 1)
    copies = []
    for d in range(1, NOUT):
        peer = lax.rem(me + d, NOUT)
        for n, (src, dst) in enumerate(((table_ref, tables_ref), (block_ref, blocks_ref))):
            copy = pltpu.make_async_remote_copy(
                src_ref=src,
                dst_ref=dst.at[me],
                send_sem=send.at[n, d],
                recv_sem=recv.at[n, d],
                device_id={"outer": peer},
                device_id_type=MESH,
            )
            copy.start()
            copies.append(copy)
    mine = [
        pltpu.make_async_copy(table_ref, tables_ref.at[me], own.at[0]),
        pltpu.make_async_copy(block_ref, blocks_ref.at[me], own.at[1]),
    ]
    for copy in mine:
        copy.start()
    for copy in mine:
        copy.wait()
    for copy in copies:
        copy.wait()


def gather_outer(block, table):
    vmem = pl.BlockSpec(memory_space=pltpu.VMEM)
    anywhere = pl.BlockSpec(memory_space=pl.ANY)
    return pl.pallas_call(
        gather_kernel,
        out_shape=(
            jax.ShapeDtypeStruct((NOUT, 16, 2048), BF16),
            jax.ShapeDtypeStruct((NOUT, 16, 128), F32),
        ),
        in_specs=[vmem, vmem],
        out_specs=(anywhere, anywhere),
        scratch_shapes=[
            pltpu.SemaphoreType.DMA((2, NOUT)),
            pltpu.SemaphoreType.DMA((2, NOUT)),
            pltpu.SemaphoreType.DMA((2,)),
        ],
        compiler_params=pltpu.CompilerParams(collective_id=0, has_side_effects=True),
        name="gather_outer",
    )(block, table)


def value_kernel(
    blocks_ref,
    tables_ref,
    world_ref,
    rate_ref,
    out_ref,
    fmat,
    fmat_t,
    level,
    weight_t,
    dwt,
    delta,
    table,
    bounds_v,
    bounds,
    res_acc,
    sens,
    sem,
):
    for g in range(GROUPS):
        cols = slice(128 * g, 128 * g + 128)
        part = blocks_ref[:, :, cols].astype(F32).reshape(16, 2, 8, 128)
        for m in range(2):
            one = part[:, m].reshape(128, 128)
            fmat[m, :, cols] = one.astype(BF16)
        fmat_t[cols, :] = part.reshape(256, 128).T.astype(BF16)

    params = tables_ref[...].reshape(256, 128)
    params_t = params.T[:16]
    key_col, key_row = params[:, KEY : KEY + 1], params_t[KEY : KEY + 1]
    rank_col = jnp.sum((key_row < key_col).astype(F32), axis=1, keepdims=True)
    rank_row = jnp.sum((key_col < key_row).astype(F32), axis=0, keepdims=True)
    place = (rank_col == iota((256, 256), 1).astype(F32)).astype(F32)
    ordered = dot(params_t, place, precision=HIGHEST)
    table[0] = ordered[:, :128]
    table[1] = ordered[:, 128:]
    mat = ordered[MAT : MAT + 1]
    first = jnp.where(ordered[TYPE : TYPE + 1] == 0.0, 1.0, mat)
    tile_of = iota((TILES, 256), 1) // 8 == iota((TILES, 256), 0)
    low = jnp.min(jnp.where(tile_of, first, 1e3), axis=1, keepdims=True)
    high = jnp.max(jnp.where(tile_of, mat, 0.0), axis=1, keepdims=True)
    low = (low.astype(jnp.int32) - 1) // 4
    high = (high.astype(jnp.int32) - 1) // 4 + 1
    bounds_v[...] = jnp.where(iota((TILES, 128), 1) == 0, low, high)
    copy = pltpu.make_async_copy(bounds_v, bounds, sem)
    copy.start()

    spread_o = (iota((16, 128), 1) % 16 == iota((16, 128), 0)).astype(F32)
    sigma = params[:, SIG : SIG + 1].reshape(16, 2, 8, 1)[:, 0].reshape(128, 1)
    total = jnp.zeros((128, 128), F32)
    rates = []
    for m in range(2):
        shock = dot(world_ref[m], spread_o, ((0,), (0,)), HIGHEST)
        total = total + (
            (DRIFT - 0.5 * sigma * sigma) / 12.0 + sigma * shock / math.sqrt(12.0)
        )
        level[m] = jnp.exp(total)
        rate = jnp.sum(rate_ref[:, m : m + 1] * spread_o, axis=0, keepdims=True)
        rates.append(jnp.broadcast_to(rate, (8, 128)))
        delta[m] = jnp.zeros((128, 128), F32)
    copy.wait()

    fund = iota((128, 128), 0).astype(F32)
    step_in = iota((8, 128), 0) % 4

    def tile(j, carry):
        where = 8 * lax.rem(j, 16) + iota((16, 128), 1) // 16
        rows = jnp.take_along_axis(table[j // 16], where, axis=1)

        def row(k):
            return rows[k : k + 1]

        share_sum = row(4) + row(5) + row(6) + row(7)
        wts = jnp.zeros((128, 128), F32)
        for k in range(4):
            wts = wts + jnp.where(fund == row(k), row(4 + k) / share_sum, 0.0)
        dwt[...] = wts * row(ACC)
        zero = jnp.zeros((16, 8, 128), F32)
        for m in range(2):
            one = (wts * level[m]).reshape(16, 8, 128)
            both = [one, zero] if m == 0 else [zero, one]
            both = jnp.stack(both, axis=1).reshape(256, 128)
            weight_t[:, 128 * m : 128 * m + 128] = both.astype(BF16)
            sens[m] = jnp.zeros((128, 128), F32)

        def wide(value):
            return jnp.broadcast_to(value, (8, 128))

        death = row(TYPE) == 0.0
        mat = row(MAT)
        log_keep = jnp.log(1.0 - row(MORT))
        first = wide(jnp.where(death, 1.0, mat))
        last = wide(mat)
        amp = wide(jnp.where(death, row(MORT), 1.0))
        slope_d = wide(jnp.where(death, log_keep, 0.0))
        shift_d = wide(jnp.where(death, -log_keep, log_keep * mat))
        fee = wide(row(FEE))
        strike = wide(row(RATIO) * (1.0 / SMOOTH))

        def group(g, sums):
            hz = (step_in + (4 * g + 1)).astype(F32)
            decay = jnp.where(
                (hz >= first) & (hz <= last), amp * jnp.exp(slope_d * hz + shift_d), 0.0
            )
            fee_decay = jnp.exp(-fee * hz) * decay
            here = pl.ds(pl.multiple_of(g * 128, 128), 128)
            raw = dot(fmat_t[here, :], weight_t[...])
            fresh = []
            for m in range(2):
                growth = jnp.exp((rates[m] - fee) * hz) * (1.0 / SMOOTH)
                weight = decay * jnp.exp(-rates[m] * hz)
                y = raw[:, 128 * m : 128 * m + 128].reshape(16, 8, 128) * growth
                x = strike - y
                small = jnp.exp(-jnp.abs(x))
                tail = jnp.where(small < 2.0**-12, small, jnp.log(1.0 + small))
                soft = jnp.maximum(x, 0.0) + tail
                slope = jnp.exp(x - soft)
                kern = (fee_decay * slope).reshape(128, 128).astype(BF16)
                soft_sum = jnp.sum(soft, axis=0)
                rho_sum = soft_sum + jnp.sum(slope * y, axis=0)
                fresh.append(sums[2 * m] + weight * soft_sum)
                fresh.append(sums[2 * m + 1] + (hz * weight) * rho_sum)
                sens[m] += dot(fmat[m, :, here], kern)
            return tuple(fresh)

        none = jnp.zeros((8, 128), F32)
        sums = lax.fori_loop(bounds[j, 0], bounds[j, 1], group, (none,) * 4)
        scale = row(ACC) * (SMOOTH / 256.0)
        for m in range(2):
            value = jnp.sum(sums[2 * m], axis=0, keepdims=True) * scale
            rho = jnp.sum(sums[2 * m + 1], axis=0, keepdims=True) * -scale
            res_acc[2 * m, pl.ds(j, 1), :] = value
            res_acc[2 * m + 1, pl.ds(j, 1), :] = rho
            delta[m] += dwt[...] * sens[m]
        return carry

    lax.fori_loop(0, TILES, tile, 0)

    tile_row = jnp.floor(rank_row * 0.125)
    slot_row = rank_row - 8.0 * tile_row
    pick = (tile_row == iota((TILES, 256), 0).astype(F32)).astype(F32)
    keep = (slot_row == (iota((128, 256), 0) // 16).astype(F32)).astype(F32)
    for m in range(2):
        parts = []
        for n in range(2):
            lanes = dot(res_acc[2 * m + n], pick, ((0,), (0,)), HIGHEST)
            parts.append(jnp.sum((lanes * keep).reshape(8, 16, 256), axis=0))
        down = delta[m].T.reshape(8, 16, 128)
        parts.append(jnp.sum(down, axis=0) * (-1.0 / 256.0))
        line = jnp.concatenate(parts, axis=1)
        for o in range(16):
            for k in range(5):
                r = (o % 2) * 10 + m * 5 + k
                out_ref[o // 2, r : r + 1, :] = line[o : o + 1, 128 * k : 128 * k + 128]
    for b in range(NIN):
        out_ref[b, 20:SLAB, :] = jnp.zeros((SLAB - 20, 128), F32)


def revalue(blocks, tables, world, rate):
    return pl.pallas_call(
        value_kernel,
        out_shape=jax.ShapeDtypeStruct((NIN, SLAB, 128), F32),
        scratch_shapes=[
            pltpu.VMEM((2, 128, 2048), BF16),
            pltpu.VMEM((2048, 256), BF16),
            pltpu.VMEM((2, 128, 128), F32),
            pltpu.VMEM((256, 256), BF16),
            pltpu.VMEM((128, 128), F32),
            pltpu.VMEM((2, 128, 128), F32),
            pltpu.VMEM((2, 16, 128), F32),
            pltpu.VMEM((TILES, 128), jnp.int32),
            pltpu.SMEM((TILES, 128), jnp.int32),
            pltpu.VMEM((4, TILES, 128), F32),
            pltpu.VMEM((2, 128, 128), F32),
            pltpu.SemaphoreType.DMA(()),
        ],
        name="revalue",
    )(blocks, tables, world, rate)


def scatter_kernel(slabs_ref, out_ref, inbox, send, recv):
    me = lax.axis_index("inner")
    barrier = pltpu.get_barrier_semaphore()
    for d in range(1, NIN):
        pl.semaphore_signal(
            barrier, inc=1, device_id={"inner": lax.rem(me + d, NIN)}, device_id_type=MESH
        )
    pl.semaphore_wait(barrier, NIN - 1)
    copies = []
    for d in range(1, NIN):
        peer = lax.rem(me + d, NIN)
        copy = pltpu.make_async_remote_copy(
            src_ref=slabs_ref.at[peer],
            dst_ref=inbox.at[d],
            send_sem=send.at[d],
            recv_sem=recv.at[d],
            device_id={"inner": peer},
            device_id_type=MESH,
        )
        copy.start()
        copies.append(copy)
    total = slabs_ref[me]
    for d in range(1, NIN):
        copies[d - 1].wait()
        total = total + inbox[d]
    out_ref[...] = total


def scatter_inner(slabs):
    vmem = pl.BlockSpec(memory_space=pltpu.VMEM)
    return pl.pallas_call(
        scatter_kernel,
        out_shape=jax.ShapeDtypeStruct((SLAB, 128), F32),
        in_specs=[vmem],
        out_specs=vmem,
        scratch_shapes=[
            pltpu.VMEM((NIN, SLAB, 128), F32),
            pltpu.SemaphoreType.DMA((NIN,)),
            pltpu.SemaphoreType.DMA((NIN,)),
        ],
        compiler_params=pltpu.CompilerParams(collective_id=1, has_side_effects=True),
        name="scatter_inner",
    )(slabs)


def cohort_table(sigma, index, alloc, kind, maturity, ratio, fee, mortality, account, me):
    mat = maturity.astype(F32)
    number = (jnp.arange(16, dtype=jnp.int32) + 16 * me).astype(F32)
    key = jnp.where(kind == 0, 128.0 - mat, 256.0 + mat) * 256.0 + number
    columns = [index.astype(F32), alloc]
    for value in (kind.astype(F32), mat, ratio, fee, mortality, account):
        columns.append(value[:, None])
    columns.append(jnp.tile(sigma, 2)[:, None])
    columns.append(key[:, None])
    columns.append(jnp.zeros((16, 112), F32))
    return jnp.concatenate(columns, axis=1)


def shards(
    world_shocks,
    short_rate,
    inner_shocks,
    fund_volatility,
    fund_index,
    allocation,
    guarantee_type,
    maturity,
    guarantee_ratio,
    fee_rate,
    mortality,
    account,
):
    table = cohort_table(
        fund_volatility,
        fund_index,
        allocation,
        guarantee_type,
        maturity,
        guarantee_ratio,
        fee_rate,
        mortality,
        account,
        lax.axis_index("outer"),
    )
    block = own_factor(inner_shocks, fund_volatility[:, None])
    blocks, tables = gather_outer(block, table)
    slabs = revalue(blocks, tables, jnp.swapaxes(world_shocks, 0, 1), short_rate)
    total = scatter_inner(slabs)[:20].reshape(2, 2, 5 * 128)
    return total[..., :256], total[..., 256:512], total[..., 512:]


def solution(mesh):
    return jax.shard_map(
        shards,
        mesh=mesh,
        in_specs=(
            P("outer", None, None),
            P("outer", None),
            P(None, "outer", "inner"),
            P("outer"),
            P("outer", None),
            P("outer", None),
            P("outer"),
            P("outer"),
            P("outer"),
            P("outer"),
            P("outer"),
            P("outer"),
        ),
        out_specs=(
            P(("outer", "inner"), None, None),
            P(("outer", "inner"), None, None),
            P(("outer", "inner"), None, None),
        ),
        check_vma=False,
    )
```

```python
import functools
import math

import jax
import jax.numpy as jnp
from jax import lax
from jax.experimental import pallas as pl
from jax.experimental.pallas import tpu as pltpu
from jax.sharding import PartitionSpec as P

MESH = pl.DeviceIdType.MESH
HIGHEST = lax.Precision.HIGHEST
F32, BF16 = jnp.float32, jnp.bfloat16

STEPS = 64
DRIFT = 0.06
SMOOTH = 0.05
NOUT = 16
NIN = 8
TILES = 32
GROUPS = 16
TYPE, MAT, RATIO, FEE, MORT, ACC, SIG, KEY = 8, 9, 10, 11, 12, 13, 14, 15
SLAB = 24
LOG2E = 1.0 / math.log(2.0)
UNIT = LOG2E / SMOOTH


def dot(a, b, dims=((1,), (0,)), precision=None):
    return lax.dot_general(
        a, b, (dims, ((), ())), precision=precision, preferred_element_type=F32
    )


def dot01(a, b, dims=((1,), (0,)), parts=3):
    b = b.astype(BF16)
    total = None
    for _ in range(parts):
        top = a.astype(BF16)
        a = a - top.astype(F32)
        one = dot(top, b, dims)
        total = one if total is None else total + one
    return total


def iota(shape, dim):
    return lax.broadcasted_iota(jnp.int32, shape, dim)


def factor_kernel(
    me,
    shocks_ref,
    sigma_ref,
    index_ref,
    alloc_ref,
    kind_ref,
    mat_ref,
    ratio_ref,
    fee_ref,
    mort_ref,
    acc_ref,
    out_ref,
    table_ref,
    scratch,
):
    me = lax.axis_index("outer") if me is None else me
    sigma_row = sigma_ref[...]
    mat = mat_ref[...].astype(F32)
    number = (iota((1, 16), 1) + 16 * me).astype(F32)
    key = jnp.where(kind_ref[...] == 0, 128.0 - mat, 256.0 + mat) * 256.0 + number
    scratch[...] = jnp.zeros((16, 128), F32)
    scratch[0:4, 0:16] = index_ref[...].astype(F32)
    scratch[4:8, 0:16] = alloc_ref[...]
    scratch[TYPE : TYPE + 1, 0:16] = kind_ref[...].astype(F32)
    scratch[MAT : MAT + 1, 0:16] = mat
    scratch[RATIO : RATIO + 1, 0:16] = ratio_ref[...]
    scratch[FEE : FEE + 1, 0:16] = fee_ref[...]
    scratch[MORT : MORT + 1, 0:16] = mort_ref[...]
    scratch[ACC : ACC + 1, 0:16] = acc_ref[...]
    scratch[SIG : SIG + 1, 0:8] = sigma_row
    scratch[KEY : KEY + 1, 0:16] = key
    table_ref[...] = pltpu.roll(scratch[...], 16 * lax.rem(me, 8), 1)

    rows = jnp.concatenate(
        [shocks_ref[m, :, 128 * j : 128 * j + 128] for m in range(2) for j in range(16)],
        axis=0,
    )
    src, dst = iota((128, 128), 0), iota((128, 128), 1)
    upper = (src // 64 == dst // 64) & (src <= dst)
    running = dot01(rows, upper.astype(F32))
    same = iota((8, 8), 0) == iota((8, 8), 1)
    sigma = jnp.sum(jnp.where(same, sigma_row, 0.0), axis=1, keepdims=True)
    sigma = jnp.broadcast_to(sigma[None], (32, 8, 1)).reshape(256, 1)
    horizon = (iota((1, 128), 1) % 64 + 1).astype(F32)
    factor = jnp.exp(-0.5 * sigma * sigma * horizon + sigma * running)
    lane = iota((8, 128), 1)
    months = []
    for m in range(2):
        regs = [factor[(m * 16 + j) * 8 : (m * 16 + j) * 8 + 8] for j in range(16)]
        for bit in range(4):
            low = (lane // (4 << bit)) % 2 == 0
            step = 4 << bit
            fresh = list(regs)
            for j in range(16):
                if j >> bit & 1:
                    continue
                k = j | 1 << bit
                a, b = regs[j], regs[k]
                fresh[j] = jnp.where(low, a, pltpu.roll(b, step, 1))
                fresh[k] = jnp.where(low, pltpu.roll(a, 128 - step, 1), b)
            regs = fresh
        months.append(regs)
    for g in range(16):
        both = jnp.concatenate([months[0][g], months[1][g]], axis=0)
        out_ref[:, 128 * g : 128 * g + 128] = both.astype(BF16)


def own_factor(shocks, sigma, index, alloc, *rest, me=None):
    return pl.pallas_call(
        functools.partial(factor_kernel, me),
        out_shape=(
            jax.ShapeDtypeStruct((16, 2048), BF16),
            jax.ShapeDtypeStruct((16, 128), F32),
        ),
        scratch_shapes=[pltpu.VMEM((16, 128), F32)],
        name="own_factor",
    )(shocks, sigma[None], index.T, alloc.T, *(value[None] for value in rest))


def gather_kernel(block_ref, table_ref, blocks_ref, tables_ref, send, recv, own):
    me = lax.axis_index("outer")
    barrier = pltpu.get_barrier_semaphore()
    for d in range(1, NOUT):
        pl.semaphore_signal(
            barrier, inc=1, device_id={"outer": lax.rem(me + d, NOUT)}, device_id_type=MESH
        )
    pl.semaphore_wait(barrier, NOUT - 1)
    copies = []
    for d in range(1, NOUT):
        peer = lax.rem(me + d, NOUT)
        for n, (src, dst) in enumerate(((table_ref, tables_ref), (block_ref, blocks_ref))):
            copy = pltpu.make_async_remote_copy(
                src_ref=src,
                dst_ref=dst.at[me],
                send_sem=send.at[n, d],
                recv_sem=recv.at[n, d],
                device_id={"outer": peer},
                device_id_type=MESH,
            )
            copy.start()
            copies.append(copy)
    mine = [
        pltpu.make_async_copy(table_ref, tables_ref.at[me], own.at[0]),
        pltpu.make_async_copy(block_ref, blocks_ref.at[me], own.at[1]),
    ]
    for copy in mine:
        copy.start()
    for copy in mine:
        copy.wait()
    for copy in copies:
        copy.wait()


def gather_outer(block, table):
    vmem = pl.BlockSpec(memory_space=pltpu.VMEM)
    anywhere = pl.BlockSpec(memory_space=pl.ANY)
    return pl.pallas_call(
        gather_kernel,
        out_shape=(
            jax.ShapeDtypeStruct((NOUT, 16, 2048), BF16),
            jax.ShapeDtypeStruct((NOUT, 16, 128), F32),
        ),
        in_specs=[vmem, vmem],
        out_specs=(anywhere, anywhere),
        scratch_shapes=[
            pltpu.SemaphoreType.DMA((2, NOUT)),
            pltpu.SemaphoreType.DMA((2, NOUT)),
            pltpu.SemaphoreType.DMA((2,)),
        ],
        compiler_params=pltpu.CompilerParams(collective_id=0, has_side_effects=True),
        name="gather_outer",
    )(block, table)


def value_kernel(
    blocks_ref,
    tables_ref,
    world_ref,
    rate_ref,
    out_ref,
    fmat,
    fmat_t,
    level,
    weight_t,
    dwt,
    rows_t,
    acc_t,
    table,
    plan_v,
    plan,
    sums_t,
    sens,
    sums_in,
    kerns,
    sem,
):
    params_t = jnp.concatenate(
        [sum(tables_ref[s] for s in range(8)), sum(tables_ref[s] for s in range(8, 16))],
        axis=1,
    )
    params = params_t.T
    key_col, key_row = params[:, KEY : KEY + 1], params_t[KEY : KEY + 1]
    rank_col = jnp.sum((key_row < key_col).astype(F32), axis=1, keepdims=True)
    rank_row = jnp.sum((key_col < key_row).astype(F32), axis=0, keepdims=True)
    place = (rank_col == iota((256, 256), 1).astype(F32)).astype(F32)
    ordered = dot01(params_t, place)
    table[0] = ordered[:, :128]
    table[1] = ordered[:, 128:]

    mat = ordered[MAT : MAT + 1]
    first = jnp.where(ordered[TYPE : TYPE + 1] == 0.0, 1.0, mat)
    tile_of = iota((TILES, 256), 1) // 8 == iota((TILES, 256), 0)
    low = jnp.min(jnp.where(tile_of, first, 1e3), axis=1, keepdims=True)
    high = jnp.max(jnp.where(tile_of, mat, 0.0), axis=1, keepdims=True)
    low = jnp.floor((low - 1.0) * 0.25)
    count = jnp.floor((jnp.floor((high - 1.0) * 0.25) - low) * 0.5) + 1.0
    before = (iota((TILES, TILES), 1) < iota((TILES, TILES), 0)).astype(F32)
    begin = dot(before, jnp.broadcast_to(count, (TILES, 384)))
    item = iota((TILES, 384), 1).astype(F32)
    mine = (begin <= item) & (item < begin + count)
    tile_id = iota((TILES, 384), 0).astype(F32)
    plan_v[0:1, :] = jnp.sum(jnp.where(mine, tile_id, 0.0), axis=0, keepdims=True).astype(jnp.int32)
    place_g = jnp.where(mine, low + 2.0 * (item - begin), 0.0)
    plan_v[1:2, :] = jnp.sum(place_g, axis=0, keepdims=True).astype(jnp.int32)
    items = jnp.sum(mine.astype(F32), axis=(0, 1), keepdims=True)
    plan_v[2:8, :] = jnp.broadcast_to(items, (6, 384)).astype(jnp.int32)
    copy = pltpu.make_async_copy(plan_v, plan, sem)
    copy.start()

    spread_o = (iota((16, 128), 1) % 16 == iota((16, 128), 0)).astype(F32)
    sigma = params[:, SIG : SIG + 1].reshape(16, 2, 8, 1)[:, 0].reshape(128, 1)
    total = jnp.zeros((128, 128), F32)
    rates = []
    rate_col = rate_ref[...].T
    for m in range(2):
        shock = dot01(world_ref[:, m, :], spread_o, ((0,), (0,)))
        total = total + (
            (DRIFT - 0.5 * sigma * sigma) / 12.0 + sigma * shock / math.sqrt(12.0)
        )
        level[m] = jnp.exp(total)
        rate = jnp.sum(rate_col[:, m : m + 1] * spread_o, axis=0, keepdims=True)
        rates.append(jnp.broadcast_to(rate, (8, 128)))

    fund = iota((128, 128), 0).astype(F32)
    step_in = iota((8, 128), 0) % 4

    def build(j, carry):
        where = 8 * lax.rem(j, 16) + iota((16, 128), 1) // 16
        rows = jnp.take_along_axis(table[j // 16], where, axis=1)

        def row(k):
            return rows[k : k + 1]

        share_sum = row(4) + row(5) + row(6) + row(7)
        wts = jnp.zeros((128, 128), F32)
        for k in range(4):
            wts = wts + jnp.where(fund == row(k), row(4 + k) / share_sum, 0.0)
        dwt[j] = wts * row(ACC)
        zero = jnp.zeros((16, 8, 128), F32)
        for m in range(2):
            one = (wts * level[m]).reshape(16, 8, 128)
            both = [one, zero] if m == 0 else [zero, one]
            both = jnp.stack(both, axis=1).reshape(256, 128)
            weight_t[j, :, 128 * m : 128 * m + 128] = both.astype(BF16)
            sens[j, m] = jnp.zeros((128, 128), F32)
        for n in range(4):
            sums_t[j, n] = jnp.zeros((8, 128), F32)
        death = row(TYPE) == 0.0
        mat = row(MAT)
        log_keep = jnp.log(1.0 - row(MORT))
        rows_t[j, 0:1] = jnp.where(death, 1.0, mat)
        rows_t[j, 1:2] = mat
        rows_t[j, 2:3] = jnp.where(death, row(MORT), 1.0)
        rows_t[j, 3:4] = jnp.where(death, log_keep, 0.0) * LOG2E
        rows_t[j, 4:5] = jnp.where(death, -log_keep, log_keep * mat) * LOG2E
        rows_t[j, 5:6] = row(FEE) * LOG2E
        rows_t[j, 6:7] = row(RATIO) * UNIT
        acc_t[pl.ds(j, 1), :] = row(ACC)
        return carry

    lax.fori_loop(0, TILES, build, 0)

    for g in range(GROUPS):
        cols = slice(128 * g, 128 * g + 128)
        part = blocks_ref[:, :, cols].astype(F32).reshape(16, 2, 8, 128)
        for m in range(2):
            one = part[:, m].reshape(128, 128)
            fmat[m, :, cols] = one.astype(BF16)
        fmat_t[cols, :] = part.reshape(256, 128).T.astype(BF16)
    fmat[:, :, 2048:] = jnp.zeros((2, 128, 128), BF16)
    fmat_t[2048:, :] = jnp.zeros((256, 256), BF16)
    copy.wait()

    def raw(j, g):
        here = pl.ds(pl.multiple_of(g * 128, 128), 128)
        return dot(fmat_t[here, :], weight_t[j])

    rates2 = [rate * LOG2E for rate in rates]

    def group(j, g, slot):
        def wide(k):
            return jnp.broadcast_to(rows_t[j, k : k + 1], (8, 128))

        hz = (step_in + (4 * g + 1)).astype(F32)
        fee = wide(5)
        decay = jnp.where(
            (hz >= wide(0)) & (hz <= wide(1)),
            wide(2) * lax.exp2(wide(3) * hz + wide(4)),
            0.0,
        )
        fee_decay = lax.exp2(-fee * hz) * decay
        strike = wide(6)
        for m in range(2):
            growth = lax.exp2((rates2[m] - fee) * hz) * UNIT
            weight = decay * lax.exp2(-rates2[m] * hz)
            y = sums_in[slot, :, 128 * m : 128 * m + 128].reshape(16, 8, 128) * growth
            x = strike - y
            up = lax.exp2(x)
            more = 1.0 + up
            soft = jnp.where(up < 2.0**-12, up, jnp.log(more))
            slope = up / more
            kern = (fee_decay * slope).reshape(128, 128).astype(BF16)
            soft_sum = jnp.sum(soft, axis=0)
            rho_sum = soft_sum + jnp.sum(slope * y, axis=0) * (1.0 / LOG2E)
            sums_t[j, 2 * m] += weight * soft_sum
            sums_t[j, 2 * m + 1] += (hz * weight) * rho_sum
            kerns[m, 128 * slot : 128 * slot + 128, :] = kern

    def flush(j, g):
        here = pl.ds(pl.multiple_of(g * 128, 128), 256)
        for m in range(2):
            sens[j, m] += dot(fmat[m, :, here], kerns[m])

    total = plan[2, 0]
    kerns[...] = jnp.zeros((2, 256, 128), BF16)
    sums_in[0] = raw(plan[0, 0], plan[1, 0])

    def work(i, carry):
        j, g = plan[0, i], plan[1, i]
        last = jnp.maximum(i - 1, 0)
        flush(plan[0, last], plan[1, last])
        sums_in[1] = raw(j, g + 1)
        group(j, g, 0)
        sums_in[0] = raw(plan[0, i + 1], plan[1, i + 1])
        group(j, g + 1, 1)
        return carry

    lax.fori_loop(0, total, work, 0)
    flush(plan[0, total - 1], plan[1, total - 1])

    def close(q, deltas):
        fresh = list(deltas)
        for k in range(4):
            j = 4 * q + k
            for m in range(2):
                fresh[m] = fresh[m] + dwt[j] * sens[j, m]
        return tuple(fresh)

    none = jnp.zeros((128, 128), F32)
    delta = lax.fori_loop(0, TILES // 4, close, (none, none))
    scale = acc_t[...] * (1.0 / 20.0 / 256.0)
    res_acc = []
    for n in range(4):
        value = jnp.sum(sums_t[:, n], axis=1)
        res_acc.append(value * (scale if n % 2 == 0 else -scale))

    tile_row = jnp.floor(rank_row * 0.125)
    slot_row = rank_row - 8.0 * tile_row
    pick = (tile_row == iota((TILES, 256), 0).astype(F32)).astype(F32)
    keep = (slot_row == (iota((128, 256), 0) // 16).astype(F32)).astype(F32)
    for m in range(2):
        parts = []
        for n in range(2):
            lanes = dot01(res_acc[2 * m + n], pick, ((0,), (0,)))
            parts.append(jnp.sum((lanes * keep).reshape(8, 16, 256), axis=0))
        down = delta[m].T.reshape(8, 16, 128)
        parts.append(jnp.sum(down, axis=0) * (-1.0 / 256.0))
        line = jnp.concatenate(parts, axis=1)
        for o in range(16):
            for k in range(5):
                r = (o % 2) * 10 + m * 5 + k
                out_ref[o // 2, r : r + 1, :] = line[o : o + 1, 128 * k : 128 * k + 128]
    for b in range(NIN):
        out_ref[b, 20:SLAB, :] = jnp.zeros((SLAB - 20, 128), F32)


def revalue(blocks, tables, world, rate):
    return pl.pallas_call(
        value_kernel,
        out_shape=jax.ShapeDtypeStruct((NIN, SLAB, 128), F32),
        scratch_shapes=[
            pltpu.VMEM((2, 128, 2176), BF16),
            pltpu.VMEM((2304, 256), BF16),
            pltpu.VMEM((2, 128, 128), F32),
            pltpu.VMEM((TILES, 256, 256), BF16),
            pltpu.VMEM((TILES, 128, 128), F32),
            pltpu.VMEM((TILES, 8, 128), F32),
            pltpu.VMEM((TILES, 128), F32),
            pltpu.VMEM((2, 16, 128), F32),
            pltpu.VMEM((8, 384), jnp.int32),
            pltpu.SMEM((8, 384), jnp.int32),
            pltpu.VMEM((TILES, 4, 8, 128), F32),
            pltpu.VMEM((TILES, 2, 128, 128), F32),
            pltpu.VMEM((2, 128, 256), F32),
            pltpu.VMEM((2, 256, 128), BF16),
            pltpu.SemaphoreType.DMA(()),
        ],
        name="revalue",
    )(blocks, tables, world, rate.T)


def scatter_kernel(slabs_ref, out_ref, inbox, send, recv):
    me = lax.axis_index("inner")
    barrier = pltpu.get_barrier_semaphore()
    for d in range(1, NIN):
        pl.semaphore_signal(
            barrier, inc=1, device_id={"inner": lax.rem(me + d, NIN)}, device_id_type=MESH
        )
    pl.semaphore_wait(barrier, NIN - 1)
    copies = []
    for d in range(1, NIN):
        peer = lax.rem(me + d, NIN)
        copy = pltpu.make_async_remote_copy(
            src_ref=slabs_ref.at[peer],
            dst_ref=inbox.at[d],
            send_sem=send.at[d],
            recv_sem=recv.at[d],
            device_id={"inner": peer},
            device_id_type=MESH,
        )
        copy.start()
        copies.append(copy)
    total = slabs_ref[me]
    for d in range(1, NIN):
        copies[d - 1].wait()
        total = total + inbox[d]
    out_ref[...] = total


def scatter_inner(slabs):
    vmem = pl.BlockSpec(memory_space=pltpu.VMEM)
    return pl.pallas_call(
        scatter_kernel,
        out_shape=jax.ShapeDtypeStruct((SLAB, 128), F32),
        in_specs=[vmem],
        out_specs=vmem,
        scratch_shapes=[
            pltpu.VMEM((NIN, SLAB, 128), F32),
            pltpu.SemaphoreType.DMA((NIN,)),
            pltpu.SemaphoreType.DMA((NIN,)),
        ],
        compiler_params=pltpu.CompilerParams(collective_id=1, has_side_effects=True),
        name="scatter_inner",
    )(slabs)


def shards(
    world_shocks,
    short_rate,
    inner_shocks,
    fund_volatility,
    fund_index,
    allocation,
    guarantee_type,
    maturity,
    guarantee_ratio,
    fee_rate,
    mortality,
    account,
):
    block, table = own_factor(
        inner_shocks,
        fund_volatility,
        fund_index,
        allocation,
        guarantee_type,
        maturity,
        guarantee_ratio,
        fee_rate,
        mortality,
        account,
    )
    blocks, tables = gather_outer(block, table)
    slabs = revalue(blocks, tables, world_shocks, short_rate)
    total = scatter_inner(slabs)[:20].reshape(2, 2, 5 * 128)
    return total[..., :256], total[..., 256:512], total[..., 512:]


def solution(mesh):
    return jax.shard_map(
        shards,
        mesh=mesh,
        in_specs=(
            P("outer", None, None),
            P("outer", None),
            P(None, "outer", "inner"),
            P("outer"),
            P("outer", None),
            P("outer", None),
            P("outer"),
            P("outer"),
            P("outer"),
            P("outer"),
            P("outer"),
            P("outer"),
        ),
        out_specs=(
            P(("outer", "inner"), None, None),
            P(("outer", "inner"), None, None),
            P(("outer", "inner"), None, None),
        ),
        check_vma=False,
    )
```

```python
import functools
import math

import jax
import jax.numpy as jnp
from jax import lax
from jax.experimental import pallas as pl
from jax.experimental.pallas import tpu as pltpu
from jax.sharding import PartitionSpec as P

MESH = pl.DeviceIdType.MESH
HIGHEST = lax.Precision.HIGHEST
F32, BF16 = jnp.float32, jnp.bfloat16

STEPS = 64
DRIFT = 0.06
SMOOTH = 0.05
NOUT = 16
NIN = 8
TILES = 32
GROUPS = 16
TYPE, MAT, RATIO, FEE, MORT, ACC, SIG, KEY = 8, 9, 10, 11, 12, 13, 14, 15
SLAB = 24
MESSAGES = 50
LOG2E = 1.0 / math.log(2.0)
UNIT = LOG2E / SMOOTH


def dot(a, b, dims=((1,), (0,)), precision=None):
    return lax.dot_general(
        a, b, (dims, ((), ())), precision=precision, preferred_element_type=F32
    )


def dot01(a, b, dims=((1,), (0,)), parts=3):
    b = b.astype(BF16)
    total = None
    for _ in range(parts):
        top = a.astype(BF16)
        a = a - top.astype(F32)
        one = dot(top, b, dims)
        total = one if total is None else total + one
    return total


def iota(shape, dim):
    return lax.broadcasted_iota(jnp.int32, shape, dim)


def factor_kernel(
    me,
    shocks_ref,
    sigma_ref,
    index_ref,
    alloc_ref,
    kind_ref,
    mat_ref,
    ratio_ref,
    fee_ref,
    mort_ref,
    acc_ref,
    out_ref,
    table_ref,
    scratch,
):
    me = lax.axis_index("outer") if me is None else me
    sigma_row = sigma_ref[...]
    mat = mat_ref[...].astype(F32)
    number = (iota((1, 16), 1) + 16 * me).astype(F32)
    key = jnp.where(kind_ref[...] == 0, 128.0 - mat, 256.0 + mat) * 256.0 + number
    scratch[...] = jnp.zeros((16, 128), F32)
    scratch[0:4, 0:16] = index_ref[...].astype(F32)
    scratch[4:8, 0:16] = alloc_ref[...]
    scratch[TYPE : TYPE + 1, 0:16] = kind_ref[...].astype(F32)
    scratch[MAT : MAT + 1, 0:16] = mat
    scratch[RATIO : RATIO + 1, 0:16] = ratio_ref[...]
    scratch[FEE : FEE + 1, 0:16] = fee_ref[...]
    scratch[MORT : MORT + 1, 0:16] = mort_ref[...]
    scratch[ACC : ACC + 1, 0:16] = acc_ref[...]
    scratch[SIG : SIG + 1, 0:8] = sigma_row
    scratch[KEY : KEY + 1, 0:16] = key
    for r in range(2):
        line = scratch[8 * r : 8 * r + 1, :]
        for k in range(1, 8):
            line = line + pltpu.roll(scratch[8 * r + k : 8 * r + k + 1, :], 16 * k, 1)
        table_ref[r : r + 1, :] = line

    rows = jnp.concatenate(
        [shocks_ref[m, :, 128 * j : 128 * j + 128] for m in range(2) for j in range(16)],
        axis=0,
    )
    src, dst = iota((128, 128), 0), iota((128, 128), 1)
    upper = (src // 64 == dst // 64) & (src <= dst)
    running = dot01(rows, upper.astype(F32))
    same = iota((8, 8), 0) == iota((8, 8), 1)
    sigma = jnp.sum(jnp.where(same, sigma_row, 0.0), axis=1, keepdims=True)
    sigma = jnp.broadcast_to(sigma[None], (32, 8, 1)).reshape(256, 1)
    horizon = (iota((1, 128), 1) % 64 + 1).astype(F32)
    factor = jnp.exp(-0.5 * sigma * sigma * horizon + sigma * running)
    lane = iota((8, 128), 1)
    months = []
    for m in range(2):
        regs = [factor[(m * 16 + j) * 8 : (m * 16 + j) * 8 + 8] for j in range(16)]
        for bit in range(4):
            low = (lane // (4 << bit)) % 2 == 0
            step = 4 << bit
            fresh = list(regs)
            for j in range(16):
                if j >> bit & 1:
                    continue
                k = j | 1 << bit
                a, b = regs[j], regs[k]
                fresh[j] = jnp.where(low, a, pltpu.roll(b, step, 1))
                fresh[k] = jnp.where(low, pltpu.roll(a, 128 - step, 1), b)
            regs = fresh
        months.append(regs)
    for g in range(16):
        both = jnp.concatenate([months[0][g], months[1][g]], axis=0)
        out_ref[g // 4, :, 128 * (g % 4) : 128 * (g % 4) + 128] = both.astype(BF16)


def own_factor(shocks, sigma, index, alloc, *rest, me=None):
    return pl.pallas_call(
        functools.partial(factor_kernel, me),
        out_shape=(
            jax.ShapeDtypeStruct((4, 16, 512), BF16),
            jax.ShapeDtypeStruct((2, 128), F32),
        ),
        scratch_shapes=[pltpu.VMEM((16, 128), F32)],
        name="own_factor",
    )(shocks, sigma[None], index.T, alloc.T, *(value[None] for value in rest))


def gather_kernel(block_ref, table_ref, blocks_ref, tables_ref, send, recv, own):
    me = lax.axis_index("outer")
    row, col = me // 4, me % 4

    def at(dy, dx):
        return ((row + dy) % 4) * 4 + (col + dx) % 4

    peers = [at(0, 1), at(0, 3), at(1, 0), at(3, 0), at(0, 2), at(2, 0)]
    barrier = pltpu.get_barrier_semaphore()
    for peer in peers:
        pl.semaphore_signal(barrier, inc=1, device_id={"outer": peer}, device_id_type=MESH)
    pl.semaphore_wait(barrier, len(peers))

    started = []

    def post(number, peer, src, dst):
        copy = pltpu.make_async_remote_copy(
            src_ref=src,
            dst_ref=dst,
            send_sem=send.at[number],
            recv_sem=recv.at[number],
            device_id={"outer": peer},
            device_id_type=MESH,
        )
        copy.start()
        started.append(copy)
        return copy

    numbers = iter(range(MESSAGES))

    def piece(origin, first, count):
        return blocks_ref.at[origin, pl.ds(first, count)]

    def send_piece(peer, origin, first, count, mine=False):
        dst = piece(origin, first, count)
        src = block_ref.at[pl.ds(first, count)] if mine else dst
        return post(next(numbers), peer, src, dst)

    local = [
        pltpu.make_async_copy(table_ref, tables_ref.at[me], own.at[0]),
        pltpu.make_async_copy(block_ref, blocks_ref.at[me], own.at[1]),
    ]
    for copy in local:
        copy.start()

    across = [post(next(numbers), at(0, d), table_ref, tables_ref.at[me]) for d in (1, 3, 2)]

    def shift(color, first_step, second_step):
        return at(second_step, first_step) if color == 0 else at(first_step, second_step)

    near = []
    for color in range(2):
        q = 2 * color
        near.append([send_piece(shift(color, d, 0), me, q, 2, True) for d in (1, 3)])
    home = []
    for color in range(2):
        q = 2 * color
        home.append([send_piece(shift(color, 0, d), me, q, 2, True) for d in (1, 3)])

    second = []
    far = []
    for side in range(2):
        for color in range(2):
            q = 2 * color
            behind, onward = (3, 1) if side == 0 else (1, 3)
            near[color][side].wait_recv()
            origin = shift(color, behind, 0)
            far.append((color, side, send_piece(shift(color, onward, 0), origin, q + side, 1)))
            for way, d in enumerate((1, 3)):
                copy = send_piece(shift(color, 0, d), origin, q, 2)
                second.append((color, behind, q, 2, way, copy))

    last = []

    def hand_on(color, first, q, count, way, copy):
        copy.wait_recv()
        behind, onward = (3, 1) if way == 0 else (1, 3)
        quarter = 2 * color + way
        if not q <= quarter < q + count:
            return
        origin = shift(color, first, behind)
        last.append(send_piece(shift(color, 0, onward), origin, quarter, 1))

    for way in range(2):
        for color in range(2):
            hand_on(color, 0, 2 * color, 2, way, home[color][way])
    for copy in across:
        copy.wait_recv()
    local[0].wait()
    line = tables_ref.at[pl.ds(row * 4, 4)]
    down = [post(next(numbers), at(d, 0), line, line) for d in (1, 3, 2)]
    for color, side, copy in far:
        copy.wait_recv()
        for way, d in enumerate((1, 3)):
            fresh = send_piece(shift(color, 0, d), shift(color, 2, 0), 2 * color + side, 1)
            second.append((color, 2, 2 * color + side, 1, way, fresh))
    for entry in second:
        hand_on(*entry)
    for copy in down + last:
        copy.wait_recv()
    local[1].wait()
    for copy in started:
        copy.wait_send()


def gather_outer(block, table):
    vmem = pl.BlockSpec(memory_space=pltpu.VMEM)
    anywhere = pl.BlockSpec(memory_space=pl.ANY)
    return pl.pallas_call(
        gather_kernel,
        out_shape=(
            jax.ShapeDtypeStruct((NOUT, 4, 16, 512), BF16),
            jax.ShapeDtypeStruct((NOUT, 2, 128), F32),
        ),
        in_specs=[vmem, vmem],
        out_specs=(anywhere, anywhere),
        scratch_shapes=[
            pltpu.SemaphoreType.DMA((MESSAGES,)),
            pltpu.SemaphoreType.DMA((MESSAGES,)),
            pltpu.SemaphoreType.DMA((2,)),
        ],
        compiler_params=pltpu.CompilerParams(collective_id=0, has_side_effects=True),
        name="gather_outer",
    )(block, table)


def value_kernel(
    blocks_ref,
    tables_ref,
    world_ref,
    rate_ref,
    out_ref,
    fmat,
    fmat_t,
    level,
    weight_t,
    dwt,
    rows_t,
    acc_t,
    table,
    plan_v,
    plan,
    sums_t,
    sens,
    sums_in,
    kerns,
    dates,
    sem,
):
    lanes = iota((8, 128), 1)
    chosen = 16 * iota((8, 128), 0) + lanes % 16
    halves = []
    for h in range(2):
        pieces = []
        for r in range(2):
            piece = jnp.zeros((8, 128), F32)
            for s in range(8):
                line = jnp.broadcast_to(tables_ref[8 * h + s, r : r + 1, :], (8, 128))
                line = jnp.take_along_axis(line, chosen, axis=1)
                piece = jnp.where(lanes // 16 == s, line, piece)
            pieces.append(piece)
        halves.append(jnp.concatenate(pieces, axis=0))
    params_t = jnp.concatenate(halves, axis=1)
    params = params_t.T
    key_col, key_row = params[:, KEY : KEY + 1], params_t[KEY : KEY + 1]
    rank_col = jnp.sum((key_row < key_col).astype(F32), axis=1, keepdims=True)
    rank_row = jnp.sum((key_col < key_row).astype(F32), axis=0, keepdims=True)
    place = (rank_col == iota((256, 256), 1).astype(F32)).astype(F32)
    ordered = dot01(params_t, place)
    table[0] = ordered[:, :128]
    table[1] = ordered[:, 128:]

    mat = ordered[MAT : MAT + 1]
    first = jnp.where(ordered[TYPE : TYPE + 1] == 0.0, 1.0, mat)
    tile_of = iota((TILES, 256), 1) // 8 == iota((TILES, 256), 0)
    low = jnp.min(jnp.where(tile_of, first, 1e3), axis=1, keepdims=True)
    high = jnp.max(jnp.where(tile_of, mat, 0.0), axis=1, keepdims=True)
    low = jnp.floor((low - 1.0) * 0.25)
    count = jnp.floor((jnp.floor((high - 1.0) * 0.25) - low) * 0.5) + 1.0
    before = (iota((TILES, TILES), 1) < iota((TILES, TILES), 0)).astype(F32)
    begin = dot(before, jnp.broadcast_to(count, (TILES, 384)))
    item = iota((TILES, 384), 1).astype(F32)
    mine = (begin <= item) & (item < begin + count)
    tile_id = iota((TILES, 384), 0).astype(F32)
    plan_v[0:1, :] = jnp.sum(jnp.where(mine, tile_id, 0.0), axis=0, keepdims=True).astype(jnp.int32)
    place_g = jnp.where(mine, low + 2.0 * (item - begin) - 16.0, 0.0)
    place_g = 16.0 + jnp.sum(place_g, axis=0, keepdims=True)
    plan_v[1:2, :] = place_g.astype(jnp.int32)
    items = jnp.sum(mine.astype(F32), axis=(0, 1), keepdims=True)
    plan_v[2:8, :] = jnp.broadcast_to(items, (6, 384)).astype(jnp.int32)
    copy = pltpu.make_async_copy(plan_v, plan, sem)
    copy.start()

    spread_o = (iota((16, 128), 1) % 16 == iota((16, 128), 0)).astype(F32)
    sigma = params[:, SIG : SIG + 1].reshape(16, 2, 8, 1)[:, 0].reshape(128, 1)
    total = jnp.zeros((128, 128), F32)
    rates = []
    rate_col = rate_ref[...].T
    for m in range(2):
        shock = dot01(world_ref[:, m, :], spread_o, ((0,), (0,)))
        total = total + (
            (DRIFT - 0.5 * sigma * sigma) / 12.0 + sigma * shock / math.sqrt(12.0)
        )
        level[m] = jnp.exp(total)
        rate = jnp.sum(rate_col[:, m : m + 1] * spread_o, axis=0, keepdims=True)
        rates.append(jnp.broadcast_to(rate, (8, 128)))

    step_in = iota((8, 128), 0) % 4
    for g in range(GROUPS + 2):
        hz = (step_in + (4 * g + 1)).astype(F32)
        for m in range(2):
            power = (LOG2E * rates[m]) * hz
            discount = lax.exp2(-power)
            dates[g, 3 * m] = discount
            dates[g, 3 * m + 1] = hz * discount
            dates[g, 3 * m + 2] = lax.exp2(power) * UNIT

    fund = iota((128, 128), 0).astype(F32)
    step_in = iota((8, 128), 0) % 4

    def build(j, carry):
        where = 8 * lax.rem(j, 16) + iota((16, 128), 1) // 16
        rows = jnp.take_along_axis(table[j // 16], where, axis=1)

        def row(k):
            return rows[k : k + 1]

        share_sum = row(4) + row(5) + row(6) + row(7)
        wts = jnp.zeros((128, 128), F32)
        for k in range(4):
            wts = wts + jnp.where(fund == row(k), row(4 + k) / share_sum, 0.0)
        dwt[j] = wts * row(ACC)
        zero = jnp.zeros((16, 8, 128), F32)
        for m in range(2):
            one = (wts * level[m]).reshape(16, 8, 128)
            both = [one, zero] if m == 0 else [zero, one]
            both = jnp.stack(both, axis=1).reshape(256, 128)
            weight_t[j, :, 128 * m : 128 * m + 128] = both.astype(BF16)
            sens[j, m] = jnp.zeros((128, 128), F32)
        for n in range(4):
            sums_t[j, n] = jnp.zeros((8, 128), F32)
        death = row(TYPE) == 0.0
        mat = row(MAT)
        log_keep = jnp.log(1.0 - row(MORT))
        rows_t[j, 0:1] = jnp.where(death, 1.0, mat)
        rows_t[j, 1:2] = mat
        rows_t[j, 2:3] = jnp.where(death, log_keep, 0.0) * LOG2E
        shift = jnp.where(death, jnp.log(row(MORT)) - log_keep, log_keep * mat)
        rows_t[j, 3:4] = shift * LOG2E
        rows_t[j, 4:5] = row(FEE) * -LOG2E
        rows_t[j, 5:6] = row(RATIO) * UNIT
        acc_t[pl.ds(j, 1), :] = row(ACC)
        return carry

    lax.fori_loop(0, TILES, build, 0)

    for g in range(GROUPS):
        cols = slice(128 * g, 128 * g + 128)
        part = blocks_ref[:, g // 4, :, 128 * (g % 4) : 128 * (g % 4) + 128]
        part = part.astype(F32).reshape(16, 2, 8, 128)
        for m in range(2):
            one = part[:, m].reshape(128, 128)
            fmat[m, :, cols] = one.astype(BF16)
        fmat_t[cols, :] = part.reshape(256, 128).T.astype(BF16)
    fmat[:, :, 2048:] = jnp.zeros((2, 128, 256), BF16)
    fmat_t[2048:, :] = jnp.zeros((256, 256), BF16)
    copy.wait()

    def raw(i, half):
        here = pl.ds(pl.multiple_of(plan[1, i] * 128, 128), 256)
        sums_in[half] = dot(fmat_t[here, :], weight_t[plan[0, i]])

    def group(j, g, half, slot):
        def wide(k):
            return jnp.broadcast_to(rows_t[j, k : k + 1], (8, 128))

        hz = (step_in + (4 * g + 1)).astype(F32)
        decay = lax.exp2(wide(2) * hz + wide(3))
        decay = jnp.where((hz >= wide(0)) & (hz <= wide(1)), decay, 0.0)
        fee_power = lax.exp2(wide(4) * hz)
        fee_decay = fee_power * decay
        strike = wide(5)
        part = slice(128 * slot, 128 * slot + 128)
        for m in range(2):
            growth = fee_power * dates[g, 3 * m + 2]
            y = sums_in[half, part, 128 * m : 128 * m + 128].reshape(16, 8, 128) * growth
            up = lax.exp2(strike - y)
            more = 1.0 + up
            soft = jnp.where(up < 2.0**-12, up, jnp.log(more))
            slope = up / more
            kerns[half, m, part, :] = (fee_decay * slope).reshape(128, 128).astype(BF16)
            soft_sum = jnp.sum(soft, axis=0)
            rho_sum = soft_sum + jnp.sum(slope * y, axis=0) * (1.0 / LOG2E)
            sums_t[j, 2 * m] += (decay * dates[g, 3 * m]) * soft_sum
            sums_t[j, 2 * m + 1] += (decay * dates[g, 3 * m + 1]) * rho_sum

    def flush(i, half):
        j = plan[0, i]
        here = pl.ds(pl.multiple_of(plan[1, i] * 128, 128), 256)
        for m in range(2):
            sens[j, m] += dot(fmat[m, :, here], kerns[half, m])

    def item_work(i, half):
        j, g = plan[0, i], plan[1, i]
        flush(jnp.maximum(i - 1, 0), 1 - half)
        raw(i + 1, 1 - half)
        group(j, g, half, 0)
        group(j, g + 1, half, 1)

    kerns[1] = jnp.zeros((2, 256, 128), BF16)
    raw(0, 0)

    def work(n, carry):
        item_work(2 * n, 0)
        item_work(2 * n + 1, 1)
        return carry

    pairs = (plan[2, 0] + 1) // 2
    lax.fori_loop(0, pairs, work, 0)
    flush(2 * pairs - 1, 1)

    def close(q, deltas):
        fresh = list(deltas)
        for k in range(4):
            j = 4 * q + k
            for m in range(2):
                fresh[m] = fresh[m] + dwt[j] * sens[j, m]
        return tuple(fresh)

    none = jnp.zeros((128, 128), F32)
    delta = lax.fori_loop(0, TILES // 4, close, (none, none))
    scale = acc_t[...] * (1.0 / 20.0 / 256.0)
    res_acc = []
    for n in range(4):
        value = jnp.sum(sums_t[:, n], axis=1)
        res_acc.append(value * (scale if n % 2 == 0 else -scale))

    tile_row = jnp.floor(rank_row * 0.125)
    slot_row = rank_row - 8.0 * tile_row
    pick = (tile_row == iota((TILES, 256), 0).astype(F32)).astype(F32)
    keep = (slot_row == (iota((128, 256), 0) // 16).astype(F32)).astype(F32)
    for m in range(2):
        parts = []
        for n in range(2):
            lanes = dot01(res_acc[2 * m + n], pick, ((0,), (0,)))
            parts.append(jnp.sum((lanes * keep).reshape(8, 16, 256), axis=0))
        down = delta[m].T.reshape(8, 16, 128)
        parts.append(jnp.sum(down, axis=0) * (-1.0 / 256.0))
        line = jnp.concatenate(parts, axis=1)
        for o in range(16):
            for k in range(5):
                r = (o % 2) * 10 + m * 5 + k
                out_ref[o // 2, r : r + 1, :] = line[o : o + 1, 128 * k : 128 * k + 128]
    for b in range(NIN):
        out_ref[b, 20:SLAB, :] = jnp.zeros((SLAB - 20, 128), F32)


def revalue(blocks, tables, world, rate):
    return pl.pallas_call(
        value_kernel,
        out_shape=jax.ShapeDtypeStruct((NIN, SLAB, 128), F32),
        scratch_shapes=[
            pltpu.VMEM((2, 128, 2304), BF16),
            pltpu.VMEM((2304, 256), BF16),
            pltpu.VMEM((2, 128, 128), F32),
            pltpu.VMEM((TILES, 256, 256), BF16),
            pltpu.VMEM((TILES, 128, 128), F32),
            pltpu.VMEM((TILES, 8, 128), F32),
            pltpu.VMEM((TILES, 128), F32),
            pltpu.VMEM((2, 16, 128), F32),
            pltpu.VMEM((8, 384), jnp.int32),
            pltpu.SMEM((8, 384), jnp.int32),
            pltpu.VMEM((TILES, 4, 8, 128), F32),
            pltpu.VMEM((TILES, 2, 128, 128), F32),
            pltpu.VMEM((2, 256, 256), F32),
            pltpu.VMEM((2, 2, 256, 128), BF16),
            pltpu.VMEM((GROUPS + 2, 6, 8, 128), F32),
            pltpu.SemaphoreType.DMA(()),
        ],
        name="revalue",
    )(blocks, tables, world, rate.T)


def scatter_kernel(slabs_ref, res_ref, rho_ref, del_ref, inbox, send, recv):
    me = lax.axis_index("inner")
    barrier = pltpu.get_barrier_semaphore()
    for d in range(1, NIN):
        pl.semaphore_signal(
            barrier, inc=1, device_id={"inner": lax.rem(me + d, NIN)}, device_id_type=MESH
        )
    pl.semaphore_wait(barrier, NIN - 1)
    copies = []
    for d in range(1, NIN):
        peer = lax.rem(me + d, NIN)
        copy = pltpu.make_async_remote_copy(
            src_ref=slabs_ref.at[peer],
            dst_ref=inbox.at[d],
            send_sem=send.at[d],
            recv_sem=recv.at[d],
            device_id={"inner": peer},
            device_id_type=MESH,
        )
        copy.start()
        copies.append(copy)
    total = slabs_ref[me]
    for d in range(1, NIN):
        copies[d - 1].wait()
        total = total + inbox[d]
    for o in range(2):
        for m in range(2):
            r = o * 10 + m * 5
            for k in range(2):
                lanes = slice(128 * k, 128 * k + 128)
                res_ref[o, m : m + 1, lanes] = total[r + k : r + k + 1]
                rho_ref[o, m : m + 1, lanes] = total[r + 2 + k : r + 3 + k]
            del_ref[o, m : m + 1, :] = total[r + 4 : r + 5]


def scatter_inner(slabs):
    vmem = pl.BlockSpec(memory_space=pltpu.VMEM)
    return pl.pallas_call(
        scatter_kernel,
        out_shape=(
            jax.ShapeDtypeStruct((2, 2, 256), F32),
            jax.ShapeDtypeStruct((2, 2, 256), F32),
            jax.ShapeDtypeStruct((2, 2, 128), F32),
        ),
        in_specs=[vmem],
        out_specs=(vmem, vmem, vmem),
        scratch_shapes=[
            pltpu.VMEM((NIN, SLAB, 128), F32),
            pltpu.SemaphoreType.DMA((NIN,)),
            pltpu.SemaphoreType.DMA((NIN,)),
        ],
        compiler_params=pltpu.CompilerParams(collective_id=1, has_side_effects=True),
        name="scatter_inner",
    )(slabs)


def shards(
    world_shocks,
    short_rate,
    inner_shocks,
    fund_volatility,
    fund_index,
    allocation,
    guarantee_type,
    maturity,
    guarantee_ratio,
    fee_rate,
    mortality,
    account,
):
    block, table = own_factor(
        inner_shocks,
        fund_volatility,
        fund_index,
        allocation,
        guarantee_type,
        maturity,
        guarantee_ratio,
        fee_rate,
        mortality,
        account,
    )
    blocks, tables = gather_outer(block, table)
    slabs = revalue(blocks, tables, world_shocks, short_rate)
    return scatter_inner(slabs)


def solution(mesh):
    return jax.shard_map(
        shards,
        mesh=mesh,
        in_specs=(
            P("outer", None, None),
            P("outer", None),
            P(None, "outer", "inner"),
            P("outer"),
            P("outer", None),
            P("outer", None),
            P("outer"),
            P("outer"),
            P("outer"),
            P("outer"),
            P("outer"),
            P("outer"),
        ),
        out_specs=(
            P(("outer", "inner"), None, None),
            P(("outer", "inner"), None, None),
            P(("outer", "inner"), None, None),
        ),
        check_vma=False,
    )
```

```python
import functools
import math

import jax
import jax.numpy as jnp
from jax import lax
from jax.experimental import pallas as pl
from jax.experimental.pallas import tpu as pltpu
from jax.sharding import PartitionSpec as P

MESH = pl.DeviceIdType.MESH
HIGHEST = lax.Precision.HIGHEST
F32, BF16 = jnp.float32, jnp.bfloat16

STEPS = 64
DRIFT = 0.06
SMOOTH = 0.05
NOUT = 16
NIN = 8
TILES = 32
GROUPS = 16
TYPE, MAT, RATIO, FEE, MORT, ACC, SIG, KEY = 8, 9, 10, 11, 12, 13, 14, 15
SLAB = 24
MESSAGES = 50
LOG2E = 1.0 / math.log(2.0)
UNIT = LOG2E / SMOOTH


def dot(a, b, dims=((1,), (0,)), precision=None):
    return lax.dot_general(
        a, b, (dims, ((), ())), precision=precision, preferred_element_type=F32
    )


def dot01(a, b, dims=((1,), (0,)), parts=3):
    b = b.astype(BF16)
    total = None
    for _ in range(parts):
        top = a.astype(BF16)
        a = a - top.astype(F32)
        one = dot(top, b, dims)
        total = one if total is None else total + one
    return total


def iota(shape, dim):
    return lax.broadcasted_iota(jnp.int32, shape, dim)


def factor_kernel(
    me,
    shocks_ref,
    sigma_ref,
    index_ref,
    alloc_ref,
    kind_ref,
    mat_ref,
    ratio_ref,
    fee_ref,
    mort_ref,
    acc_ref,
    out_ref,
    table_ref,
    scratch,
):
    me = lax.axis_index("outer") if me is None else me
    sigma_row = sigma_ref[...]
    mat = mat_ref[...].astype(F32)
    number = (iota((1, 16), 1) + 16 * me).astype(F32)
    key = jnp.where(kind_ref[...] == 0, 128.0 - mat, 256.0 + mat) * 256.0 + number
    scratch[...] = jnp.zeros((16, 128), F32)
    scratch[0:4, 0:16] = index_ref[...].astype(F32)
    scratch[4:8, 0:16] = alloc_ref[...]
    scratch[TYPE : TYPE + 1, 0:16] = kind_ref[...].astype(F32)
    scratch[MAT : MAT + 1, 0:16] = mat
    scratch[RATIO : RATIO + 1, 0:16] = ratio_ref[...]
    scratch[FEE : FEE + 1, 0:16] = fee_ref[...]
    scratch[MORT : MORT + 1, 0:16] = mort_ref[...]
    scratch[ACC : ACC + 1, 0:16] = acc_ref[...]
    scratch[SIG : SIG + 1, 0:8] = sigma_row
    scratch[KEY : KEY + 1, 0:16] = key
    for r in range(2):
        line = scratch[8 * r : 8 * r + 1, :]
        for k in range(1, 8):
            line = line + pltpu.roll(scratch[8 * r + k : 8 * r + k + 1, :], 16 * k, 1)
        table_ref[r : r + 1, :] = line

    rows = jnp.concatenate(
        [shocks_ref[m, :, 128 * j : 128 * j + 128] for m in range(2) for j in range(16)],
        axis=0,
    )
    src, dst = iota((128, 128), 0), iota((128, 128), 1)
    upper = (src // 64 == dst // 64) & (src <= dst)
    running = dot01(rows, upper.astype(F32))
    same = iota((8, 8), 0) == iota((8, 8), 1)
    sigma = jnp.sum(jnp.where(same, sigma_row, 0.0), axis=1, keepdims=True)
    sigma = jnp.broadcast_to(sigma[None], (32, 8, 1)).reshape(256, 1)
    horizon = (iota((1, 128), 1) % 64 + 1).astype(F32)
    factor = jnp.exp(-0.5 * sigma * sigma * horizon + sigma * running)
    lane = iota((8, 128), 1)
    months = []
    for m in range(2):
        regs = [factor[(m * 16 + j) * 8 : (m * 16 + j) * 8 + 8] for j in range(16)]
        for bit in range(4):
            low = (lane // (4 << bit)) % 2 == 0
            step = 4 << bit
            fresh = list(regs)
            for j in range(16):
                if j >> bit & 1:
                    continue
                k = j | 1 << bit
                a, b = regs[j], regs[k]
                fresh[j] = jnp.where(low, a, pltpu.roll(b, step, 1))
                fresh[k] = jnp.where(low, pltpu.roll(a, 128 - step, 1), b)
            regs = fresh
        months.append(regs)
    for g in range(16):
        both = jnp.concatenate([months[0][g], months[1][g]], axis=0)
        out_ref[g // 4, :, 128 * (g % 4) : 128 * (g % 4) + 128] = both.astype(BF16)


def own_factor(shocks, sigma, index, alloc, *rest, me=None):
    return pl.pallas_call(
        functools.partial(factor_kernel, me),
        out_shape=(
            pltpu.VMEM((4, 16, 512), BF16),
            pltpu.VMEM((2, 128), F32),
        ),
        scratch_shapes=[pltpu.VMEM((16, 128), F32)],
        compiler_params=pltpu.CompilerParams(vmem_limit_bytes=8 << 20),
        name="own_factor",
    )(shocks, sigma[None], index.T, alloc.T, *(value[None] for value in rest))


def spread():
    return (iota((16, 128), 1) % 16 == iota((16, 128), 0)).astype(F32)


def date_tables(rate_ref, dates):
    rate_col = rate_ref[...].T
    rates = []
    for m in range(2):
        rate = jnp.sum(rate_col[:, m : m + 1] * spread(), axis=0, keepdims=True)
        rates.append(jnp.broadcast_to(rate, (8, 128)))
    step_in = iota((8, 128), 0) % 4
    for g in range(GROUPS + 2):
        hz = (step_in + (4 * g + 1)).astype(F32)
        for m in range(2):
            power = (LOG2E * rates[m]) * hz
            discount = lax.exp2(-power)
            dates[g, 3 * m] = discount
            dates[g, 3 * m + 1] = hz * discount
            dates[g, 3 * m + 2] = lax.exp2(power) * UNIT


def cohort_order(tables_ref, table, plan_v, rank_ref):
    lanes = iota((8, 128), 1)
    chosen = 16 * iota((8, 128), 0) + lanes % 16
    halves = []
    for h in range(2):
        pieces = []
        for r in range(2):
            piece = jnp.zeros((8, 128), F32)
            for s in range(8):
                line = jnp.broadcast_to(tables_ref[8 * h + s, r : r + 1, :], (8, 128))
                line = jnp.take_along_axis(line, chosen, axis=1)
                piece = jnp.where(lanes // 16 == s, line, piece)
            pieces.append(piece)
        halves.append(jnp.concatenate(pieces, axis=0))
    params_t = jnp.concatenate(halves, axis=1)
    params = params_t.T
    key_col, key_row = params[:, KEY : KEY + 1], params_t[KEY : KEY + 1]
    rank_col = jnp.sum((key_row < key_col).astype(F32), axis=1, keepdims=True)
    rank_row = jnp.sum((key_col < key_row).astype(F32), axis=0, keepdims=True)
    place = (rank_col == iota((256, 256), 1).astype(F32)).astype(F32)
    ordered = dot01(params_t, place)
    rank_ref[...] = jnp.broadcast_to(rank_row, (8, 256))
    table[0] = ordered[:, :128]
    table[1] = ordered[:, 128:]

    mat = ordered[MAT : MAT + 1]
    first = jnp.where(ordered[TYPE : TYPE + 1] == 0.0, 1.0, mat)
    tile_of = iota((TILES, 256), 1) // 8 == iota((TILES, 256), 0)
    low = jnp.min(jnp.where(tile_of, first, 1e3), axis=1, keepdims=True)
    high = jnp.max(jnp.where(tile_of, mat, 0.0), axis=1, keepdims=True)
    low = jnp.floor((low - 1.0) * 0.25)
    count = jnp.floor((jnp.floor((high - 1.0) * 0.25) - low) * 0.5) + 1.0
    before = (iota((TILES, TILES), 1) < iota((TILES, TILES), 0)).astype(F32)
    begin = dot(before, jnp.broadcast_to(count, (TILES, 384)))
    item = iota((TILES, 384), 1).astype(F32)
    mine = (begin <= item) & (item < begin + count)
    tile_id = iota((TILES, 384), 0).astype(F32)
    plan_v[0:1, :] = jnp.sum(jnp.where(mine, tile_id, 0.0), axis=0, keepdims=True).astype(jnp.int32)
    place_g = jnp.where(mine, low + 2.0 * (item - begin) - 16.0, 0.0)
    place_g = 16.0 + jnp.sum(place_g, axis=0, keepdims=True)
    plan_v[1:2, :] = place_g.astype(jnp.int32)
    items = jnp.sum(mine.astype(F32), axis=(0, 1), keepdims=True)
    plan_v[2:8, :] = jnp.broadcast_to(items, (6, 384)).astype(jnp.int32)
    return params


def fund_levels(params, world_ref, level):
    spread_o = spread()
    sigma = params[:, SIG : SIG + 1].reshape(16, 2, 8, 1)[:, 0].reshape(128, 1)
    total = jnp.zeros((128, 128), F32)
    for m in range(2):
        shock = dot01(world_ref[:, m, :], spread_o, ((0,), (0,)))
        total = total + (
            (DRIFT - 0.5 * sigma * sigma) / 12.0 + sigma * shock / math.sqrt(12.0)
        )
        level[m] = jnp.exp(total)


def build_tiles(first_tile, count, table, level, weight_t, dwt, rows_t, acc_t):
    fund = iota((128, 128), 0).astype(F32)

    def build(j, carry):
        where = 8 * lax.rem(j, 16) + iota((16, 128), 1) // 16
        rows = jnp.take_along_axis(table[j // 16], where, axis=1)

        def row(k):
            return rows[k : k + 1]

        share_sum = row(4) + row(5) + row(6) + row(7)
        wts = jnp.zeros((128, 128), F32)
        for k in range(4):
            wts = wts + jnp.where(fund == row(k), row(4 + k) / share_sum, 0.0)
        dwt[j] = wts * row(ACC)
        zero = jnp.zeros((16, 8, 128), F32)
        for m in range(2):
            one = (wts * level[m]).reshape(16, 8, 128)
            both = [one, zero] if m == 0 else [zero, one]
            both = jnp.stack(both, axis=1).reshape(256, 128)
            weight_t[j, :, 128 * m : 128 * m + 128] = both.astype(BF16)
        death = row(TYPE) == 0.0
        mat = row(MAT)
        log_keep = jnp.log(1.0 - row(MORT))
        rows_t[j, 0:1] = jnp.where(death, 1.0, mat)
        rows_t[j, 1:2] = mat
        rows_t[j, 2:3] = jnp.where(death, log_keep, 0.0) * LOG2E
        shift = jnp.where(death, jnp.log(row(MORT)) - log_keep, log_keep * mat)
        rows_t[j, 3:4] = shift * LOG2E
        rows_t[j, 4:5] = row(FEE) * -LOG2E
        rows_t[j, 5:6] = row(RATIO) * UNIT
        acc_t[pl.ds(j, 1), :] = row(ACC)
        return carry

    lax.fori_loop(first_tile, first_tile + count, build, 0, unroll=2)


def gather_kernel(
    block_ref,
    table_ref,
    world_ref,
    rate_ref,
    blocks_ref,
    weight_t,
    dwt,
    rows_t,
    acc_t,
    dates,
    plan_v,
    rank_ref,
    tables_ref,
    table,
    level,
    send,
    recv,
    own,
):
    me = lax.axis_index("outer")
    row, col = me // 4, me % 4

    def at(dy, dx):
        return ((row + dy) % 4) * 4 + (col + dx) % 4

    peers = [at(0, 1), at(0, 3), at(1, 0), at(3, 0), at(0, 2), at(2, 0)]
    barrier = pltpu.get_barrier_semaphore()
    for peer in peers:
        pl.semaphore_signal(barrier, inc=1, device_id={"outer": peer}, device_id_type=MESH)
    pl.semaphore_wait(barrier, len(peers))

    started = []

    def post(number, peer, src, dst):
        copy = pltpu.make_async_remote_copy(
            src_ref=src,
            dst_ref=dst,
            send_sem=send.at[number],
            recv_sem=recv.at[number],
            device_id={"outer": peer},
            device_id_type=MESH,
        )
        copy.start()
        started.append(copy)
        return copy

    numbers = iter(range(MESSAGES))

    def piece(origin, first, count):
        return blocks_ref.at[origin, pl.ds(first, count)]

    def send_piece(peer, origin, first, count, mine=False):
        dst = piece(origin, first, count)
        src = block_ref.at[pl.ds(first, count)] if mine else dst
        return post(next(numbers), peer, src, dst)

    local = [
        pltpu.make_async_copy(table_ref, tables_ref.at[me], own.at[0]),
        pltpu.make_async_copy(block_ref, blocks_ref.at[me], own.at[1]),
    ]
    for copy in local:
        copy.start()

    across = [post(next(numbers), at(0, d), table_ref, tables_ref.at[me]) for d in (1, 3, 2)]

    def shift(color, first_step, second_step):
        return at(second_step, first_step) if color == 0 else at(first_step, second_step)

    near = []
    for color in range(2):
        q = 2 * color
        near.append([send_piece(shift(color, d, 0), me, q, 2, True) for d in (1, 3)])
    home = []
    for color in range(2):
        q = 2 * color
        home.append([send_piece(shift(color, 0, d), me, q, 2, True) for d in (1, 3)])

    date_tables(rate_ref, dates)

    second = []
    far = []
    for side in range(2):
        for color in range(2):
            q = 2 * color
            behind, onward = (3, 1) if side == 0 else (1, 3)
            near[color][side].wait_recv()
            origin = shift(color, behind, 0)
            far.append((color, side, send_piece(shift(color, onward, 0), origin, q + side, 1)))
            for way, d in enumerate((1, 3)):
                copy = send_piece(shift(color, 0, d), origin, q, 2)
                second.append((color, behind, q, 2, way, copy))

    last = []

    def hand_on(color, first, q, count, way, copy):
        copy.wait_recv()
        behind, onward = (3, 1) if way == 0 else (1, 3)
        quarter = 2 * color + way
        if not q <= quarter < q + count:
            return
        origin = shift(color, first, behind)
        last.append(send_piece(shift(color, 0, onward), origin, quarter, 1))

    for way in range(2):
        for color in range(2):
            hand_on(color, 0, 2 * color, 2, way, home[color][way])
    for copy in across:
        copy.wait_recv()
    local[0].wait()
    line = tables_ref.at[pl.ds(row * 4, 4)]
    down = [post(next(numbers), at(d, 0), line, line) for d in (1, 3, 2)]
    for color, side, copy in far:
        copy.wait_recv()
        for way, d in enumerate((1, 3)):
            fresh = send_piece(shift(color, 0, d), shift(color, 2, 0), 2 * color + side, 1)
            second.append((color, 2, 2 * color + side, 1, way, fresh))
    for copy in down:
        copy.wait_recv()
    params = cohort_order(tables_ref, table, plan_v, rank_ref)
    fund_levels(params, world_ref, level)
    for n, entry in enumerate(second):
        hand_on(*entry)
        if n % 2 == 0:
            build_tiles(2 * n, 4, table, level, weight_t, dwt, rows_t, acc_t)
    for copy in last:
        copy.wait_recv()
    local[1].wait()
    for copy in started:
        copy.wait_send()


def in_vmem(*arrays):
    return [pltpu.with_memory_space_constraint(array, pltpu.VMEM) for array in arrays]


def gather_outer(block, table, world, rate):
    vmem = pl.BlockSpec(memory_space=pltpu.VMEM)
    out_shape = (
        pltpu.VMEM((NOUT, 4, 16, 512), BF16),
        pltpu.VMEM((TILES, 256, 256), BF16),
        pltpu.VMEM((TILES, 128, 128), F32),
        pltpu.VMEM((TILES, 8, 128), F32),
        pltpu.VMEM((TILES, 128), F32),
        pltpu.VMEM((GROUPS + 2, 6, 8, 128), F32),
        pltpu.VMEM((8, 384), jnp.int32),
        pltpu.VMEM((8, 256), F32),
    )
    return pl.pallas_call(
        gather_kernel,
        out_shape=out_shape,
        in_specs=[vmem] * 4,
        out_specs=(vmem,) * len(out_shape),
        scratch_shapes=[
            pltpu.VMEM((NOUT, 2, 128), F32),
            pltpu.VMEM((2, 16, 128), F32),
            pltpu.VMEM((2, 128, 128), F32),
            pltpu.SemaphoreType.DMA((MESSAGES,)),
            pltpu.SemaphoreType.DMA((MESSAGES,)),
            pltpu.SemaphoreType.DMA((2,)),
        ],
        compiler_params=pltpu.CompilerParams(
            collective_id=0, has_side_effects=True, vmem_limit_bytes=24 << 20
        ),
        name="gather_outer",
    )(*in_vmem(block, table), world, rate.T)


def value_kernel(
    blocks_ref,
    weight_t,
    dwt,
    rows_t,
    acc_t,
    dates,
    plan_v,
    rank_ref,
    out_ref,
    fmat,
    fmat_t,
    plan,
    sums_t,
    sens,
    sums_in,
    kerns,
    sem,
):
    copy = pltpu.make_async_copy(plan_v, plan, sem)
    copy.start()
    step_in = iota((8, 128), 0) % 4
    for j in range(TILES):
        sens[j] = jnp.zeros((2, 128, 128), F32)
        sums_t[j] = jnp.zeros((4, 8, 128), F32)

    for g in range(GROUPS):
        cols = slice(128 * g, 128 * g + 128)
        part = blocks_ref[:, g // 4, :, 128 * (g % 4) : 128 * (g % 4) + 128]
        part = part.astype(F32).reshape(16, 2, 8, 128)
        for m in range(2):
            one = part[:, m].reshape(128, 128)
            fmat[m, :, cols] = one.astype(BF16)
        fmat_t[cols, :] = part.reshape(256, 128).T.astype(BF16)
    fmat[:, :, 2048:] = jnp.zeros((2, 128, 256), BF16)
    fmat_t[2048:, :] = jnp.zeros((256, 256), BF16)
    copy.wait()

    def raw(i, half):
        here = pl.ds(pl.multiple_of(plan[1, i] * 128, 128), 256)
        sums_in[half] = dot(fmat_t[here, :], weight_t[plan[0, i]])

    def group(j, g, half, slot):
        def wide(k):
            return jnp.broadcast_to(rows_t[j, k : k + 1], (8, 128))

        hz = (step_in + (4 * g + 1)).astype(F32)
        decay = lax.exp2(wide(2) * hz + wide(3))
        decay = jnp.where((hz >= wide(0)) & (hz <= wide(1)), decay, 0.0)
        fee_power = lax.exp2(wide(4) * hz)
        fee_decay = fee_power * decay
        strike = wide(5)
        part = slice(128 * slot, 128 * slot + 128)
        for m in range(2):
            growth = fee_power * dates[g, 3 * m + 2]
            y = sums_in[half, part, 128 * m : 128 * m + 128].reshape(16, 8, 128) * growth
            up = lax.exp2(strike - y)
            more = 1.0 + up
            soft = jnp.where(up < 2.0**-12, up, jnp.log(more))
            slope = up / more
            kerns[half, m, part, :] = (fee_decay * slope).reshape(128, 128).astype(BF16)
            soft_sum = jnp.sum(soft, axis=0)
            rho_sum = soft_sum + jnp.sum(slope * y, axis=0) * (1.0 / LOG2E)
            sums_t[j, 2 * m] += (decay * dates[g, 3 * m]) * soft_sum
            sums_t[j, 2 * m + 1] += (decay * dates[g, 3 * m + 1]) * rho_sum

    def flush(i, half):
        j = plan[0, i]
        here = pl.ds(pl.multiple_of(plan[1, i] * 128, 128), 256)
        for m in range(2):
            sens[j, m] += dot(fmat[m, :, here], kerns[half, m])

    def item_work(i, half):
        j, g = plan[0, i], plan[1, i]
        flush(jnp.maximum(i - 1, 0), 1 - half)
        raw(i + 1, 1 - half)
        group(j, g, half, 0)
        group(j, g + 1, half, 1)

    kerns[1] = jnp.zeros((2, 256, 128), BF16)
    raw(0, 0)

    def work(n, carry):
        item_work(2 * n, 0)
        item_work(2 * n + 1, 1)
        return carry

    pairs = (plan[2, 0] + 1) // 2
    lax.fori_loop(0, pairs, work, 0)
    flush(2 * pairs - 1, 1)

    def close(q, deltas):
        fresh = list(deltas)
        for k in range(4):
            j = 4 * q + k
            for m in range(2):
                fresh[m] = fresh[m] + dwt[j] * sens[j, m]
        return tuple(fresh)

    none = jnp.zeros((128, 128), F32)
    delta = lax.fori_loop(0, TILES // 4, close, (none, none))
    scale = acc_t[...] * (1.0 / 20.0 / 256.0)
    res_acc = []
    for n in range(4):
        value = jnp.sum(sums_t[:, n], axis=1)
        res_acc.append(value * (scale if n % 2 == 0 else -scale))

    rank_row = rank_ref[0:1, :]
    tile_row = jnp.floor(rank_row * 0.125)
    slot_row = rank_row - 8.0 * tile_row
    pick = (tile_row == iota((TILES, 256), 0).astype(F32)).astype(F32)
    keep = (slot_row == (iota((128, 256), 0) // 16).astype(F32)).astype(F32)
    for m in range(2):
        parts = []
        for n in range(2):
            lanes = dot01(res_acc[2 * m + n], pick, ((0,), (0,)))
            parts.append(jnp.sum((lanes * keep).reshape(8, 16, 256), axis=0))
        down = delta[m].T.reshape(8, 16, 128)
        parts.append(jnp.sum(down, axis=0) * (-1.0 / 256.0))
        line = jnp.concatenate(parts, axis=1)
        for o in range(16):
            for k in range(5):
                r = (o % 2) * 10 + m * 5 + k
                out_ref[o // 2, r : r + 1, :] = line[o : o + 1, 128 * k : 128 * k + 128]
    for b in range(NIN):
        out_ref[b, 20:SLAB, :] = jnp.zeros((SLAB - 20, 128), F32)


def revalue(*tables):
    vmem = pl.BlockSpec(memory_space=pltpu.VMEM)
    return pl.pallas_call(
        value_kernel,
        out_shape=pltpu.VMEM((NIN, SLAB, 128), F32),
        in_specs=[vmem] * len(tables),
        out_specs=vmem,
        scratch_shapes=[
            pltpu.VMEM((2, 128, 2304), BF16),
            pltpu.VMEM((2304, 256), BF16),
            pltpu.SMEM((8, 384), jnp.int32),
            pltpu.VMEM((TILES, 4, 8, 128), F32),
            pltpu.VMEM((TILES, 2, 128, 128), F32),
            pltpu.VMEM((2, 256, 256), F32),
            pltpu.VMEM((2, 2, 256, 128), BF16),
            pltpu.SemaphoreType.DMA(()),
        ],
        compiler_params=pltpu.CompilerParams(vmem_limit_bytes=32 << 20),
        name="revalue",
    )(*in_vmem(*tables))


def scatter_kernel(slabs_ref, inbox, send, recv, own):
    me = lax.axis_index("inner")
    barrier = pltpu.get_barrier_semaphore()
    for d in range(1, NIN):
        pl.semaphore_signal(
            barrier, inc=1, device_id={"inner": lax.rem(me + d, NIN)}, device_id_type=MESH
        )
    local = pltpu.make_async_copy(slabs_ref.at[me], inbox.at[0], own)
    local.start()
    pl.semaphore_wait(barrier, NIN - 1)
    copies = []
    for d in (4, 3, 5, 2, 6, 7, 1):
        peer = lax.rem(me + d, NIN)
        copy = pltpu.make_async_remote_copy(
            src_ref=slabs_ref.at[peer],
            dst_ref=inbox.at[d],
            send_sem=send.at[d],
            recv_sem=recv.at[d],
            device_id={"inner": peer},
            device_id_type=MESH,
        )
        copy.start()
        copies.append(copy)
    local.wait()
    for copy in copies:
        copy.wait()


def total_kernel(inbox_ref, res_ref, rho_ref, del_ref):
    total = inbox_ref[0]
    for d in range(1, NIN):
        total = total + inbox_ref[d]
    for o in range(2):
        for m in range(2):
            r = o * 10 + m * 5
            for k in range(2):
                lanes = slice(128 * k, 128 * k + 128)
                res_ref[o, m : m + 1, lanes] = total[r + k : r + k + 1]
                rho_ref[o, m : m + 1, lanes] = total[r + 2 + k : r + 3 + k]
            del_ref[o, m : m + 1, :] = total[r + 4 : r + 5]


def scatter_inner(slabs):
    vmem = pl.BlockSpec(memory_space=pltpu.VMEM)
    inbox = pl.pallas_call(
        scatter_kernel,
        out_shape=pltpu.VMEM((NIN, SLAB, 128), F32),
        in_specs=[vmem],
        out_specs=vmem,
        scratch_shapes=[
            pltpu.SemaphoreType.DMA((NIN,)),
            pltpu.SemaphoreType.DMA((NIN,)),
            pltpu.SemaphoreType.DMA(()),
        ],
        compiler_params=pltpu.CompilerParams(
            collective_id=1, has_side_effects=True, vmem_limit_bytes=8 << 20
        ),
        name="scatter_inner",
    )(*in_vmem(slabs))
    return pl.pallas_call(
        total_kernel,
        out_shape=(
            jax.ShapeDtypeStruct((2, 2, 256), F32),
            jax.ShapeDtypeStruct((2, 2, 256), F32),
            jax.ShapeDtypeStruct((2, 2, 128), F32),
        ),
        in_specs=[vmem],
        out_specs=(vmem, vmem, vmem),
        compiler_params=pltpu.CompilerParams(vmem_limit_bytes=8 << 20),
        name="total_inner",
    )(*in_vmem(inbox))


def shards(
    world_shocks,
    short_rate,
    inner_shocks,
    fund_volatility,
    fund_index,
    allocation,
    guarantee_type,
    maturity,
    guarantee_ratio,
    fee_rate,
    mortality,
    account,
):
    block, table = own_factor(
        inner_shocks,
        fund_volatility,
        fund_index,
        allocation,
        guarantee_type,
        maturity,
        guarantee_ratio,
        fee_rate,
        mortality,
        account,
    )
    slabs = revalue(*gather_outer(block, table, world_shocks, short_rate))
    return scatter_inner(slabs)


def solution(mesh):
    return jax.shard_map(
        shards,
        mesh=mesh,
        in_specs=(
            P("outer", None, None),
            P("outer", None),
            P(None, "outer", "inner"),
            P("outer"),
            P("outer", None),
            P("outer", None),
            P("outer"),
            P("outer"),
            P("outer"),
            P("outer"),
            P("outer"),
            P("outer"),
        ),
        out_specs=(
            P(("outer", "inner"), None, None),
            P(("outer", "inner"), None, None),
            P(("outer", "inner"), None, None),
        ),
        check_vma=False,
    )
```

```python
import functools
import math

import jax
import jax.numpy as jnp
from jax import lax
from jax.experimental import pallas as pl
from jax.experimental.pallas import tpu as pltpu
from jax.sharding import PartitionSpec as P

MESH = pl.DeviceIdType.MESH
HIGHEST = lax.Precision.HIGHEST
F32, BF16 = jnp.float32, jnp.bfloat16

STEPS = 64
DRIFT = 0.06
SMOOTH = 0.05
NOUT = 16
NIN = 8
TILES = 32
GROUPS = 16
TYPE, MAT, RATIO, FEE, MORT, ACC, SIG, KEY = 8, 9, 10, 11, 12, 13, 14, 15
SLAB = 24
MESSAGES = 50
LOG2E = 1.0 / math.log(2.0)
UNIT = LOG2E / SMOOTH


def dot(a, b, dims=((1,), (0,)), precision=None):
    return lax.dot_general(
        a, b, (dims, ((), ())), precision=precision, preferred_element_type=F32
    )


def in_vmem(*arrays):
    return [pltpu.with_memory_space_constraint(array, pltpu.VMEM) for array in arrays]


def in_hbm(*arrays):
    return [pltpu.with_memory_space_constraint(array, pltpu.HBM) for array in arrays]


def dot01(a, b, dims=((1,), (0,)), parts=3):
    b = b.astype(BF16)
    total = None
    for _ in range(parts):
        top = a.astype(BF16)
        a = a - top.astype(F32)
        one = dot(top, b, dims)
        total = one if total is None else total + one
    return total


def iota(shape, dim):
    return lax.broadcasted_iota(jnp.int32, shape, dim)


def factor_kernel(
    me,
    shocks_ref,
    sigma_ref,
    index_ref,
    alloc_ref,
    kind_ref,
    mat_ref,
    ratio_ref,
    fee_ref,
    mort_ref,
    acc_ref,
    out_ref,
    table_ref,
    scratch,
):
    me = lax.axis_index("outer") if me is None else me
    sigma_row = sigma_ref[...]
    mat = mat_ref[...].astype(F32)
    number = (iota((1, 16), 1) + 16 * me).astype(F32)
    key = jnp.where(kind_ref[...] == 0, 128.0 - mat, 256.0 + mat) * 256.0 + number
    scratch[...] = jnp.zeros((16, 128), F32)
    scratch[0:4, 0:16] = index_ref[...].astype(F32)
    scratch[4:8, 0:16] = alloc_ref[...]
    scratch[TYPE : TYPE + 1, 0:16] = kind_ref[...].astype(F32)
    scratch[MAT : MAT + 1, 0:16] = mat
    scratch[RATIO : RATIO + 1, 0:16] = ratio_ref[...]
    scratch[FEE : FEE + 1, 0:16] = fee_ref[...]
    scratch[MORT : MORT + 1, 0:16] = mort_ref[...]
    scratch[ACC : ACC + 1, 0:16] = acc_ref[...]
    scratch[SIG : SIG + 1, 0:8] = sigma_row
    scratch[KEY : KEY + 1, 0:16] = key
    for r in range(2):
        line = scratch[8 * r : 8 * r + 1, :]
        for k in range(1, 8):
            line = line + pltpu.roll(scratch[8 * r + k : 8 * r + k + 1, :], 16 * k, 1)
        table_ref[r : r + 1, :] = line

    rows = jnp.concatenate(
        [shocks_ref[m, :, 128 * j : 128 * j + 128] for m in range(2) for j in range(16)],
        axis=0,
    )
    src, dst = iota((128, 128), 0), iota((128, 128), 1)
    upper = (src // 64 == dst // 64) & (src <= dst)
    running = dot01(rows, upper.astype(F32))
    same = iota((8, 8), 0) == iota((8, 8), 1)
    sigma = jnp.sum(jnp.where(same, sigma_row, 0.0), axis=1, keepdims=True)
    sigma = jnp.broadcast_to(sigma[None], (32, 8, 1)).reshape(256, 1)
    horizon = (iota((1, 128), 1) % 64 + 1).astype(F32)
    factor = jnp.exp(-0.5 * sigma * sigma * horizon + sigma * running)
    lane = iota((8, 128), 1)
    months = []
    for m in range(2):
        regs = [factor[(m * 16 + j) * 8 : (m * 16 + j) * 8 + 8] for j in range(16)]
        for bit in range(4):
            low = (lane // (4 << bit)) % 2 == 0
            step = 4 << bit
            fresh = list(regs)
            for j in range(16):
                if j >> bit & 1:
                    continue
                k = j | 1 << bit
                a, b = regs[j], regs[k]
                fresh[j] = jnp.where(low, a, pltpu.roll(b, step, 1))
                fresh[k] = jnp.where(low, pltpu.roll(a, 128 - step, 1), b)
            regs = fresh
        months.append(regs)
    for g in range(16):
        both = jnp.concatenate([months[0][g], months[1][g]], axis=0)
        out_ref[g // 4, :, 128 * (g % 4) : 128 * (g % 4) + 128] = both.astype(BF16)


def own_factor(shocks, sigma, index, alloc, *rest, me=None):
    return pl.pallas_call(
        functools.partial(factor_kernel, me),
        out_shape=(
            pltpu.VMEM((4, 16, 512), BF16),
            pltpu.VMEM((2, 128), F32),
        ),
        scratch_shapes=[pltpu.VMEM((16, 128), F32)],
        compiler_params=pltpu.CompilerParams(vmem_limit_bytes=8 << 20),
        name="own_factor",
    )(*in_hbm(shocks, sigma[None], index.T, alloc.T, *(value[None] for value in rest)))


def spread():
    return (iota((16, 128), 1) % 16 == iota((16, 128), 0)).astype(F32)


def date_tables(rate_ref, dates):
    rate_col = rate_ref[...].T
    rates = []
    for m in range(2):
        rate = jnp.sum(rate_col[:, m : m + 1] * spread(), axis=0, keepdims=True)
        rates.append(jnp.broadcast_to(rate, (8, 128)))
    step_in = iota((8, 128), 0) % 4
    for g in range(GROUPS + 2):
        hz = (step_in + (4 * g + 1)).astype(F32)
        for m in range(2):
            power = (LOG2E * rates[m]) * hz
            discount = lax.exp2(-power)
            dates[g, 3 * m] = discount
            dates[g, 3 * m + 1] = hz * discount
            dates[g, 3 * m + 2] = lax.exp2(power) * UNIT


def cohort_order(tables_ref, table, plan_v, rank_ref):
    lanes = iota((8, 128), 1)
    chosen = 16 * iota((8, 128), 0) + lanes % 16
    halves = []
    for h in range(2):
        pieces = []
        for r in range(2):
            piece = jnp.zeros((8, 128), F32)
            for s in range(8):
                line = jnp.broadcast_to(tables_ref[8 * h + s, r : r + 1, :], (8, 128))
                line = jnp.take_along_axis(line, chosen, axis=1)
                piece = jnp.where(lanes // 16 == s, line, piece)
            pieces.append(piece)
        halves.append(jnp.concatenate(pieces, axis=0))
    params_t = jnp.concatenate(halves, axis=1)
    params = params_t.T
    key_col, key_row = params[:, KEY : KEY + 1], params_t[KEY : KEY + 1]
    rank_col = jnp.sum((key_row < key_col).astype(F32), axis=1, keepdims=True)
    rank_row = jnp.sum((key_col < key_row).astype(F32), axis=0, keepdims=True)
    place = (rank_col == iota((256, 256), 1).astype(F32)).astype(F32)
    ordered = dot01(params_t, place)
    rank_ref[...] = jnp.broadcast_to(rank_row, (8, 256))
    table[0] = ordered[:, :128]
    table[1] = ordered[:, 128:]

    mat = ordered[MAT : MAT + 1]
    first = jnp.where(ordered[TYPE : TYPE + 1] == 0.0, 1.0, mat)
    tile_of = iota((TILES, 256), 1) // 8 == iota((TILES, 256), 0)
    low = jnp.min(jnp.where(tile_of, first, 1e3), axis=1, keepdims=True)
    high = jnp.max(jnp.where(tile_of, mat, 0.0), axis=1, keepdims=True)
    low = jnp.floor((low - 1.0) * 0.25)
    count = jnp.floor((jnp.floor((high - 1.0) * 0.25) - low) * 0.5) + 1.0
    before = (iota((TILES, TILES), 1) < iota((TILES, TILES), 0)).astype(F32)
    begin = dot(before, jnp.broadcast_to(count, (TILES, 384)))
    item = iota((TILES, 384), 1).astype(F32)
    mine = (begin <= item) & (item < begin + count)
    tile_id = iota((TILES, 384), 0).astype(F32)
    plan_v[0:1, :] = jnp.sum(jnp.where(mine, tile_id, 0.0), axis=0, keepdims=True).astype(jnp.int32)
    place_g = jnp.where(mine, low + 2.0 * (item - begin) - 16.0, 0.0)
    place_g = 16.0 + jnp.sum(place_g, axis=0, keepdims=True)
    plan_v[1:2, :] = place_g.astype(jnp.int32)
    items = jnp.sum(mine.astype(F32), axis=(0, 1), keepdims=True)
    plan_v[2:8, :] = jnp.broadcast_to(items, (6, 384)).astype(jnp.int32)
    return params


def fund_levels(params, world_ref, level):
    spread_o = spread()
    sigma = params[:, SIG : SIG + 1].reshape(16, 2, 8, 1)[:, 0].reshape(128, 1)
    total = jnp.zeros((128, 128), F32)
    for m in range(2):
        shock = dot01(world_ref[:, m, :], spread_o, ((0,), (0,)))
        total = total + (
            (DRIFT - 0.5 * sigma * sigma) / 12.0 + sigma * shock / math.sqrt(12.0)
        )
        level[m] = jnp.exp(total)


def build_tiles(first_tile, count, table, level, weight_t, dwt, rows_t, acc_t):
    fund = iota((128, 128), 0).astype(F32)

    def build(j, carry):
        where = 8 * lax.rem(j, 16) + iota((16, 128), 1) // 16
        rows = jnp.take_along_axis(table[j // 16], where, axis=1)

        def row(k):
            return rows[k : k + 1]

        share_sum = row(4) + row(5) + row(6) + row(7)
        wts = jnp.zeros((128, 128), F32)
        for k in range(4):
            wts = wts + jnp.where(fund == row(k), row(4 + k) / share_sum, 0.0)
        dwt[j] = wts * row(ACC)
        zero = jnp.zeros((16, 8, 128), F32)
        for m in range(2):
            one = (wts * level[m]).reshape(16, 8, 128)
            both = [one, zero] if m == 0 else [zero, one]
            both = jnp.stack(both, axis=1).reshape(256, 128)
            weight_t[j, :, 128 * m : 128 * m + 128] = both.astype(BF16)
        death = row(TYPE) == 0.0
        mat = row(MAT)
        log_keep = jnp.log(1.0 - row(MORT))
        rows_t[j, 0:1] = jnp.where(death, 1.0, mat)
        rows_t[j, 1:2] = mat
        rows_t[j, 2:3] = jnp.where(death, log_keep, 0.0) * LOG2E
        shift = jnp.where(death, jnp.log(row(MORT)) - log_keep, log_keep * mat)
        rows_t[j, 3:4] = shift * LOG2E
        rows_t[j, 4:5] = row(FEE) * -LOG2E
        rows_t[j, 5:6] = row(RATIO) * UNIT
        acc_t[pl.ds(j, 1), :] = row(ACC)
        return carry

    lax.fori_loop(first_tile, first_tile + count, build, 0, unroll=2)


def gather_kernel(
    block_ref,
    table_ref,
    world_ref,
    rate_ref,
    blocks_ref,
    weight_t,
    dwt,
    rows_t,
    acc_t,
    dates,
    plan_v,
    rank_ref,
    tables_ref,
    table,
    level,
    send,
    recv,
    own,
):
    me = lax.axis_index("outer")
    row, col = me // 4, me % 4

    def at(dy, dx):
        return ((row + dy) % 4) * 4 + (col + dx) % 4

    peers = [at(0, 1), at(0, 3), at(1, 0), at(3, 0), at(0, 2), at(2, 0)]
    barrier = pltpu.get_barrier_semaphore()
    for peer in peers:
        pl.semaphore_signal(barrier, inc=1, device_id={"outer": peer}, device_id_type=MESH)
    pl.semaphore_wait(barrier, len(peers))

    started = []

    def post(number, peer, src, dst):
        copy = pltpu.make_async_remote_copy(
            src_ref=src,
            dst_ref=dst,
            send_sem=send.at[number],
            recv_sem=recv.at[number],
            device_id={"outer": peer},
            device_id_type=MESH,
        )
        copy.start()
        started.append(copy)
        return copy

    numbers = iter(range(MESSAGES))

    def piece(origin, first, count):
        return blocks_ref.at[origin, pl.ds(first, count)]

    def send_piece(peer, origin, first, count, mine=False):
        dst = piece(origin, first, count)
        src = block_ref.at[pl.ds(first, count)] if mine else dst
        return post(next(numbers), peer, src, dst)

    local = [
        pltpu.make_async_copy(table_ref, tables_ref.at[me], own.at[0]),
        pltpu.make_async_copy(block_ref, blocks_ref.at[me], own.at[1]),
    ]
    for copy in local:
        copy.start()

    across = [post(next(numbers), at(0, d), table_ref, tables_ref.at[me]) for d in (1, 3, 2)]

    def shift(color, first_step, second_step):
        return at(second_step, first_step) if color == 0 else at(first_step, second_step)

    near = []
    for color in range(2):
        q = 2 * color
        near.append([send_piece(shift(color, d, 0), me, q, 2, True) for d in (1, 3)])
    home = []
    for color in range(2):
        q = 2 * color
        home.append([send_piece(shift(color, 0, d), me, q, 2, True) for d in (1, 3)])

    date_tables(rate_ref, dates)

    second = []
    far = []
    for side in range(2):
        for color in range(2):
            q = 2 * color
            behind, onward = (3, 1) if side == 0 else (1, 3)
            near[color][side].wait_recv()
            origin = shift(color, behind, 0)
            far.append((color, side, send_piece(shift(color, onward, 0), origin, q + side, 1)))
            for way, d in enumerate((1, 3)):
                copy = send_piece(shift(color, 0, d), origin, q, 2)
                second.append((color, behind, q, 2, way, copy))

    last = []

    def hand_on(color, first, q, count, way, copy):
        copy.wait_recv()
        behind, onward = (3, 1) if way == 0 else (1, 3)
        quarter = 2 * color + way
        if not q <= quarter < q + count:
            return
        origin = shift(color, first, behind)
        last.append(send_piece(shift(color, 0, onward), origin, quarter, 1))

    for way in range(2):
        for color in range(2):
            hand_on(color, 0, 2 * color, 2, way, home[color][way])
    for copy in across:
        copy.wait_recv()
    local[0].wait()
    line = tables_ref.at[pl.ds(row * 4, 4)]
    down = [post(next(numbers), at(d, 0), line, line) for d in (1, 3, 2)]
    for color, side, copy in far:
        copy.wait_recv()
        for way, d in enumerate((1, 3)):
            fresh = send_piece(shift(color, 0, d), shift(color, 2, 0), 2 * color + side, 1)
            second.append((color, 2, 2 * color + side, 1, way, fresh))
    for copy in down:
        copy.wait_recv()
    params = cohort_order(tables_ref, table, plan_v, rank_ref)
    fund_levels(params, world_ref, level)
    for n, entry in enumerate(second):
        hand_on(*entry)
        if n % 2 == 0:
            build_tiles(2 * n, 4, table, level, weight_t, dwt, rows_t, acc_t)
    for copy in last:
        copy.wait_recv()
    local[1].wait()
    for copy in started:
        copy.wait_send()


def gather_outer(block, table, world, rate):
    vmem = pl.BlockSpec(memory_space=pltpu.VMEM)
    out_shape = (
        pltpu.VMEM((NOUT, 4, 16, 512), BF16),
        pltpu.VMEM((TILES, 256, 256), BF16),
        pltpu.VMEM((TILES, 128, 128), F32),
        pltpu.VMEM((TILES, 8, 128), F32),
        pltpu.VMEM((TILES, 128), F32),
        pltpu.VMEM((GROUPS + 2, 6, 8, 128), F32),
        pltpu.VMEM((8, 384), jnp.int32),
        pltpu.VMEM((8, 256), F32),
    )
    return pl.pallas_call(
        gather_kernel,
        out_shape=out_shape,
        in_specs=[vmem] * 4,
        out_specs=(vmem,) * len(out_shape),
        scratch_shapes=[
            pltpu.VMEM((NOUT, 2, 128), F32),
            pltpu.VMEM((2, 16, 128), F32),
            pltpu.VMEM((2, 128, 128), F32),
            pltpu.SemaphoreType.DMA((MESSAGES,)),
            pltpu.SemaphoreType.DMA((MESSAGES,)),
            pltpu.SemaphoreType.DMA((2,)),
        ],
        compiler_params=pltpu.CompilerParams(
            collective_id=0, has_side_effects=True, vmem_limit_bytes=24 << 20
        ),
        name="gather_outer",
    )(*in_vmem(block, table), *in_hbm(world, rate.T))


def value_kernel(
    blocks_ref,
    weight_t,
    dwt,
    rows_t,
    acc_t,
    dates,
    plan_v,
    rank_ref,
    out_ref,
    fmat,
    fmat_t,
    plan,
    sums_t,
    sens,
    sums_in,
    kerns,
    sem,
):
    copy = pltpu.make_async_copy(plan_v, plan, sem)
    copy.start()
    step_in = iota((8, 128), 0) % 4
    for j in range(TILES):
        sens[j] = jnp.zeros((2, 128, 128), F32)
        sums_t[j] = jnp.zeros((4, 8, 128), F32)

    for g in range(GROUPS):
        cols = slice(128 * g, 128 * g + 128)
        part = blocks_ref[:, g // 4, :, 128 * (g % 4) : 128 * (g % 4) + 128]
        part = part.astype(F32).reshape(16, 2, 8, 128)
        for m in range(2):
            one = part[:, m].reshape(128, 128)
            fmat[m, :, cols] = one.astype(BF16)
        fmat_t[cols, :] = part.reshape(256, 128).T.astype(BF16)
    fmat[:, :, 2048:] = jnp.zeros((2, 128, 256), BF16)
    fmat_t[2048:, :] = jnp.zeros((256, 256), BF16)
    copy.wait()

    def raw(i, half):
        here = pl.ds(pl.multiple_of(plan[1, i] * 128, 128), 256)
        sums_in[half] = dot(fmat_t[here, :], weight_t[plan[0, i]])

    def group(j, g, half, slot):
        def wide(k):
            return jnp.broadcast_to(rows_t[j, k : k + 1], (8, 128))

        hz = (step_in + (4 * g + 1)).astype(F32)
        decay = lax.exp2(wide(2) * hz + wide(3))
        decay = jnp.where((hz >= wide(0)) & (hz <= wide(1)), decay, 0.0)
        fee_power = lax.exp2(wide(4) * hz)
        fee_decay = fee_power * decay
        strike = wide(5)
        part = slice(128 * slot, 128 * slot + 128)
        for m in range(2):
            growth = fee_power * dates[g, 3 * m + 2]
            y = sums_in[half, part, 128 * m : 128 * m + 128].reshape(16, 8, 128) * growth
            up = lax.exp2(strike - y)
            more = 1.0 + up
            slope = up / more
            some = jnp.concatenate(
                [up[0:4] + up[4:8] + up[8:12], up[12:14] + up[14:16]], axis=0
            )
            many = jnp.concatenate(
                [more[0:4] * more[4:8] * more[8:12], more[12:14] * more[14:16]], axis=0
            )
            soft_sum = jnp.sum(jnp.where(some < 2.0**-12, some, jnp.log(many)), axis=0)
            kerns[half, m, part, :] = (fee_decay * slope).reshape(128, 128).astype(BF16)
            rho_sum = soft_sum + jnp.sum(slope * y, axis=0) * (1.0 / LOG2E)
            sums_t[j, 2 * m] += (decay * dates[g, 3 * m]) * soft_sum
            sums_t[j, 2 * m + 1] += (decay * dates[g, 3 * m + 1]) * rho_sum

    def flush(i, half):
        j = plan[0, i]
        here = pl.ds(pl.multiple_of(plan[1, i] * 128, 128), 256)
        for m in range(2):
            sens[j, m] += dot(fmat[m, :, here], kerns[half, m])

    def item_work(i, half):
        j, g = plan[0, i], plan[1, i]
        flush(jnp.maximum(i - 1, 0), 1 - half)
        raw(i + 1, 1 - half)
        group(j, g, half, 0)
        group(j, g + 1, half, 1)

    kerns[1] = jnp.zeros((2, 256, 128), BF16)
    raw(0, 0)

    def work(n, carry):
        item_work(2 * n, 0)
        item_work(2 * n + 1, 1)
        return carry

    pairs = (plan[2, 0] + 1) // 2
    lax.fori_loop(0, pairs, work, 0)
    flush(2 * pairs - 1, 1)

    def close(q, deltas):
        fresh = list(deltas)
        for k in range(4):
            j = 4 * q + k
            for m in range(2):
                fresh[m] = fresh[m] + dwt[j] * sens[j, m]
        return tuple(fresh)

    none = jnp.zeros((128, 128), F32)
    delta = lax.fori_loop(0, TILES // 4, close, (none, none))
    scale = acc_t[...] * (1.0 / 20.0 / 256.0)
    res_acc = []
    for n in range(4):
        value = jnp.sum(sums_t[:, n], axis=1)
        res_acc.append(value * (scale if n % 2 == 0 else -scale))

    rank_row = rank_ref[0:1, :]
    tile_row = jnp.floor(rank_row * 0.125)
    slot_row = rank_row - 8.0 * tile_row
    pick = (tile_row == iota((TILES, 256), 0).astype(F32)).astype(F32)
    keep = (slot_row == (iota((128, 256), 0) // 16).astype(F32)).astype(F32)
    for m in range(2):
        parts = []
        for n in range(2):
            lanes = dot01(res_acc[2 * m + n], pick, ((0,), (0,)))
            parts.append(jnp.sum((lanes * keep).reshape(8, 16, 256), axis=0))
        down = delta[m].T.reshape(8, 16, 128)
        parts.append(jnp.sum(down, axis=0) * (-1.0 / 256.0))
        line = jnp.concatenate(parts, axis=1)
        for o in range(16):
            for k in range(5):
                r = (o % 2) * 10 + m * 5 + k
                out_ref[o // 2, r : r + 1, :] = line[o : o + 1, 128 * k : 128 * k + 128]
    for b in range(NIN):
        out_ref[b, 20:SLAB, :] = jnp.zeros((SLAB - 20, 128), F32)


def revalue(*tables):
    vmem = pl.BlockSpec(memory_space=pltpu.VMEM)
    return pl.pallas_call(
        value_kernel,
        out_shape=pltpu.VMEM((NIN, SLAB, 128), F32),
        in_specs=[vmem] * len(tables),
        out_specs=vmem,
        scratch_shapes=[
            pltpu.VMEM((2, 128, 2304), BF16),
            pltpu.VMEM((2304, 256), BF16),
            pltpu.SMEM((8, 384), jnp.int32),
            pltpu.VMEM((TILES, 4, 8, 128), F32),
            pltpu.VMEM((TILES, 2, 128, 128), F32),
            pltpu.VMEM((2, 256, 256), F32),
            pltpu.VMEM((2, 2, 256, 128), BF16),
            pltpu.SemaphoreType.DMA(()),
        ],
        compiler_params=pltpu.CompilerParams(vmem_limit_bytes=32 << 20),
        name="revalue",
    )(*in_vmem(*tables))


def scatter_kernel(slabs_ref, inbox, send, recv, own):
    me = lax.axis_index("inner")
    barrier = pltpu.get_barrier_semaphore()
    for d in range(1, NIN):
        pl.semaphore_signal(
            barrier, inc=1, device_id={"inner": lax.rem(me + d, NIN)}, device_id_type=MESH
        )
    local = pltpu.make_async_copy(slabs_ref.at[me], inbox.at[0], own)
    local.start()
    pl.semaphore_wait(barrier, NIN - 1)
    copies = []
    for d in (4, 3, 5, 2, 6, 7, 1):
        peer = lax.rem(me + d, NIN)
        copy = pltpu.make_async_remote_copy(
            src_ref=slabs_ref.at[peer],
            dst_ref=inbox.at[d],
            send_sem=send.at[d],
            recv_sem=recv.at[d],
            device_id={"inner": peer},
            device_id_type=MESH,
        )
        copy.start()
        copies.append(copy)
    local.wait()
    for copy in copies:
        copy.wait()


def total_kernel(inbox_ref, res_ref, rho_ref, del_ref):
    total = inbox_ref[0]
    for d in range(1, NIN):
        total = total + inbox_ref[d]
    for o in range(2):
        for m in range(2):
            r = o * 10 + m * 5
            for k in range(2):
                lanes = slice(128 * k, 128 * k + 128)
                res_ref[o, m : m + 1, lanes] = total[r + k : r + k + 1]
                rho_ref[o, m : m + 1, lanes] = total[r + 2 + k : r + 3 + k]
            del_ref[o, m : m + 1, :] = total[r + 4 : r + 5]


def scatter_inner(slabs):
    vmem = pl.BlockSpec(memory_space=pltpu.VMEM)
    inbox = pl.pallas_call(
        scatter_kernel,
        out_shape=pltpu.VMEM((NIN, SLAB, 128), F32),
        in_specs=[vmem],
        out_specs=vmem,
        scratch_shapes=[
            pltpu.SemaphoreType.DMA((NIN,)),
            pltpu.SemaphoreType.DMA((NIN,)),
            pltpu.SemaphoreType.DMA(()),
        ],
        compiler_params=pltpu.CompilerParams(
            collective_id=1, has_side_effects=True, vmem_limit_bytes=8 << 20
        ),
        name="scatter_inner",
    )(*in_vmem(slabs))
    return pl.pallas_call(
        total_kernel,
        out_shape=(
            jax.ShapeDtypeStruct((2, 2, 256), F32),
            jax.ShapeDtypeStruct((2, 2, 256), F32),
            jax.ShapeDtypeStruct((2, 2, 128), F32),
        ),
        in_specs=[vmem],
        out_specs=(vmem, vmem, vmem),
        compiler_params=pltpu.CompilerParams(vmem_limit_bytes=8 << 20),
        name="total_inner",
    )(*in_vmem(inbox))


def shards(
    world_shocks,
    short_rate,
    inner_shocks,
    fund_volatility,
    fund_index,
    allocation,
    guarantee_type,
    maturity,
    guarantee_ratio,
    fee_rate,
    mortality,
    account,
):
    block, table = own_factor(
        inner_shocks,
        fund_volatility,
        fund_index,
        allocation,
        guarantee_type,
        maturity,
        guarantee_ratio,
        fee_rate,
        mortality,
        account,
    )
    slabs = revalue(*gather_outer(block, table, world_shocks, short_rate))
    return scatter_inner(slabs)


def solution(mesh):
    return jax.shard_map(
        shards,
        mesh=mesh,
        in_specs=(
            P("outer", None, None),
            P("outer", None),
            P(None, "outer", "inner"),
            P("outer"),
            P("outer", None),
            P("outer", None),
            P("outer"),
            P("outer"),
            P("outer"),
            P("outer"),
            P("outer"),
            P("outer"),
        ),
        out_specs=(
            P(("outer", "inner"), None, None),
            P(("outer", "inner"), None, None),
            P(("outer", "inner"), None, None),
        ),
        check_vma=False,
    )
```

```python
import functools
import math

import jax
import jax.numpy as jnp
from jax import lax
from jax.experimental import pallas as pl
from jax.experimental.pallas import tpu as pltpu
from jax.sharding import PartitionSpec as P

MESH = pl.DeviceIdType.MESH
HIGHEST = lax.Precision.HIGHEST
F32, BF16 = jnp.float32, jnp.bfloat16

STEPS = 64
DRIFT = 0.06
SMOOTH = 0.05
NOUT = 16
NIN = 8
TILES = 32
GROUPS = 16
TYPE, MAT, RATIO, FEE, MORT, ACC, SIG, KEY = 8, 9, 10, 11, 12, 13, 14, 15
SLAB = 24
MESSAGES = 44
UNROLL = 4
LOG2E = 1.0 / math.log(2.0)
UNIT = LOG2E / SMOOTH


def dot(a, b, dims=((1,), (0,)), precision=None):
    return lax.dot_general(
        a, b, (dims, ((), ())), precision=precision, preferred_element_type=F32
    )


def in_vmem(*arrays):
    return [pltpu.with_memory_space_constraint(array, pltpu.VMEM) for array in arrays]


def in_hbm(*arrays):
    return [pltpu.with_memory_space_constraint(array, pltpu.HBM) for array in arrays]


def dot01(a, b, dims=((1,), (0,)), parts=3):
    b = b.astype(BF16)
    total = None
    for _ in range(parts):
        top = a.astype(BF16)
        a = a - top.astype(F32)
        one = dot(top, b, dims)
        total = one if total is None else total + one
    return total


def iota(shape, dim):
    return lax.broadcasted_iota(jnp.int32, shape, dim)


def own_factor(
    me,
    shocks_ref,
    sigma_ref,
    index_ref,
    alloc_ref,
    kind_ref,
    mat_ref,
    ratio_ref,
    fee_ref,
    mort_ref,
    acc_ref,
    out_ref,
    table_ref,
    scratch,
):
    sigma_row = sigma_ref[...]
    mat = mat_ref[...].astype(F32)
    number = (iota((1, 16), 1) + 16 * me).astype(F32)
    key = jnp.where(kind_ref[...] == 0, 128.0 - mat, 256.0 + mat) * 256.0 + number
    scratch[...] = jnp.zeros((16, 128), F32)
    scratch[0:4, 0:16] = index_ref[...].astype(F32)
    scratch[4:8, 0:16] = alloc_ref[...]
    scratch[TYPE : TYPE + 1, 0:16] = kind_ref[...].astype(F32)
    scratch[MAT : MAT + 1, 0:16] = mat
    scratch[RATIO : RATIO + 1, 0:16] = ratio_ref[...]
    scratch[FEE : FEE + 1, 0:16] = fee_ref[...]
    scratch[MORT : MORT + 1, 0:16] = mort_ref[...]
    scratch[ACC : ACC + 1, 0:16] = acc_ref[...]
    scratch[SIG : SIG + 1, 0:8] = sigma_row
    scratch[KEY : KEY + 1, 0:16] = key
    for r in range(2):
        line = scratch[8 * r : 8 * r + 1, :]
        for k in range(1, 8):
            line = line + pltpu.roll(scratch[8 * r + k : 8 * r + k + 1, :], 16 * k, 1)
        table_ref[r : r + 1, :] = line

    rows = jnp.concatenate(
        [shocks_ref[m, :, 128 * j : 128 * j + 128] for m in range(2) for j in range(16)],
        axis=0,
    )
    src, dst = iota((128, 128), 0), iota((128, 128), 1)
    upper = (src // 64 == dst // 64) & (src <= dst)
    running = dot01(rows, upper.astype(F32))
    same = iota((8, 8), 0) == iota((8, 8), 1)
    sigma = jnp.sum(jnp.where(same, sigma_row, 0.0), axis=1, keepdims=True)
    sigma = jnp.broadcast_to(sigma[None], (32, 8, 1)).reshape(256, 1)
    horizon = (iota((1, 128), 1) % 64 + 1).astype(F32)
    factor = jnp.exp(-0.5 * sigma * sigma * horizon + sigma * running)
    lane = iota((8, 128), 1)
    months = []
    for m in range(2):
        regs = [factor[(m * 16 + j) * 8 : (m * 16 + j) * 8 + 8] for j in range(16)]
        for bit in range(4):
            low = (lane // (4 << bit)) % 2 == 0
            step = 4 << bit
            fresh = list(regs)
            for j in range(16):
                if j >> bit & 1:
                    continue
                k = j | 1 << bit
                a, b = regs[j], regs[k]
                fresh[j] = jnp.where(low, a, pltpu.roll(b, step, 1))
                fresh[k] = jnp.where(low, pltpu.roll(a, 128 - step, 1), b)
            regs = fresh
        months.append(regs)
    for g in range(16):
        both = jnp.concatenate([months[0][g], months[1][g]], axis=0)
        out_ref[g // 4, :, 128 * (g % 4) : 128 * (g % 4) + 128] = both.astype(BF16)


def spread():
    return (iota((16, 128), 1) % 16 == iota((16, 128), 0)).astype(F32)


def date_tables(rate_ref, dates):
    rate_col = rate_ref[...].T
    rates = []
    for m in range(2):
        rate = jnp.sum(rate_col[:, m : m + 1] * spread(), axis=0, keepdims=True)
        rates.append(jnp.broadcast_to(rate, (8, 128)))
    step_in = iota((8, 128), 0) % 4
    for g in range(GROUPS + 2):
        hz = (step_in + (4 * g + 1)).astype(F32)
        for m in range(2):
            power = (LOG2E * rates[m]) * hz
            discount = lax.exp2(-power)
            dates[g, 3 * m] = discount
            dates[g, 3 * m + 1] = hz * discount
            dates[g, 3 * m + 2] = lax.exp2(power) * UNIT


def cohort_order(tables_ref, table, plan_v, rank_ref):
    lanes = iota((8, 128), 1)
    chosen = 16 * iota((8, 128), 0) + lanes % 16
    halves = []
    for h in range(2):
        pieces = []
        for r in range(2):
            piece = jnp.zeros((8, 128), F32)
            for s in range(8):
                line = jnp.broadcast_to(tables_ref[8 * h + s, r : r + 1, :], (8, 128))
                line = jnp.take_along_axis(line, chosen, axis=1)
                piece = jnp.where(lanes // 16 == s, line, piece)
            pieces.append(piece)
        halves.append(jnp.concatenate(pieces, axis=0))
    params_t = jnp.concatenate(halves, axis=1)
    params = params_t.T
    key_col, key_row = params[:, KEY : KEY + 1], params_t[KEY : KEY + 1]
    rank_col = jnp.sum((key_row < key_col).astype(F32), axis=1, keepdims=True)
    rank_row = jnp.sum((key_col < key_row).astype(F32), axis=0, keepdims=True)
    place = (rank_col == iota((256, 256), 1).astype(F32)).astype(F32)
    ordered = dot01(params_t, place)
    rank_ref[...] = jnp.broadcast_to(rank_row, (8, 256))
    table[0] = ordered[:, :128]
    table[1] = ordered[:, 128:]

    mat = ordered[MAT : MAT + 1]
    first = jnp.where(ordered[TYPE : TYPE + 1] == 0.0, 1.0, mat)
    tile_of = iota((TILES, 256), 1) // 8 == iota((TILES, 256), 0)
    low = jnp.min(jnp.where(tile_of, first, 1e3), axis=1, keepdims=True)
    high = jnp.max(jnp.where(tile_of, mat, 0.0), axis=1, keepdims=True)
    low = jnp.floor((low - 1.0) * 0.25)
    count = jnp.floor((jnp.floor((high - 1.0) * 0.25) - low) * 0.5) + 1.0
    before = (iota((TILES, TILES), 1) < iota((TILES, TILES), 0)).astype(F32)
    begin = dot(before, jnp.broadcast_to(count, (TILES, 384)))
    item = iota((TILES, 384), 1).astype(F32)
    mine = (begin <= item) & (item < begin + count)
    tile_id = iota((TILES, 384), 0).astype(F32)
    plan_v[0:1, :] = jnp.sum(jnp.where(mine, tile_id, 0.0), axis=0, keepdims=True).astype(jnp.int32)
    place_g = jnp.where(mine, low + 2.0 * (item - begin) - 16.0, 0.0)
    place_g = 16.0 + jnp.sum(place_g, axis=0, keepdims=True)
    plan_v[1:2, :] = place_g.astype(jnp.int32)
    items = jnp.sum(mine.astype(F32), axis=(0, 1), keepdims=True)
    plan_v[2:8, :] = jnp.broadcast_to(items, (6, 384)).astype(jnp.int32)
    return params


def fund_levels(params, world_ref, level):
    spread_o = spread()
    sigma = params[:, SIG : SIG + 1].reshape(16, 2, 8, 1)[:, 0].reshape(128, 1)
    total = jnp.zeros((128, 128), F32)
    for m in range(2):
        shock = dot01(world_ref[:, m, :], spread_o, ((0,), (0,)))
        total = total + (
            (DRIFT - 0.5 * sigma * sigma) / 12.0 + sigma * shock / math.sqrt(12.0)
        )
        level[m] = jnp.exp(total)


def build_tiles(first_tile, count, table, level, weight_t, dwt, rows_t, acc_t):
    fund = iota((128, 128), 0).astype(F32)

    def build(j, carry):
        where = 8 * lax.rem(j, 16) + iota((16, 128), 1) // 16
        rows = jnp.take_along_axis(table[j // 16], where, axis=1)

        def row(k):
            return rows[k : k + 1]

        share_sum = row(4) + row(5) + row(6) + row(7)
        wts = jnp.zeros((128, 128), F32)
        for k in range(4):
            wts = wts + jnp.where(fund == row(k), row(4 + k) / share_sum, 0.0)
        dwt[j] = wts * row(ACC)
        zero = jnp.zeros((16, 8, 128), F32)
        for m in range(2):
            one = (wts * level[m]).reshape(16, 8, 128)
            both = [one, zero] if m == 0 else [zero, one]
            both = jnp.stack(both, axis=1).reshape(256, 128)
            weight_t[j, :, 128 * m : 128 * m + 128] = both.astype(BF16)
        death = row(TYPE) == 0.0
        mat = row(MAT)
        log_keep = jnp.log(1.0 - row(MORT))
        rows_t[j, 0:1] = jnp.where(death, 1.0, mat)
        rows_t[j, 1:2] = mat
        rows_t[j, 2:3] = jnp.where(death, log_keep, 0.0) * LOG2E
        shift = jnp.where(death, jnp.log(row(MORT)) - log_keep, log_keep * mat)
        rows_t[j, 3:4] = shift * LOG2E
        rows_t[j, 4:5] = row(FEE) * -LOG2E
        rows_t[j, 5:6] = row(RATIO) * UNIT
        acc_t[pl.ds(j, 1), :] = row(ACC)
        return carry

    lax.fori_loop(first_tile, first_tile + count, build, 0, unroll=2)


def gather_kernel(
    shocks_ref,
    sigma_ref,
    index_ref,
    alloc_ref,
    kind_ref,
    mat_ref,
    ratio_ref,
    fee_ref,
    mort_ref,
    account_ref,
    world_ref,
    rate_ref,
    blocks_ref,
    weight_t,
    dwt,
    rows_t,
    acc_t,
    dates,
    plan_v,
    rank_ref,
    block_ref,
    table_ref,
    scratch,
    tables_ref,
    table,
    level,
    send,
    recv,
    own,
):
    me = lax.axis_index("outer")
    row, col = me // 4, me % 4

    def at(dy, dx):
        return ((row + dy) % 4) * 4 + (col + dx) % 4

    peers = [at(0, 1), at(0, 3), at(1, 0), at(3, 0), at(0, 2), at(2, 0)]
    barrier = pltpu.get_barrier_semaphore()
    for peer in peers:
        pl.semaphore_signal(barrier, inc=1, device_id={"outer": peer}, device_id_type=MESH)
    own_factor(
        me,
        shocks_ref,
        sigma_ref,
        index_ref,
        alloc_ref,
        kind_ref,
        mat_ref,
        ratio_ref,
        fee_ref,
        mort_ref,
        account_ref,
        block_ref,
        table_ref,
        scratch,
    )
    date_tables(rate_ref, dates)
    pl.semaphore_wait(barrier, len(peers))

    started = []

    def post(number, peer, src, dst):
        copy = pltpu.make_async_remote_copy(
            src_ref=src,
            dst_ref=dst,
            send_sem=send.at[number],
            recv_sem=recv.at[number],
            device_id={"outer": peer},
            device_id_type=MESH,
        )
        copy.start()
        started.append(copy)
        return copy

    numbers = iter(range(MESSAGES))

    def piece(origin, first, count):
        return blocks_ref.at[origin, pl.ds(first, count)]

    def send_piece(peer, origin, first, count, mine=False):
        dst = piece(origin, first, count)
        src = block_ref.at[pl.ds(first, count)] if mine else dst
        return post(next(numbers), peer, src, dst)

    local = [
        pltpu.make_async_copy(table_ref, tables_ref.at[me], own.at[0]),
        pltpu.make_async_copy(block_ref, blocks_ref.at[me], own.at[1]),
    ]
    for copy in local:
        copy.start()

    across = [post(next(numbers), at(0, d), table_ref, tables_ref.at[me]) for d in (1, 3, 2)]

    def shift(color, first_step, second_step):
        return at(second_step, first_step) if color == 0 else at(first_step, second_step)

    near = []
    for color in range(2):
        q = 2 * color
        near.append([send_piece(shift(color, d, 0), me, q, 2, True) for d in (1, 3)])
    far = [send_piece(shift(color, 2, 0), me, 2 * color, 2, True) for color in range(2)]
    home = []
    for color in range(2):
        q = 2 * color
        home.append([send_piece(shift(color, 0, d), me, q, 2, True) for d in (1, 3)])

    second = []
    for side in range(2):
        for color in range(2):
            q = 2 * color
            behind = 3 if side == 0 else 1
            near[color][side].wait_recv()
            origin = shift(color, behind, 0)
            for way, d in enumerate((1, 3)):
                copy = send_piece(shift(color, 0, d), origin, q, 2)
                second.append((color, behind, q, 2, way, copy))

    for color in range(2):
        far[color].wait_recv()
        for way, d in enumerate((1, 3)):
            copy = send_piece(shift(color, 0, d), shift(color, 2, 0), 2 * color, 2)
            second.append((color, 2, 2 * color, 2, way, copy))

    last = []

    def hand_on(color, first, q, count, way, copy):
        copy.wait_recv()
        behind, onward = (3, 1) if way == 0 else (1, 3)
        quarter = 2 * color + way
        if not q <= quarter < q + count:
            return
        origin = shift(color, first, behind)
        last.append(send_piece(shift(color, 0, onward), origin, quarter, 1))

    for way in range(2):
        for color in range(2):
            hand_on(color, 0, 2 * color, 2, way, home[color][way])
    for copy in across:
        copy.wait_recv()
    local[0].wait()
    line = tables_ref.at[pl.ds(row * 4, 4)]
    down = [post(next(numbers), at(d, 0), line, line) for d in (1, 3, 2)]
    for copy in down:
        copy.wait_recv()
    params = cohort_order(tables_ref, table, plan_v, rank_ref)
    fund_levels(params, world_ref, level)
    for n, entry in enumerate(second):
        hand_on(*entry)
        if n < 8:
            build_tiles(4 * n, 4, table, level, weight_t, dwt, rows_t, acc_t)
    for copy in last:
        copy.wait_recv()
    local[1].wait()
    for copy in started:
        copy.wait_send()


def gather_outer(shocks, sigma, index, alloc, rows, world, rate):
    vmem = pl.BlockSpec(memory_space=pltpu.VMEM)
    arguments = (shocks, sigma[None], index.T, alloc.T, *rows, world, rate.T)
    out_shape = (
        pltpu.VMEM((NOUT, 4, 16, 512), BF16),
        pltpu.VMEM((TILES, 256, 256), BF16),
        pltpu.VMEM((TILES, 128, 128), F32),
        pltpu.VMEM((TILES, 8, 128), F32),
        pltpu.VMEM((TILES, 128), F32),
        pltpu.VMEM((GROUPS + 2, 6, 8, 128), F32),
        pltpu.VMEM((8, 384), jnp.int32),
        pltpu.VMEM((8, 256), F32),
    )
    return pl.pallas_call(
        gather_kernel,
        out_shape=out_shape,
        in_specs=[vmem] * len(arguments),
        out_specs=(vmem,) * len(out_shape),
        scratch_shapes=[
            pltpu.VMEM((4, 16, 512), BF16),
            pltpu.VMEM((2, 128), F32),
            pltpu.VMEM((16, 128), F32),
            pltpu.VMEM((NOUT, 2, 128), F32),
            pltpu.VMEM((2, 16, 128), F32),
            pltpu.VMEM((2, 128, 128), F32),
            pltpu.SemaphoreType.DMA((MESSAGES,)),
            pltpu.SemaphoreType.DMA((MESSAGES,)),
            pltpu.SemaphoreType.DMA((2,)),
        ],
        compiler_params=pltpu.CompilerParams(
            collective_id=0, has_side_effects=True, vmem_limit_bytes=24 << 20
        ),
        name="gather_outer",
    )(*in_hbm(*arguments))


def value_kernel(
    blocks_ref,
    weight_t,
    dwt,
    rows_t,
    acc_t,
    dates,
    plan_v,
    rank_ref,
    out_ref,
    fmat,
    fmat_t,
    plan,
    sums_t,
    sens,
    sums_in,
    kerns,
    sem,
):
    copy = pltpu.make_async_copy(plan_v, plan, sem)
    copy.start()
    step_in = iota((8, 128), 0) % 4
    for j in range(TILES):
        sens[j] = jnp.zeros((2, 128, 128), F32)
        sums_t[j] = jnp.zeros((4, 8, 128), F32)

    for g in range(GROUPS):
        cols = slice(128 * g, 128 * g + 128)
        part = blocks_ref[:, g // 4, :, 128 * (g % 4) : 128 * (g % 4) + 128]
        part = part.astype(F32).reshape(16, 2, 8, 128)
        for m in range(2):
            one = part[:, m].reshape(128, 128)
            fmat[m, :, cols] = one.astype(BF16)
        fmat_t[cols, :] = part.reshape(256, 128).T.astype(BF16)
    fmat[:, :, 2048:] = jnp.zeros((2, 128, 256), BF16)
    fmat_t[2048:, :] = jnp.zeros((256, 256), BF16)
    copy.wait()

    def raw(i, half):
        here = pl.ds(pl.multiple_of(plan[1, i] * 128, 128), 256)
        sums_in[half] = dot(fmat_t[here, :], weight_t[plan[0, i]])

    def group(j, g, half, slot):
        def wide(k):
            return jnp.broadcast_to(rows_t[j, k : k + 1], (8, 128))

        hz = (step_in + (4 * g + 1)).astype(F32)
        decay = lax.exp2(wide(2) * hz + wide(3))
        decay = jnp.where((hz >= wide(0)) & (hz <= wide(1)), decay, 0.0)
        fee_power = lax.exp2(wide(4) * hz)
        fee_decay = fee_power * decay
        strike = wide(5)
        part = slice(128 * slot, 128 * slot + 128)
        for m in range(2):
            growth = fee_power * dates[g, 3 * m + 2]
            y = sums_in[half, part, 128 * m : 128 * m + 128].reshape(16, 8, 128) * growth
            up = lax.exp2(strike - y)
            more = 1.0 + up
            slope = up / more
            some = jnp.concatenate(
                [up[0:4] + up[4:8] + up[8:12], up[12:14] + up[14:16]], axis=0
            )
            many = jnp.concatenate(
                [more[0:4] * more[4:8] * more[8:12], more[12:14] * more[14:16]], axis=0
            )
            soft_sum = jnp.sum(jnp.where(some < 2.0**-12, some, jnp.log(many)), axis=0)
            kerns[half, m, part, :] = (fee_decay * slope).reshape(128, 128).astype(BF16)
            rho_sum = soft_sum + jnp.sum(slope * y, axis=0) * (1.0 / LOG2E)
            sums_t[j, 2 * m] += (decay * dates[g, 3 * m]) * soft_sum
            sums_t[j, 2 * m + 1] += (decay * dates[g, 3 * m + 1]) * rho_sum

    def flush(i, half):
        j = plan[0, i]
        here = pl.ds(pl.multiple_of(plan[1, i] * 128, 128), 256)
        for m in range(2):
            sens[j, m] += dot(fmat[m, :, here], kerns[half, m])

    def item_work(i, half):
        j, g = plan[0, i], plan[1, i]
        flush(jnp.maximum(i - 1, 0), 1 - half)
        raw(i + 1, 1 - half)
        group(j, g, half, 0)
        group(j, g + 1, half, 1)

    kerns[1] = jnp.zeros((2, 256, 128), BF16)
    raw(0, 0)

    def work(n, carry):
        for k in range(UNROLL):
            item_work(UNROLL * n + k, k % 2)
        return carry

    rounds = (plan[2, 0] + (UNROLL - 1)) // UNROLL
    lax.fori_loop(0, rounds, work, 0)
    flush(UNROLL * rounds - 1, 1)

    def close(q, deltas):
        fresh = list(deltas)
        for k in range(4):
            j = 4 * q + k
            for m in range(2):
                fresh[m] = fresh[m] + dwt[j] * sens[j, m]
        return tuple(fresh)

    none = jnp.zeros((128, 128), F32)
    delta = lax.fori_loop(0, TILES // 4, close, (none, none))
    scale = acc_t[...] * (1.0 / 20.0 / 256.0)
    res_acc = []
    for n in range(4):
        value = jnp.sum(sums_t[:, n], axis=1)
        res_acc.append(value * (scale if n % 2 == 0 else -scale))

    rank_row = rank_ref[0:1, :]
    tile_row = jnp.floor(rank_row * 0.125)
    slot_row = rank_row - 8.0 * tile_row
    pick = (tile_row == iota((TILES, 256), 0).astype(F32)).astype(F32)
    keep = (slot_row == (iota((128, 256), 0) // 16).astype(F32)).astype(F32)
    for m in range(2):
        parts = []
        for n in range(2):
            lanes = dot01(res_acc[2 * m + n], pick, ((0,), (0,)))
            parts.append(jnp.sum((lanes * keep).reshape(8, 16, 256), axis=0))
        down = delta[m].T.reshape(8, 16, 128)
        parts.append(jnp.sum(down, axis=0) * (-1.0 / 256.0))
        line = jnp.concatenate(parts, axis=1)
        for o in range(16):
            for k in range(5):
                r = (o % 2) * 10 + m * 5 + k
                out_ref[o // 2, r : r + 1, :] = line[o : o + 1, 128 * k : 128 * k + 128]
    for b in range(NIN):
        out_ref[b, 20:SLAB, :] = jnp.zeros((SLAB - 20, 128), F32)


def revalue(*tables):
    vmem = pl.BlockSpec(memory_space=pltpu.VMEM)
    return pl.pallas_call(
        value_kernel,
        out_shape=pltpu.VMEM((NIN, SLAB, 128), F32),
        in_specs=[vmem] * len(tables),
        out_specs=vmem,
        scratch_shapes=[
            pltpu.VMEM((2, 128, 2304), BF16),
            pltpu.VMEM((2304, 256), BF16),
            pltpu.SMEM((8, 384), jnp.int32),
            pltpu.VMEM((TILES, 4, 8, 128), F32),
            pltpu.VMEM((TILES, 2, 128, 128), F32),
            pltpu.VMEM((2, 256, 256), F32),
            pltpu.VMEM((2, 2, 256, 128), BF16),
            pltpu.SemaphoreType.DMA(()),
        ],
        compiler_params=pltpu.CompilerParams(vmem_limit_bytes=32 << 20),
        name="revalue",
    )(*in_vmem(*tables))


def scatter_kernel(slabs_ref, inbox, send, recv, own):
    me = lax.axis_index("inner")
    barrier = pltpu.get_barrier_semaphore()
    for d in range(1, NIN):
        pl.semaphore_signal(
            barrier, inc=1, device_id={"inner": lax.rem(me + d, NIN)}, device_id_type=MESH
        )
    local = pltpu.make_async_copy(slabs_ref.at[me], inbox.at[0], own)
    local.start()
    pl.semaphore_wait(barrier, NIN - 1)
    copies = []
    for d in (4, 3, 5, 2, 6, 7, 1):
        peer = lax.rem(me + d, NIN)
        copy = pltpu.make_async_remote_copy(
            src_ref=slabs_ref.at[peer],
            dst_ref=inbox.at[d],
            send_sem=send.at[d],
            recv_sem=recv.at[d],
            device_id={"inner": peer},
            device_id_type=MESH,
        )
        copy.start()
        copies.append(copy)
    local.wait()
    for copy in copies:
        copy.wait()


def total_kernel(inbox_ref, res_ref, rho_ref, del_ref):
    total = inbox_ref[0]
    for d in range(1, NIN):
        total = total + inbox_ref[d]
    for o in range(2):
        for m in range(2):
            r = o * 10 + m * 5
            for k in range(2):
                lanes = slice(128 * k, 128 * k + 128)
                res_ref[o, m : m + 1, lanes] = total[r + k : r + k + 1]
                rho_ref[o, m : m + 1, lanes] = total[r + 2 + k : r + 3 + k]
            del_ref[o, m : m + 1, :] = total[r + 4 : r + 5]


def scatter_inner(slabs):
    vmem = pl.BlockSpec(memory_space=pltpu.VMEM)
    inbox = pl.pallas_call(
        scatter_kernel,
        out_shape=pltpu.VMEM((NIN, SLAB, 128), F32),
        in_specs=[vmem],
        out_specs=vmem,
        scratch_shapes=[
            pltpu.SemaphoreType.DMA((NIN,)),
            pltpu.SemaphoreType.DMA((NIN,)),
            pltpu.SemaphoreType.DMA(()),
        ],
        compiler_params=pltpu.CompilerParams(
            collective_id=1, has_side_effects=True, vmem_limit_bytes=8 << 20
        ),
        name="scatter_inner",
    )(*in_vmem(slabs))
    return pl.pallas_call(
        total_kernel,
        out_shape=(
            jax.ShapeDtypeStruct((2, 2, 256), F32),
            jax.ShapeDtypeStruct((2, 2, 256), F32),
            jax.ShapeDtypeStruct((2, 2, 128), F32),
        ),
        in_specs=[vmem],
        out_specs=(vmem, vmem, vmem),
        compiler_params=pltpu.CompilerParams(vmem_limit_bytes=8 << 20),
        name="total_inner",
    )(*in_vmem(inbox))


def shards(
    world_shocks,
    short_rate,
    inner_shocks,
    fund_volatility,
    fund_index,
    allocation,
    guarantee_type,
    maturity,
    guarantee_ratio,
    fee_rate,
    mortality,
    account,
):
    kinds = (guarantee_type, maturity, guarantee_ratio, fee_rate, mortality, account)
    rows = [value[None] for value in kinds]
    slabs = revalue(
        *gather_outer(
            inner_shocks,
            fund_volatility,
            fund_index,
            allocation,
            rows,
            world_shocks,
            short_rate,
        )
    )
    return scatter_inner(slabs)


def solution(mesh):
    return jax.shard_map(
        shards,
        mesh=mesh,
        in_specs=(
            P("outer", None, None),
            P("outer", None),
            P(None, "outer", "inner"),
            P("outer"),
            P("outer", None),
            P("outer", None),
            P("outer"),
            P("outer"),
            P("outer"),
            P("outer"),
            P("outer"),
            P("outer"),
        ),
        out_specs=(
            P(("outer", "inner"), None, None),
            P(("outer", "inner"), None, None),
            P(("outer", "inner"), None, None),
        ),
        check_vma=False,
    )
```

```python
import functools
import math

import jax
import jax.numpy as jnp
from jax import lax
from jax.experimental import pallas as pl
from jax.experimental.pallas import tpu as pltpu
from jax.sharding import PartitionSpec as P

MESH = pl.DeviceIdType.MESH
HIGHEST = lax.Precision.HIGHEST
F32, BF16 = jnp.float32, jnp.bfloat16

STEPS = 64
DRIFT = 0.06
SMOOTH = 0.05
NOUT = 16
NIN = 8
TILES = 32
GROUPS = 16
TYPE, MAT, RATIO, FEE, MORT, ACC, SIG, KEY = 8, 9, 10, 11, 12, 13, 14, 15
SLAB = 24
MESSAGES = 25
UNROLL = 4
LOG2E = 1.0 / math.log(2.0)
UNIT = LOG2E / SMOOTH


def dot(a, b, dims=((1,), (0,)), precision=None):
    return lax.dot_general(
        a, b, (dims, ((), ())), precision=precision, preferred_element_type=F32
    )


def in_vmem(*arrays):
    return [pltpu.with_memory_space_constraint(array, pltpu.VMEM) for array in arrays]


def in_hbm(*arrays):
    return [pltpu.with_memory_space_constraint(array, pltpu.HBM) for array in arrays]


def dot01(a, b, dims=((1,), (0,)), parts=3):
    b = b.astype(BF16)
    total = None
    for _ in range(parts):
        top = a.astype(BF16)
        a = a - top.astype(F32)
        one = dot(top, b, dims)
        total = one if total is None else total + one
    return total


def iota(shape, dim):
    return lax.broadcasted_iota(jnp.int32, shape, dim)


def own_factor(
    me,
    shocks_ref,
    sigma_ref,
    index_ref,
    alloc_ref,
    kind_ref,
    mat_ref,
    ratio_ref,
    fee_ref,
    mort_ref,
    acc_ref,
    out_ref,
    table_ref,
    scratch,
):
    sigma_row = sigma_ref[...]
    mat = mat_ref[...].astype(F32)
    number = (iota((1, 16), 1) + 16 * me).astype(F32)
    key = jnp.where(kind_ref[...] == 0, 128.0 - mat, 256.0 + mat) * 256.0 + number
    scratch[...] = jnp.zeros((16, 128), F32)
    scratch[0:4, 0:16] = index_ref[...].astype(F32)
    scratch[4:8, 0:16] = alloc_ref[...]
    scratch[TYPE : TYPE + 1, 0:16] = kind_ref[...].astype(F32)
    scratch[MAT : MAT + 1, 0:16] = mat
    scratch[RATIO : RATIO + 1, 0:16] = ratio_ref[...]
    scratch[FEE : FEE + 1, 0:16] = fee_ref[...]
    scratch[MORT : MORT + 1, 0:16] = mort_ref[...]
    scratch[ACC : ACC + 1, 0:16] = acc_ref[...]
    scratch[SIG : SIG + 1, 0:8] = sigma_row
    scratch[KEY : KEY + 1, 0:16] = key
    for r in range(2):
        line = scratch[8 * r : 8 * r + 1, :]
        for k in range(1, 8):
            line = line + pltpu.roll(scratch[8 * r + k : 8 * r + k + 1, :], 16 * k, 1)
        table_ref[r : r + 1, :] = line

    rows = jnp.concatenate(
        [shocks_ref[m, :, 128 * j : 128 * j + 128] for m in range(2) for j in range(16)],
        axis=0,
    )
    src, dst = iota((128, 128), 0), iota((128, 128), 1)
    upper = (src // 64 == dst // 64) & (src <= dst)
    running = dot01(rows, upper.astype(F32))
    same = iota((8, 8), 0) == iota((8, 8), 1)
    sigma = jnp.sum(jnp.where(same, sigma_row, 0.0), axis=1, keepdims=True)
    sigma = jnp.broadcast_to(sigma[None], (32, 8, 1)).reshape(256, 1)
    horizon = (iota((1, 128), 1) % 64 + 1).astype(F32)
    factor = jnp.exp(-0.5 * sigma * sigma * horizon + sigma * running)
    lane = iota((8, 128), 1)
    months = []
    for m in range(2):
        regs = [factor[(m * 16 + j) * 8 : (m * 16 + j) * 8 + 8] for j in range(16)]
        for bit in range(4):
            low = (lane // (4 << bit)) % 2 == 0
            step = 4 << bit
            fresh = list(regs)
            for j in range(16):
                if j >> bit & 1:
                    continue
                k = j | 1 << bit
                a, b = regs[j], regs[k]
                fresh[j] = jnp.where(low, a, pltpu.roll(b, step, 1))
                fresh[k] = jnp.where(low, pltpu.roll(a, 128 - step, 1), b)
            regs = fresh
        months.append(regs)
    for g in range(16):
        both = jnp.concatenate([months[0][g], months[1][g]], axis=0)
        out_ref[g // 4, :, 128 * (g % 4) : 128 * (g % 4) + 128] = both.astype(BF16)


def spread():
    return (iota((16, 128), 1) % 16 == iota((16, 128), 0)).astype(F32)


def date_tables(rate_ref, dates):
    rate_col = rate_ref[...].T
    rates = []
    for m in range(2):
        rate = jnp.sum(rate_col[:, m : m + 1] * spread(), axis=0, keepdims=True)
        rates.append(jnp.broadcast_to(rate, (8, 128)))
    step_in = iota((8, 128), 0) % 4
    for g in range(GROUPS + 2):
        hz = (step_in + (4 * g + 1)).astype(F32)
        for m in range(2):
            power = (LOG2E * rates[m]) * hz
            discount = lax.exp2(-power)
            dates[g, 3 * m] = discount
            dates[g, 3 * m + 1] = hz * discount
            dates[g, 3 * m + 2] = lax.exp2(power) * UNIT


def cohort_order(tables_ref, table, plan_v, rank_ref):
    lanes = iota((8, 128), 1)
    chosen = 16 * iota((8, 128), 0) + lanes % 16
    halves = []
    for h in range(2):
        pieces = []
        for r in range(2):
            piece = jnp.zeros((8, 128), F32)
            for s in range(8):
                line = jnp.broadcast_to(tables_ref[8 * h + s, r : r + 1, :], (8, 128))
                line = jnp.take_along_axis(line, chosen, axis=1)
                piece = jnp.where(lanes // 16 == s, line, piece)
            pieces.append(piece)
        halves.append(jnp.concatenate(pieces, axis=0))
    params_t = jnp.concatenate(halves, axis=1)
    params = params_t.T
    key_col, key_row = params[:, KEY : KEY + 1], params_t[KEY : KEY + 1]
    rank_col = jnp.sum((key_row < key_col).astype(F32), axis=1, keepdims=True)
    rank_row = jnp.sum((key_col < key_row).astype(F32), axis=0, keepdims=True)
    place = (rank_col == iota((256, 256), 1).astype(F32)).astype(F32)
    ordered = dot01(params_t, place)
    rank_ref[...] = jnp.broadcast_to(rank_row, (8, 256))
    table[0] = ordered[:, :128]
    table[1] = ordered[:, 128:]

    mat = ordered[MAT : MAT + 1]
    first = jnp.where(ordered[TYPE : TYPE + 1] == 0.0, 1.0, mat)
    tile_of = iota((TILES, 256), 1) // 8 == iota((TILES, 256), 0)
    low = jnp.min(jnp.where(tile_of, first, 1e3), axis=1, keepdims=True)
    high = jnp.max(jnp.where(tile_of, mat, 0.0), axis=1, keepdims=True)
    low = jnp.floor((low - 1.0) * 0.25)
    count = jnp.floor((jnp.floor((high - 1.0) * 0.25) - low) * 0.5) + 1.0
    before = (iota((TILES, TILES), 1) < iota((TILES, TILES), 0)).astype(F32)
    begin = dot(before, jnp.broadcast_to(count, (TILES, 384)))
    item = iota((TILES, 384), 1).astype(F32)
    mine = (begin <= item) & (item < begin + count)
    tile_id = iota((TILES, 384), 0).astype(F32)
    plan_v[0:1, :] = jnp.sum(jnp.where(mine, tile_id, 0.0), axis=0, keepdims=True).astype(jnp.int32)
    place_g = jnp.where(mine, low + 2.0 * (item - begin) - 16.0, 0.0)
    place_g = 16.0 + jnp.sum(place_g, axis=0, keepdims=True)
    plan_v[1:2, :] = place_g.astype(jnp.int32)
    items = jnp.sum(mine.astype(F32), axis=(0, 1), keepdims=True)
    plan_v[2:8, :] = jnp.broadcast_to(items, (6, 384)).astype(jnp.int32)
    return params


def fund_levels(params, world_ref, level):
    spread_o = spread()
    sigma = params[:, SIG : SIG + 1].reshape(16, 2, 8, 1)[:, 0].reshape(128, 1)
    total = jnp.zeros((128, 128), F32)
    for m in range(2):
        shock = dot01(world_ref[:, m, :], spread_o, ((0,), (0,)))
        total = total + (
            (DRIFT - 0.5 * sigma * sigma) / 12.0 + sigma * shock / math.sqrt(12.0)
        )
        level[m] = jnp.exp(total)


def build_tiles(first_tile, count, table, level, weight_t, dwt, rows_t, acc_t):
    fund = iota((128, 128), 0).astype(F32)

    def build(j, carry):
        where = 8 * lax.rem(j, 16) + iota((16, 128), 1) // 16
        rows = jnp.take_along_axis(table[j // 16], where, axis=1)

        def row(k):
            return rows[k : k + 1]

        share_sum = row(4) + row(5) + row(6) + row(7)
        wts = jnp.zeros((128, 128), F32)
        for k in range(4):
            wts = wts + jnp.where(fund == row(k), row(4 + k) / share_sum, 0.0)
        dwt[j] = wts * row(ACC)
        zero = jnp.zeros((16, 8, 128), F32)
        for m in range(2):
            one = (wts * level[m]).reshape(16, 8, 128)
            both = [one, zero] if m == 0 else [zero, one]
            both = jnp.stack(both, axis=1).reshape(256, 128)
            weight_t[j, :, 128 * m : 128 * m + 128] = both.astype(BF16)
        death = row(TYPE) == 0.0
        mat = row(MAT)
        log_keep = jnp.log(1.0 - row(MORT))
        rows_t[j, 0:1] = jnp.where(death, 1.0, mat)
        rows_t[j, 1:2] = mat
        rows_t[j, 2:3] = jnp.where(death, log_keep, 0.0) * LOG2E
        shift = jnp.where(death, jnp.log(row(MORT)) - log_keep, log_keep * mat)
        rows_t[j, 3:4] = shift * LOG2E
        rows_t[j, 4:5] = row(FEE) * -LOG2E
        rows_t[j, 5:6] = row(RATIO) * UNIT
        acc_t[pl.ds(j, 1), :] = row(ACC)
        return carry

    lax.fori_loop(first_tile, first_tile + count, build, 0, unroll=2)


def gather_kernel(
    shocks_ref,
    sigma_ref,
    index_ref,
    alloc_ref,
    kind_ref,
    mat_ref,
    ratio_ref,
    fee_ref,
    mort_ref,
    account_ref,
    world_ref,
    rate_ref,
    blocks_ref,
    weight_t,
    dwt,
    rows_t,
    acc_t,
    dates,
    plan_v,
    rank_ref,
    block_ref,
    table_ref,
    scratch,
    tables_ref,
    table,
    level,
    send,
    recv,
    own,
):
    me = lax.axis_index("outer")
    row, col = me // 4, me % 4

    def at(dy, dx):
        return ((row + dy) % 4) * 4 + (col + dx) % 4

    peers = [at(0, 1), at(0, 3), at(1, 0), at(3, 0), at(0, 2), at(2, 0)]
    barrier = pltpu.get_barrier_semaphore()
    for peer in peers:
        pl.semaphore_signal(barrier, inc=1, device_id={"outer": peer}, device_id_type=MESH)
    own_factor(
        me,
        shocks_ref,
        sigma_ref,
        index_ref,
        alloc_ref,
        kind_ref,
        mat_ref,
        ratio_ref,
        fee_ref,
        mort_ref,
        account_ref,
        block_ref,
        table_ref,
        scratch,
    )
    date_tables(rate_ref, dates)
    pl.semaphore_wait(barrier, len(peers))

    def post(number, peer, src, dst, sent=0):
        copy = pltpu.make_async_remote_copy(
            src_ref=src,
            dst_ref=dst,
            send_sem=send.at[sent],
            recv_sem=recv.at[number],
            device_id={"outer": peer},
            device_id_type=MESH,
        )
        copy.start()
        return copy

    def whole(ref, count, semaphore):
        view = ref.at[pl.ds(0, count)]
        return pltpu.make_async_copy(view, view, semaphore)

    numbers = iter(range(3, MESSAGES))

    def send_piece(peer, origin, first, count, mine=False, number=None):
        dst = blocks_ref.at[origin, pl.ds(first, count)]
        src = block_ref.at[pl.ds(first, count)] if mine else dst
        return post(next(numbers) if number is None else number, peer, src, dst)

    local = [
        pltpu.make_async_copy(table_ref, tables_ref.at[me], own.at[0]),
        pltpu.make_async_copy(block_ref, blocks_ref.at[me], own.at[1]),
    ]
    for copy in local:
        copy.start()

    for d in (1, 3, 2):
        post(0, at(0, d), table_ref, tables_ref.at[me], 1)

    def shift(color, first_step, second_step):
        return at(second_step, first_step) if color == 0 else at(first_step, second_step)

    near = []
    for color in range(2):
        q = 2 * color
        near.append([send_piece(shift(color, d, 0), me, q, 2, True) for d in (1, 3)])
    far = [send_piece(shift(color, 2, 0), me, 2 * color, 2, True) for color in range(2)]
    home = []
    for color in range(2):
        q = 2 * color
        home.append([send_piece(shift(color, 0, d), me, q, 2, True) for d in (1, 3)])

    whole(tables_ref, 3, recv.at[0]).wait()
    local[0].wait()
    line = tables_ref.at[pl.ds(row * 4, 4)]
    for d in (1, 3, 2):
        post(1, at(d, 0), line, line, 1)

    second = []

    def spread_second(color, offset):
        for way, d in enumerate((1, 3)):
            copy = send_piece(shift(color, 0, d), shift(color, offset, 0), 2 * color, 2)
            second.append((color, offset, way, copy))

    for side in range(2):
        for color in range(2):
            near[color][side].wait_recv()
            spread_second(color, 3 if side == 0 else 1)

    def hand_on(color, offset, way, copy):
        copy.wait_recv()
        behind, onward = (3, 1) if way == 0 else (1, 3)
        origin = shift(color, offset, behind)
        send_piece(shift(color, 0, onward), origin, 2 * color + way, 1, number=2)

    for color in range(2):
        far[color].wait_recv()
        spread_second(color, 2)
    for way in range(2):
        for color in range(2):
            hand_on(color, 0, way, home[color][way])
    whole(tables_ref, 12, recv.at[1]).wait()
    params = cohort_order(tables_ref, table, plan_v, rank_ref)
    fund_levels(params, world_ref, level)
    tiles = 0
    for n, entry in enumerate(second):
        more = (TILES * (n + 1) // 10) // 2 * 2 - tiles if n < 10 else 0
        if more:
            build_tiles(tiles, more, table, level, weight_t, dwt, rows_t, acc_t)
            tiles += more
        hand_on(*entry)
    whole(blocks_ref, 4, recv.at[2]).wait()
    local[1].wait()
    whole(blocks_ref, 15, send.at[0]).wait()
    whole(tables_ref, 15, send.at[1]).wait()


def gather_outer(shocks, sigma, index, alloc, rows, world, rate):
    vmem = pl.BlockSpec(memory_space=pltpu.VMEM)
    arguments = (shocks, sigma[None], index.T, alloc.T, *rows, world, rate.T)
    out_shape = (
        pltpu.VMEM((NOUT, 4, 16, 512), BF16),
        pltpu.VMEM((TILES, 256, 256), BF16),
        pltpu.VMEM((TILES, 128, 128), F32),
        pltpu.VMEM((TILES, 8, 128), F32),
        pltpu.VMEM((TILES, 128), F32),
        pltpu.VMEM((GROUPS + 2, 6, 8, 128), F32),
        pltpu.VMEM((8, 384), jnp.int32),
        pltpu.VMEM((8, 256), F32),
    )
    return pl.pallas_call(
        gather_kernel,
        out_shape=out_shape,
        in_specs=[vmem] * len(arguments),
        out_specs=(vmem,) * len(out_shape),
        scratch_shapes=[
            pltpu.VMEM((4, 16, 512), BF16),
            pltpu.VMEM((2, 128), F32),
            pltpu.VMEM((16, 128), F32),
            pltpu.VMEM((NOUT, 2, 128), F32),
            pltpu.VMEM((2, 16, 128), F32),
            pltpu.VMEM((2, 128, 128), F32),
            pltpu.SemaphoreType.DMA((2,)),
            pltpu.SemaphoreType.DMA((MESSAGES,)),
            pltpu.SemaphoreType.DMA((2,)),
        ],
        compiler_params=pltpu.CompilerParams(
            collective_id=0, has_side_effects=True, vmem_limit_bytes=24 << 20
        ),
        name="gather_outer",
    )(*in_hbm(*arguments))


def value_kernel(
    blocks_ref,
    weight_t,
    dwt,
    rows_t,
    acc_t,
    dates,
    plan_v,
    rank_ref,
    out_ref,
    fmat,
    fmat_t,
    plan,
    sums_t,
    sens,
    sums_in,
    kerns,
    sem,
):
    copy = pltpu.make_async_copy(plan_v, plan, sem)
    copy.start()
    step_in = iota((8, 128), 0) % 4
    for j in range(TILES):
        sens[j] = jnp.zeros((2, 128, 128), F32)
        sums_t[j] = jnp.zeros((4, 8, 128), F32)

    for g in range(GROUPS):
        cols = slice(128 * g, 128 * g + 128)
        part = blocks_ref[:, g // 4, :, 128 * (g % 4) : 128 * (g % 4) + 128]
        part = part.astype(F32).reshape(16, 2, 8, 128)
        for m in range(2):
            one = part[:, m].reshape(128, 128)
            fmat[m, :, cols] = one.astype(BF16)
        fmat_t[cols, :] = part.reshape(256, 128).T.astype(BF16)
    fmat[:, :, 2048:] = jnp.zeros((2, 128, 256), BF16)
    fmat_t[2048:, :] = jnp.zeros((256, 256), BF16)
    copy.wait()

    def raw(i, half):
        here = pl.ds(pl.multiple_of(plan[1, i] * 128, 128), 256)
        sums_in[half] = dot(fmat_t[here, :], weight_t[plan[0, i]])

    def group(j, g, half, slot):
        def wide(k):
            return jnp.broadcast_to(rows_t[j, k : k + 1], (8, 128))

        hz = (step_in + (4 * g + 1)).astype(F32)
        decay = lax.exp2(wide(2) * hz + wide(3))
        decay = jnp.where((hz >= wide(0)) & (hz <= wide(1)), decay, 0.0)
        fee_power = lax.exp2(wide(4) * hz)
        fee_decay = fee_power * decay
        strike = wide(5)
        part = slice(128 * slot, 128 * slot + 128)
        for m in range(2):
            growth = fee_power * dates[g, 3 * m + 2]
            y = sums_in[half, part, 128 * m : 128 * m + 128].reshape(16, 8, 128) * growth
            up = lax.exp2(strike - y)
            more = 1.0 + up
            slope = up / more
            some = jnp.concatenate(
                [up[0:4] + up[4:8] + up[8:12], up[12:14] + up[14:16]], axis=0
            )
            many = jnp.concatenate(
                [more[0:4] * more[4:8] * more[8:12], more[12:14] * more[14:16]], axis=0
            )
            soft_sum = jnp.sum(jnp.where(some < 2.0**-12, some, jnp.log(many)), axis=0)
            kerns[half, m, part, :] = (fee_decay * slope).reshape(128, 128).astype(BF16)
            rho_sum = soft_sum + jnp.sum(slope * y, axis=0) * (1.0 / LOG2E)
            sums_t[j, 2 * m] += (decay * dates[g, 3 * m]) * soft_sum
            sums_t[j, 2 * m + 1] += (decay * dates[g, 3 * m + 1]) * rho_sum

    def flush(i, half):
        j = plan[0, i]
        here = pl.ds(pl.multiple_of(plan[1, i] * 128, 128), 256)
        for m in range(2):
            sens[j, m] += dot(fmat[m, :, here], kerns[half, m])

    def item_work(i, half):
        j, g = plan[0, i], plan[1, i]
        flush(jnp.maximum(i - 1, 0), 1 - half)
        raw(i + 1, 1 - half)
        group(j, g, half, 0)
        group(j, g + 1, half, 1)

    kerns[1] = jnp.zeros((2, 256, 128), BF16)
    raw(0, 0)

    def work(n, carry):
        for k in range(UNROLL):
            item_work(UNROLL * n + k, k % 2)
        return carry

    rounds = (plan[2, 0] + (UNROLL - 1)) // UNROLL
    lax.fori_loop(0, rounds, work, 0)
    flush(UNROLL * rounds - 1, 1)

    def close(q, deltas):
        fresh = list(deltas)
        for k in range(4):
            j = 4 * q + k
            for m in range(2):
                fresh[m] = fresh[m] + dwt[j] * sens[j, m]
        return tuple(fresh)

    none = jnp.zeros((128, 128), F32)
    delta = lax.fori_loop(0, TILES // 4, close, (none, none))
    scale = acc_t[...] * (1.0 / 20.0 / 256.0)
    res_acc = []
    for n in range(4):
        value = jnp.sum(sums_t[:, n], axis=1)
        res_acc.append(value * (scale if n % 2 == 0 else -scale))

    rank_row = rank_ref[0:1, :]
    tile_row = jnp.floor(rank_row * 0.125)
    slot_row = rank_row - 8.0 * tile_row
    pick = (tile_row == iota((TILES, 256), 0).astype(F32)).astype(F32)
    keep = (slot_row == (iota((128, 256), 0) // 16).astype(F32)).astype(F32)
    for m in range(2):
        parts = []
        for n in range(2):
            lanes = dot01(res_acc[2 * m + n], pick, ((0,), (0,)))
            parts.append(jnp.sum((lanes * keep).reshape(8, 16, 256), axis=0))
        down = delta[m].T.reshape(8, 16, 128)
        parts.append(jnp.sum(down, axis=0) * (-1.0 / 256.0))
        line = jnp.concatenate(parts, axis=1)
        for o in range(16):
            for k in range(5):
                r = (o % 2) * 10 + m * 5 + k
                out_ref[o // 2, r : r + 1, :] = line[o : o + 1, 128 * k : 128 * k + 128]
    for b in range(NIN):
        out_ref[b, 20:SLAB, :] = jnp.zeros((SLAB - 20, 128), F32)


def revalue(*tables):
    vmem = pl.BlockSpec(memory_space=pltpu.VMEM)
    return pl.pallas_call(
        value_kernel,
        out_shape=pltpu.VMEM((NIN, SLAB, 128), F32),
        in_specs=[vmem] * len(tables),
        out_specs=vmem,
        scratch_shapes=[
            pltpu.VMEM((2, 128, 2304), BF16),
            pltpu.VMEM((2304, 256), BF16),
            pltpu.SMEM((8, 384), jnp.int32),
            pltpu.VMEM((TILES, 4, 8, 128), F32),
            pltpu.VMEM((TILES, 2, 128, 128), F32),
            pltpu.VMEM((2, 256, 256), F32),
            pltpu.VMEM((2, 2, 256, 128), BF16),
            pltpu.SemaphoreType.DMA(()),
        ],
        compiler_params=pltpu.CompilerParams(vmem_limit_bytes=32 << 20),
        name="revalue",
    )(*in_vmem(*tables))


def scatter_kernel(slabs_ref, inbox, send, recv, own):
    me = lax.axis_index("inner")
    barrier = pltpu.get_barrier_semaphore()
    for d in range(1, NIN):
        pl.semaphore_signal(
            barrier, inc=1, device_id={"inner": lax.rem(me + d, NIN)}, device_id_type=MESH
        )
    local = pltpu.make_async_copy(slabs_ref.at[me], inbox.at[0], own)
    local.start()
    pl.semaphore_wait(barrier, NIN - 1)
    copies = []
    for d in (4, 3, 5, 2, 6, 7, 1):
        peer = lax.rem(me + d, NIN)
        copy = pltpu.make_async_remote_copy(
            src_ref=slabs_ref.at[peer],
            dst_ref=inbox.at[d],
            send_sem=send.at[d],
            recv_sem=recv.at[d],
            device_id={"inner": peer},
            device_id_type=MESH,
        )
        copy.start()
        copies.append(copy)
    local.wait()
    for copy in copies:
        copy.wait()


def total_kernel(inbox_ref, res_ref, rho_ref, del_ref):
    total = inbox_ref[0]
    for d in range(1, NIN):
        total = total + inbox_ref[d]
    for o in range(2):
        for m in range(2):
            r = o * 10 + m * 5
            for k in range(2):
                lanes = slice(128 * k, 128 * k + 128)
                res_ref[o, m : m + 1, lanes] = total[r + k : r + k + 1]
                rho_ref[o, m : m + 1, lanes] = total[r + 2 + k : r + 3 + k]
            del_ref[o, m : m + 1, :] = total[r + 4 : r + 5]


def scatter_inner(slabs):
    vmem = pl.BlockSpec(memory_space=pltpu.VMEM)
    inbox = pl.pallas_call(
        scatter_kernel,
        out_shape=pltpu.VMEM((NIN, SLAB, 128), F32),
        in_specs=[vmem],
        out_specs=vmem,
        scratch_shapes=[
            pltpu.SemaphoreType.DMA((NIN,)),
            pltpu.SemaphoreType.DMA((NIN,)),
            pltpu.SemaphoreType.DMA(()),
        ],
        compiler_params=pltpu.CompilerParams(
            collective_id=1, has_side_effects=True, vmem_limit_bytes=8 << 20
        ),
        name="scatter_inner",
    )(*in_vmem(slabs))
    return pl.pallas_call(
        total_kernel,
        out_shape=(
            jax.ShapeDtypeStruct((2, 2, 256), F32),
            jax.ShapeDtypeStruct((2, 2, 256), F32),
            jax.ShapeDtypeStruct((2, 2, 128), F32),
        ),
        in_specs=[vmem],
        out_specs=(vmem, vmem, vmem),
        compiler_params=pltpu.CompilerParams(vmem_limit_bytes=8 << 20),
        name="total_inner",
    )(*in_vmem(inbox))


def shards(
    world_shocks,
    short_rate,
    inner_shocks,
    fund_volatility,
    fund_index,
    allocation,
    guarantee_type,
    maturity,
    guarantee_ratio,
    fee_rate,
    mortality,
    account,
):
    kinds = (guarantee_type, maturity, guarantee_ratio, fee_rate, mortality, account)
    rows = [value[None] for value in kinds]
    slabs = revalue(
        *gather_outer(
            inner_shocks,
            fund_volatility,
            fund_index,
            allocation,
            rows,
            world_shocks,
            short_rate,
        )
    )
    return scatter_inner(slabs)


def solution(mesh):
    return jax.shard_map(
        shards,
        mesh=mesh,
        in_specs=(
            P("outer", None, None),
            P("outer", None),
            P(None, "outer", "inner"),
            P("outer"),
            P("outer", None),
            P("outer", None),
            P("outer"),
            P("outer"),
            P("outer"),
            P("outer"),
            P("outer"),
            P("outer"),
        ),
        out_specs=(
            P(("outer", "inner"), None, None),
            P(("outer", "inner"), None, None),
            P(("outer", "inner"), None, None),
        ),
        check_vma=False,
    )
```

```python
import functools
import math

import jax
import jax.numpy as jnp
from jax import lax
from jax.experimental import pallas as pl
from jax.experimental.pallas import tpu as pltpu
from jax.sharding import PartitionSpec as P

MESH = pl.DeviceIdType.MESH
HIGHEST = lax.Precision.HIGHEST
F32, BF16 = jnp.float32, jnp.bfloat16

STEPS = 64
DRIFT = 0.06
SMOOTH = 0.05
NOUT = 16
NIN = 8
TILES = 32
GROUPS = 16
TYPE, MAT, RATIO, FEE, MORT, ACC, SIG, KEY = 8, 9, 10, 11, 12, 13, 14, 15
SLAB = 24
MESSAGES = 25
UNROLL = 8
LOG2E = 1.0 / math.log(2.0)
UNIT = LOG2E / SMOOTH


def dot(a, b, dims=((1,), (0,)), precision=None):
    return lax.dot_general(
        a, b, (dims, ((), ())), precision=precision, preferred_element_type=F32
    )


def in_vmem(*arrays):
    return [pltpu.with_memory_space_constraint(array, pltpu.VMEM) for array in arrays]


def in_hbm(*arrays):
    return [pltpu.with_memory_space_constraint(array, pltpu.HBM) for array in arrays]


def dot01(a, b, dims=((1,), (0,)), parts=3):
    b = b.astype(BF16)
    total = None
    for _ in range(parts):
        top = a.astype(BF16)
        a = a - top.astype(F32)
        one = dot(top, b, dims)
        total = one if total is None else total + one
    return total


def iota(shape, dim):
    return lax.broadcasted_iota(jnp.int32, shape, dim)


def own_factor(
    me,
    shocks_ref,
    sigma_ref,
    index_ref,
    alloc_ref,
    kind_ref,
    mat_ref,
    ratio_ref,
    fee_ref,
    mort_ref,
    acc_ref,
    out_ref,
    table_ref,
    scratch,
):
    sigma_row = sigma_ref[...]
    mat = mat_ref[...].astype(F32)
    number = (iota((1, 16), 1) + 16 * me).astype(F32)
    key = jnp.where(kind_ref[...] == 0, 128.0 - mat, 256.0 + mat) * 256.0 + number
    scratch[...] = jnp.zeros((16, 128), F32)
    scratch[0:4, 0:16] = index_ref[...].astype(F32)
    scratch[4:8, 0:16] = alloc_ref[...]
    scratch[TYPE : TYPE + 1, 0:16] = kind_ref[...].astype(F32)
    scratch[MAT : MAT + 1, 0:16] = mat
    scratch[RATIO : RATIO + 1, 0:16] = ratio_ref[...]
    scratch[FEE : FEE + 1, 0:16] = fee_ref[...]
    scratch[MORT : MORT + 1, 0:16] = mort_ref[...]
    scratch[ACC : ACC + 1, 0:16] = acc_ref[...]
    scratch[SIG : SIG + 1, 0:8] = sigma_row
    scratch[KEY : KEY + 1, 0:16] = key
    for r in range(2):
        line = scratch[8 * r : 8 * r + 1, :]
        for k in range(1, 8):
            line = line + pltpu.roll(scratch[8 * r + k : 8 * r + k + 1, :], 16 * k, 1)
        table_ref[r : r + 1, :] = line

    rows = jnp.concatenate(
        [shocks_ref[m, :, 128 * j : 128 * j + 128] for m in range(2) for j in range(16)],
        axis=0,
    )
    src, dst = iota((128, 128), 0), iota((128, 128), 1)
    upper = (src // 64 == dst // 64) & (src <= dst)
    running = dot01(rows, upper.astype(F32))
    same = iota((8, 8), 0) == iota((8, 8), 1)
    sigma = jnp.sum(jnp.where(same, sigma_row, 0.0), axis=1, keepdims=True)
    sigma = jnp.broadcast_to(sigma[None], (32, 8, 1)).reshape(256, 1)
    horizon = (iota((1, 128), 1) % 64 + 1).astype(F32)
    factor = jnp.exp(-0.5 * sigma * sigma * horizon + sigma * running)
    lane = iota((8, 128), 1)
    months = []
    for m in range(2):
        regs = [factor[(m * 16 + j) * 8 : (m * 16 + j) * 8 + 8] for j in range(16)]
        for bit in range(4):
            low = (lane // (4 << bit)) % 2 == 0
            step = 4 << bit
            fresh = list(regs)
            for j in range(16):
                if j >> bit & 1:
                    continue
                k = j | 1 << bit
                a, b = regs[j], regs[k]
                fresh[j] = jnp.where(low, a, pltpu.roll(b, step, 1))
                fresh[k] = jnp.where(low, pltpu.roll(a, 128 - step, 1), b)
            regs = fresh
        months.append(regs)
    for g in range(16):
        both = jnp.concatenate([months[0][g], months[1][g]], axis=0)
        out_ref[g // 4, :, 128 * (g % 4) : 128 * (g % 4) + 128] = both.astype(BF16)


def spread():
    return (iota((16, 128), 1) % 16 == iota((16, 128), 0)).astype(F32)


def date_tables(rate_ref, dates):
    rate_col = rate_ref[...].T
    rates = []
    for m in range(2):
        rate = jnp.sum(rate_col[:, m : m + 1] * spread(), axis=0, keepdims=True)
        rates.append(jnp.broadcast_to(rate, (8, 128)))
    step_in = iota((8, 128), 0) % 4
    for g in range(GROUPS + 2):
        hz = (step_in + (4 * g + 1)).astype(F32)
        for m in range(2):
            power = (LOG2E * rates[m]) * hz
            discount = lax.exp2(-power)
            dates[g, 3 * m] = discount
            dates[g, 3 * m + 1] = hz * discount
            dates[g, 3 * m + 2] = lax.exp2(power) * UNIT


def cohort_order(tables_ref, table, plan_v, rank_ref):
    lanes = iota((8, 128), 1)
    chosen = 16 * iota((8, 128), 0) + lanes % 16
    halves = []
    for h in range(2):
        pieces = []
        for r in range(2):
            piece = jnp.zeros((8, 128), F32)
            for s in range(8):
                line = jnp.broadcast_to(tables_ref[8 * h + s, r : r + 1, :], (8, 128))
                line = jnp.take_along_axis(line, chosen, axis=1)
                piece = jnp.where(lanes // 16 == s, line, piece)
            pieces.append(piece)
        halves.append(jnp.concatenate(pieces, axis=0))
    params_t = jnp.concatenate(halves, axis=1)
    params = params_t.T
    key_col, key_row = params[:, KEY : KEY + 1], params_t[KEY : KEY + 1]
    rank_col = jnp.sum((key_row < key_col).astype(F32), axis=1, keepdims=True)
    rank_row = jnp.sum((key_col < key_row).astype(F32), axis=0, keepdims=True)
    place = (rank_col == iota((256, 256), 1).astype(F32)).astype(F32)
    ordered = dot01(params_t, place)
    rank_ref[...] = jnp.broadcast_to(rank_row, (8, 256))
    table[0] = ordered[:, :128]
    table[1] = ordered[:, 128:]

    mat = ordered[MAT : MAT + 1]
    first = jnp.where(ordered[TYPE : TYPE + 1] == 0.0, 1.0, mat)
    tile_of = iota((TILES, 256), 1) // 8 == iota((TILES, 256), 0)
    low = jnp.min(jnp.where(tile_of, first, 1e3), axis=1, keepdims=True)
    high = jnp.max(jnp.where(tile_of, mat, 0.0), axis=1, keepdims=True)
    low = jnp.floor((low - 1.0) * 0.25)
    count = jnp.floor((jnp.floor((high - 1.0) * 0.25) - low) * 0.5) + 1.0
    before = (iota((TILES, TILES), 1) < iota((TILES, TILES), 0)).astype(F32)
    begin = dot(before, jnp.broadcast_to(count, (TILES, 384)))
    item = iota((TILES, 384), 1).astype(F32)
    mine = (begin <= item) & (item < begin + count)
    tile_id = iota((TILES, 384), 0).astype(F32)
    plan_v[0:1, :] = jnp.sum(jnp.where(mine, tile_id, 0.0), axis=0, keepdims=True).astype(jnp.int32)
    place_g = jnp.where(mine, low + 2.0 * (item - begin) - 16.0, 0.0)
    place_g = 16.0 + jnp.sum(place_g, axis=0, keepdims=True)
    plan_v[1:2, :] = place_g.astype(jnp.int32)
    items = jnp.sum(mine.astype(F32), axis=(0, 1), keepdims=True)
    plan_v[2:8, :] = jnp.broadcast_to(items, (6, 384)).astype(jnp.int32)
    return params


def fund_levels(params, world_ref, level):
    spread_o = spread()
    sigma = params[:, SIG : SIG + 1].reshape(16, 2, 8, 1)[:, 0].reshape(128, 1)
    total = jnp.zeros((128, 128), F32)
    for m in range(2):
        shock = dot01(world_ref[:, m, :], spread_o, ((0,), (0,)))
        total = total + (
            (DRIFT - 0.5 * sigma * sigma) / 12.0 + sigma * shock / math.sqrt(12.0)
        )
        level[m] = jnp.exp(total)


def build_tiles(first_tile, count, table, level, weight_t, dwt, rows_t, acc_t):
    fund = iota((128, 128), 0).astype(F32)

    def build(j, carry):
        where = 8 * lax.rem(j, 16) + iota((16, 128), 1) // 16
        rows = jnp.take_along_axis(table[j // 16], where, axis=1)

        def row(k):
            return rows[k : k + 1]

        share_sum = row(4) + row(5) + row(6) + row(7)
        wts = jnp.zeros((128, 128), F32)
        for k in range(4):
            wts = wts + jnp.where(fund == row(k), row(4 + k) / share_sum, 0.0)
        dwt[j] = wts * row(ACC)
        zero = jnp.zeros((16, 8, 128), F32)
        for m in range(2):
            one = (wts * level[m]).reshape(16, 8, 128)
            both = [one, zero] if m == 0 else [zero, one]
            both = jnp.stack(both, axis=1).reshape(256, 128)
            weight_t[j, :, 128 * m : 128 * m + 128] = both.astype(BF16)
        death = row(TYPE) == 0.0
        mat = row(MAT)
        log_keep = jnp.log(1.0 - row(MORT))
        rows_t[j, 0:1] = jnp.where(death, 1.0, mat)
        rows_t[j, 1:2] = mat
        rows_t[j, 2:3] = jnp.where(death, log_keep, 0.0) * LOG2E
        shift = jnp.where(death, jnp.log(row(MORT)) - log_keep, log_keep * mat)
        rows_t[j, 3:4] = shift * LOG2E
        rows_t[j, 4:5] = row(FEE) * -LOG2E
        rows_t[j, 5:6] = row(RATIO) * UNIT
        acc_t[pl.ds(j, 1), :] = row(ACC)
        return carry

    lax.fori_loop(first_tile, first_tile + count, build, 0, unroll=2)


def gather_kernel(
    shocks_ref,
    sigma_ref,
    index_ref,
    alloc_ref,
    kind_ref,
    mat_ref,
    ratio_ref,
    fee_ref,
    mort_ref,
    account_ref,
    world_ref,
    rate_ref,
    blocks_ref,
    weight_t,
    dwt,
    rows_t,
    acc_t,
    dates,
    plan_v,
    rank_ref,
    block_ref,
    table_ref,
    scratch,
    tables_ref,
    table,
    level,
    send,
    recv,
    own,
):
    me = lax.axis_index("outer")
    row, col = me // 4, me % 4

    def at(dy, dx):
        return ((row + dy) % 4) * 4 + (col + dx) % 4

    peers = [at(0, 1), at(0, 3), at(1, 0), at(3, 0), at(0, 2), at(2, 0)]
    barrier = pltpu.get_barrier_semaphore()
    for peer in peers:
        pl.semaphore_signal(barrier, inc=1, device_id={"outer": peer}, device_id_type=MESH)
    own_factor(
        me,
        shocks_ref,
        sigma_ref,
        index_ref,
        alloc_ref,
        kind_ref,
        mat_ref,
        ratio_ref,
        fee_ref,
        mort_ref,
        account_ref,
        block_ref,
        table_ref,
        scratch,
    )
    pl.semaphore_wait(barrier, len(peers))

    def post(number, peer, src, dst, sent=0):
        copy = pltpu.make_async_remote_copy(
            src_ref=src,
            dst_ref=dst,
            send_sem=send.at[sent],
            recv_sem=recv.at[number],
            device_id={"outer": peer},
            device_id_type=MESH,
        )
        copy.start()
        return copy

    def whole(ref, count, semaphore):
        view = ref.at[pl.ds(0, count)]
        return pltpu.make_async_copy(view, view, semaphore)

    numbers = iter(range(3, MESSAGES))

    def send_piece(peer, origin, first, count, mine=False, number=None):
        dst = blocks_ref.at[origin, pl.ds(first, count)]
        src = block_ref.at[pl.ds(first, count)] if mine else dst
        return post(next(numbers) if number is None else number, peer, src, dst)

    local = [
        pltpu.make_async_copy(table_ref, tables_ref.at[me], own.at[0]),
        pltpu.make_async_copy(block_ref, blocks_ref.at[me], own.at[1]),
    ]
    for copy in local:
        copy.start()

    for d in (1, 3, 2):
        post(0, at(0, d), table_ref, tables_ref.at[me], 1)

    def shift(color, first_step, second_step):
        return at(second_step, first_step) if color == 0 else at(first_step, second_step)

    near = []
    for color in range(2):
        q = 2 * color
        near.append([send_piece(shift(color, d, 0), me, q, 2, True) for d in (1, 3)])
    far = [send_piece(shift(color, 2, 0), me, 2 * color, 2, True) for color in range(2)]
    home = []
    for color in range(2):
        q = 2 * color
        home.append([send_piece(shift(color, 0, d), me, q, 2, True) for d in (1, 3)])

    date_tables(rate_ref, dates)
    whole(tables_ref, 3, recv.at[0]).wait()
    local[0].wait()
    line = tables_ref.at[pl.ds(row * 4, 4)]
    for d in (1, 3, 2):
        post(1, at(d, 0), line, line, 1)

    second = []

    def spread_second(color, offset):
        for way, d in enumerate((1, 3)):
            copy = send_piece(shift(color, 0, d), shift(color, offset, 0), 2 * color, 2)
            second.append((color, offset, way, copy))

    for side in range(2):
        for color in range(2):
            near[color][side].wait_recv()
            spread_second(color, 3 if side == 0 else 1)

    def hand_on(color, offset, way, copy):
        copy.wait_recv()
        behind, onward = (3, 1) if way == 0 else (1, 3)
        origin = shift(color, offset, behind)
        send_piece(shift(color, 0, onward), origin, 2 * color + way, 1, number=2)

    for color in range(2):
        far[color].wait_recv()
        spread_second(color, 2)
    for way in range(2):
        for color in range(2):
            hand_on(color, 0, way, home[color][way])
    whole(tables_ref, 12, recv.at[1]).wait()
    params = cohort_order(tables_ref, table, plan_v, rank_ref)
    fund_levels(params, world_ref, level)
    tiles = 0
    for n, entry in enumerate(second):
        more = (TILES * (n + 1) // 10) // 2 * 2 - tiles if n < 10 else 0
        if more:
            build_tiles(tiles, more, table, level, weight_t, dwt, rows_t, acc_t)
            tiles += more
        hand_on(*entry)
    whole(blocks_ref, 4, recv.at[2]).wait()
    local[1].wait()
    whole(blocks_ref, 15, send.at[0]).wait()
    whole(tables_ref, 15, send.at[1]).wait()


def gather_outer(shocks, sigma, index, alloc, rows, world, rate):
    vmem = pl.BlockSpec(memory_space=pltpu.VMEM)
    arguments = (shocks, sigma[None], index.T, alloc.T, *rows, world, rate.T)
    out_shape = (
        pltpu.VMEM((NOUT, 4, 16, 512), BF16),
        pltpu.VMEM((TILES, 256, 256), BF16),
        pltpu.VMEM((TILES, 128, 128), F32),
        pltpu.VMEM((TILES, 8, 128), F32),
        pltpu.VMEM((TILES, 128), F32),
        pltpu.VMEM((GROUPS + 2, 6, 8, 128), F32),
        pltpu.VMEM((8, 384), jnp.int32),
        pltpu.VMEM((8, 256), F32),
    )
    return pl.pallas_call(
        gather_kernel,
        out_shape=out_shape,
        in_specs=[vmem] * len(arguments),
        out_specs=(vmem,) * len(out_shape),
        scratch_shapes=[
            pltpu.VMEM((4, 16, 512), BF16),
            pltpu.VMEM((2, 128), F32),
            pltpu.VMEM((16, 128), F32),
            pltpu.VMEM((NOUT, 2, 128), F32),
            pltpu.VMEM((2, 16, 128), F32),
            pltpu.VMEM((2, 128, 128), F32),
            pltpu.SemaphoreType.DMA((2,)),
            pltpu.SemaphoreType.DMA((MESSAGES,)),
            pltpu.SemaphoreType.DMA((2,)),
        ],
        compiler_params=pltpu.CompilerParams(
            collective_id=0, has_side_effects=True, vmem_limit_bytes=24 << 20
        ),
        name="gather_outer",
    )(*in_hbm(*arguments))


def value_kernel(
    blocks_ref,
    weight_t,
    dwt,
    rows_t,
    acc_t,
    dates,
    plan_v,
    rank_ref,
    out_ref,
    fmat,
    fmat_t,
    plan,
    sums_t,
    sens,
    sums_in,
    kerns,
    sem,
):
    copy = pltpu.make_async_copy(plan_v, plan, sem)
    copy.start()
    step_in = iota((8, 128), 0) % 4
    for j in range(TILES):
        sens[j] = jnp.zeros((2, 128, 128), F32)
        sums_t[j] = jnp.zeros((4, 8, 128), F32)

    for g in range(GROUPS):
        cols = slice(128 * g, 128 * g + 128)
        part = blocks_ref[:, g // 4, :, 128 * (g % 4) : 128 * (g % 4) + 128]
        part = part.astype(F32).reshape(16, 2, 8, 128)
        for m in range(2):
            one = part[:, m].reshape(128, 128)
            fmat[m, :, cols] = one.astype(BF16)
        fmat_t[cols, :] = part.reshape(256, 128).T.astype(BF16)
    fmat[:, :, 2048:] = jnp.zeros((2, 128, 256), BF16)
    fmat_t[2048:, :] = jnp.zeros((256, 256), BF16)
    copy.wait()

    def raw(i, half):
        here = pl.ds(pl.multiple_of(plan[1, i] * 128, 128), 256)
        sums_in[half] = dot(fmat_t[here, :], weight_t[plan[0, i]])

    def group(j, g, half, slot):
        def wide(k):
            return jnp.broadcast_to(rows_t[j, k : k + 1], (8, 128))

        hz = (step_in + (4 * g + 1)).astype(F32)
        decay = lax.exp2(wide(2) * hz + wide(3))
        decay = jnp.where((hz >= wide(0)) & (hz <= wide(1)), decay, 0.0)
        fee_power = lax.exp2(wide(4) * hz)
        fee_decay = fee_power * decay
        strike = wide(5)
        part = slice(128 * slot, 128 * slot + 128)
        for m in range(2):
            growth = fee_power * dates[g, 3 * m + 2]
            y = sums_in[half, part, 128 * m : 128 * m + 128].reshape(16, 8, 128) * growth
            up = lax.exp2(strike - y)
            more = 1.0 + up
            slope = up / more
            some = jnp.concatenate(
                [up[0:4] + up[4:8] + up[8:12], up[12:14] + up[14:16]], axis=0
            )
            many = jnp.concatenate(
                [more[0:4] * more[4:8] * more[8:12], more[12:14] * more[14:16]], axis=0
            )
            soft_sum = jnp.sum(jnp.where(some < 2.0**-12, some, jnp.log(many)), axis=0)
            kerns[half, m, part, :] = (fee_decay * slope).reshape(128, 128).astype(BF16)
            rho_sum = soft_sum + jnp.sum(slope * y, axis=0) * (1.0 / LOG2E)
            sums_t[j, 2 * m] += (decay * dates[g, 3 * m]) * soft_sum
            sums_t[j, 2 * m + 1] += (decay * dates[g, 3 * m + 1]) * rho_sum

    def flush(i, half):
        j = plan[0, i]
        here = pl.ds(pl.multiple_of(plan[1, i] * 128, 128), 256)
        for m in range(2):
            sens[j, m] += dot(fmat[m, :, here], kerns[half, m])

    def item_work(i, half):
        j, g = plan[0, i], plan[1, i]
        flush(jnp.maximum(i - 1, 0), 1 - half)
        raw(i + 1, 1 - half)
        group(j, g, half, 0)
        group(j, g + 1, half, 1)

    kerns[1] = jnp.zeros((2, 256, 128), BF16)
    raw(0, 0)

    def rounds(first, count, size):
        def work(n, carry):
            for k in range(size):
                item_work(first + size * n + k, k % 2)
            return carry

        lax.fori_loop(0, count, work, 0)

    items = plan[2, 0]
    full = items // UNROLL
    pairs = (items - UNROLL * full + 1) // 2
    rounds(0, full, UNROLL)
    rounds(UNROLL * full, pairs, 2)
    flush(UNROLL * full + 2 * pairs - 1, 1)

    def close(q, deltas):
        fresh = list(deltas)
        for k in range(4):
            j = 4 * q + k
            for m in range(2):
                fresh[m] = fresh[m] + dwt[j] * sens[j, m]
        return tuple(fresh)

    none = jnp.zeros((128, 128), F32)
    delta = lax.fori_loop(0, TILES // 4, close, (none, none))
    scale = acc_t[...] * (1.0 / 20.0 / 256.0)
    res_acc = []
    for n in range(4):
        value = jnp.sum(sums_t[:, n], axis=1)
        res_acc.append(value * (scale if n % 2 == 0 else -scale))

    rank_row = rank_ref[0:1, :]
    tile_row = jnp.floor(rank_row * 0.125)
    slot_row = rank_row - 8.0 * tile_row
    pick = (tile_row == iota((TILES, 256), 0).astype(F32)).astype(F32)
    keep = (slot_row == (iota((128, 256), 0) // 16).astype(F32)).astype(F32)
    for m in range(2):
        parts = []
        for n in range(2):
            lanes = dot01(res_acc[2 * m + n], pick, ((0,), (0,)))
            parts.append(jnp.sum((lanes * keep).reshape(8, 16, 256), axis=0))
        down = delta[m].T.reshape(8, 16, 128)
        parts.append(jnp.sum(down, axis=0) * (-1.0 / 256.0))
        line = jnp.concatenate(parts, axis=1)
        for o in range(16):
            for k in range(5):
                r = (o % 2) * 10 + m * 5 + k
                out_ref[o // 2, r : r + 1, :] = line[o : o + 1, 128 * k : 128 * k + 128]
    for b in range(NIN):
        out_ref[b, 20:SLAB, :] = jnp.zeros((SLAB - 20, 128), F32)


def revalue(*tables):
    vmem = pl.BlockSpec(memory_space=pltpu.VMEM)
    return pl.pallas_call(
        value_kernel,
        out_shape=pltpu.VMEM((NIN, SLAB, 128), F32),
        in_specs=[vmem] * len(tables),
        out_specs=vmem,
        scratch_shapes=[
            pltpu.VMEM((2, 128, 2304), BF16),
            pltpu.VMEM((2304, 256), BF16),
            pltpu.SMEM((8, 384), jnp.int32),
            pltpu.VMEM((TILES, 4, 8, 128), F32),
            pltpu.VMEM((TILES, 2, 128, 128), F32),
            pltpu.VMEM((2, 256, 256), F32),
            pltpu.VMEM((2, 2, 256, 128), BF16),
            pltpu.SemaphoreType.DMA(()),
        ],
        compiler_params=pltpu.CompilerParams(vmem_limit_bytes=32 << 20),
        name="revalue",
    )(*in_vmem(*tables))


def scatter_kernel(slabs_ref, inbox, send, recv, own):
    me = lax.axis_index("inner")
    barrier = pltpu.get_barrier_semaphore()
    for d in range(1, NIN):
        pl.semaphore_signal(
            barrier, inc=1, device_id={"inner": lax.rem(me + d, NIN)}, device_id_type=MESH
        )
    local = pltpu.make_async_copy(slabs_ref.at[me], inbox.at[0], own)
    local.start()
    pl.semaphore_wait(barrier, NIN - 1)
    for d in (4, 3, 5, 2, 6, 7, 1):
        peer = lax.rem(me + d, NIN)
        pltpu.make_async_remote_copy(
            src_ref=slabs_ref.at[peer],
            dst_ref=inbox.at[d],
            send_sem=send,
            recv_sem=recv,
            device_id={"inner": peer},
            device_id_type=MESH,
        ).start()
    local.wait()
    view = inbox.at[pl.ds(0, NIN - 1)]
    pltpu.make_async_copy(view, view, recv).wait()
    pltpu.make_async_copy(view, view, send).wait()


def total_kernel(inbox_ref, res_ref, rho_ref, del_ref):
    total = inbox_ref[0]
    for d in range(1, NIN):
        total = total + inbox_ref[d]
    for o in range(2):
        for m in range(2):
            r = o * 10 + m * 5
            for k in range(2):
                lanes = slice(128 * k, 128 * k + 128)
                res_ref[o, m : m + 1, lanes] = total[r + k : r + k + 1]
                rho_ref[o, m : m + 1, lanes] = total[r + 2 + k : r + 3 + k]
            del_ref[o, m : m + 1, :] = total[r + 4 : r + 5]


def scatter_inner(slabs):
    vmem = pl.BlockSpec(memory_space=pltpu.VMEM)
    inbox = pl.pallas_call(
        scatter_kernel,
        out_shape=pltpu.VMEM((NIN, SLAB, 128), F32),
        in_specs=[vmem],
        out_specs=vmem,
        scratch_shapes=[
            pltpu.SemaphoreType.DMA(()),
            pltpu.SemaphoreType.DMA(()),
            pltpu.SemaphoreType.DMA(()),
        ],
        compiler_params=pltpu.CompilerParams(
            collective_id=1, has_side_effects=True, vmem_limit_bytes=8 << 20
        ),
        name="scatter_inner",
    )(*in_vmem(slabs))
    return pl.pallas_call(
        total_kernel,
        out_shape=(
            jax.ShapeDtypeStruct((2, 2, 256), F32),
            jax.ShapeDtypeStruct((2, 2, 256), F32),
            jax.ShapeDtypeStruct((2, 2, 128), F32),
        ),
        in_specs=[vmem],
        out_specs=(vmem, vmem, vmem),
        compiler_params=pltpu.CompilerParams(vmem_limit_bytes=8 << 20),
        name="total_inner",
    )(*in_vmem(inbox))


def shards(
    world_shocks,
    short_rate,
    inner_shocks,
    fund_volatility,
    fund_index,
    allocation,
    guarantee_type,
    maturity,
    guarantee_ratio,
    fee_rate,
    mortality,
    account,
):
    kinds = (guarantee_type, maturity, guarantee_ratio, fee_rate, mortality, account)
    rows = [value[None] for value in kinds]
    slabs = revalue(
        *gather_outer(
            inner_shocks,
            fund_volatility,
            fund_index,
            allocation,
            rows,
            world_shocks,
            short_rate,
        )
    )
    return scatter_inner(slabs)


def solution(mesh):
    return jax.shard_map(
        shards,
        mesh=mesh,
        in_specs=(
            P("outer", None, None),
            P("outer", None),
            P(None, "outer", "inner"),
            P("outer"),
            P("outer", None),
            P("outer", None),
            P("outer"),
            P("outer"),
            P("outer"),
            P("outer"),
            P("outer"),
            P("outer"),
        ),
        out_specs=(
            P(("outer", "inner"), None, None),
            P(("outer", "inner"), None, None),
            P(("outer", "inner"), None, None),
        ),
        check_vma=False,
    )
```

```python
import functools
import math

import jax
import jax.numpy as jnp
from jax import lax
from jax.experimental import pallas as pl
from jax.experimental.pallas import tpu as pltpu
from jax.sharding import PartitionSpec as P

MESH = pl.DeviceIdType.MESH
HIGHEST = lax.Precision.HIGHEST
F32, BF16 = jnp.float32, jnp.bfloat16

STEPS = 64
DRIFT = 0.06
SMOOTH = 0.05
NOUT = 16
NIN = 8
TILES = 32
GROUPS = 16
TYPE, MAT, RATIO, FEE, MORT, ACC, SIG, KEY = 8, 9, 10, 11, 12, 13, 14, 15
SLAB = 24
MESSAGES = 25
UNROLL = 12
LOG2E = 1.0 / math.log(2.0)
UNIT = LOG2E / SMOOTH


def dot(a, b, dims=((1,), (0,)), precision=None):
    return lax.dot_general(
        a, b, (dims, ((), ())), precision=precision, preferred_element_type=F32
    )


def in_vmem(*arrays):
    return [pltpu.with_memory_space_constraint(array, pltpu.VMEM) for array in arrays]


def in_hbm(*arrays):
    return [pltpu.with_memory_space_constraint(array, pltpu.HBM) for array in arrays]


def dot01(a, b, dims=((1,), (0,)), parts=3):
    b = b.astype(BF16)
    total = None
    for _ in range(parts):
        top = a.astype(BF16)
        a = a - top.astype(F32)
        one = dot(top, b, dims)
        total = one if total is None else total + one
    return total


def iota(shape, dim):
    return lax.broadcasted_iota(jnp.int32, shape, dim)


def own_factor(
    me,
    shocks_ref,
    sigma_ref,
    index_ref,
    alloc_ref,
    kind_ref,
    mat_ref,
    ratio_ref,
    fee_ref,
    mort_ref,
    acc_ref,
    out_ref,
    table_ref,
    scratch,
):
    sigma_row = sigma_ref[...]
    mat = mat_ref[...].astype(F32)
    number = (iota((1, 16), 1) + 16 * me).astype(F32)
    key = jnp.where(kind_ref[...] == 0, 128.0 - mat, 256.0 + mat) * 256.0 + number
    scratch[...] = jnp.zeros((16, 128), F32)
    scratch[0:4, 0:16] = index_ref[...].astype(F32)
    scratch[4:8, 0:16] = alloc_ref[...]
    scratch[TYPE : TYPE + 1, 0:16] = kind_ref[...].astype(F32)
    scratch[MAT : MAT + 1, 0:16] = mat
    scratch[RATIO : RATIO + 1, 0:16] = ratio_ref[...]
    scratch[FEE : FEE + 1, 0:16] = fee_ref[...]
    scratch[MORT : MORT + 1, 0:16] = mort_ref[...]
    scratch[ACC : ACC + 1, 0:16] = acc_ref[...]
    scratch[SIG : SIG + 1, 0:8] = sigma_row
    scratch[KEY : KEY + 1, 0:16] = key
    for r in range(2):
        line = scratch[8 * r : 8 * r + 1, :]
        for k in range(1, 8):
            line = line + pltpu.roll(scratch[8 * r + k : 8 * r + k + 1, :], 16 * k, 1)
        table_ref[r : r + 1, :] = line

    rows = jnp.concatenate(
        [shocks_ref[m, :, 128 * j : 128 * j + 128] for m in range(2) for j in range(16)],
        axis=0,
    )
    src, dst = iota((128, 128), 0), iota((128, 128), 1)
    upper = (src // 64 == dst // 64) & (src <= dst)
    running = dot01(rows, upper.astype(F32))
    same = iota((8, 8), 0) == iota((8, 8), 1)
    sigma = jnp.sum(jnp.where(same, sigma_row, 0.0), axis=1, keepdims=True)
    sigma = jnp.broadcast_to(sigma[None], (32, 8, 1)).reshape(256, 1)
    horizon = (iota((1, 128), 1) % 64 + 1).astype(F32)
    factor = jnp.exp(-0.5 * sigma * sigma * horizon + sigma * running)
    lane = iota((8, 128), 1)
    months = []
    for m in range(2):
        regs = [factor[(m * 16 + j) * 8 : (m * 16 + j) * 8 + 8] for j in range(16)]
        for bit in range(4):
            low = (lane // (4 << bit)) % 2 == 0
            step = 4 << bit
            fresh = list(regs)
            for j in range(16):
                if j >> bit & 1:
                    continue
                k = j | 1 << bit
                a, b = regs[j], regs[k]
                fresh[j] = jnp.where(low, a, pltpu.roll(b, step, 1))
                fresh[k] = jnp.where(low, pltpu.roll(a, 128 - step, 1), b)
            regs = fresh
        months.append(regs)
    for g in range(16):
        both = jnp.concatenate([months[0][g], months[1][g]], axis=0)
        out_ref[g // 4, :, 128 * (g % 4) : 128 * (g % 4) + 128] = both.astype(BF16)


def spread():
    return (iota((16, 128), 1) % 16 == iota((16, 128), 0)).astype(F32)


def date_tables(rate_ref, dates):
    rate_col = rate_ref[...].T
    rates = []
    for m in range(2):
        rate = jnp.sum(rate_col[:, m : m + 1] * spread(), axis=0, keepdims=True)
        rates.append(jnp.broadcast_to(rate, (8, 128)))
    step_in = iota((8, 128), 0) % 4
    for g in range(GROUPS + 2):
        hz = (step_in + (4 * g + 1)).astype(F32)
        for m in range(2):
            power = (LOG2E * rates[m]) * hz
            discount = lax.exp2(-power)
            dates[g, 3 * m] = discount
            dates[g, 3 * m + 1] = hz * discount
            dates[g, 3 * m + 2] = lax.exp2(power) * UNIT


def cohort_order(tables_ref, table, plan_v, rank_ref):
    lanes = iota((8, 128), 1)
    chosen = 16 * iota((8, 128), 0) + lanes % 16
    halves = []
    for h in range(2):
        pieces = []
        for r in range(2):
            piece = jnp.zeros((8, 128), F32)
            for s in range(8):
                line = jnp.broadcast_to(tables_ref[8 * h + s, r : r + 1, :], (8, 128))
                line = jnp.take_along_axis(line, chosen, axis=1)
                piece = jnp.where(lanes // 16 == s, line, piece)
            pieces.append(piece)
        halves.append(jnp.concatenate(pieces, axis=0))
    params_t = jnp.concatenate(halves, axis=1)
    params = params_t.T
    key_col, key_row = params[:, KEY : KEY + 1], params_t[KEY : KEY + 1]
    rank_col = jnp.sum((key_row < key_col).astype(F32), axis=1, keepdims=True)
    rank_row = jnp.sum((key_col < key_row).astype(F32), axis=0, keepdims=True)
    place = (rank_col == iota((256, 256), 1).astype(F32)).astype(F32)
    ordered = dot01(params_t, place)
    rank_ref[...] = jnp.broadcast_to(rank_row, (8, 256))
    table[0] = ordered[:, :128]
    table[1] = ordered[:, 128:]

    mat = ordered[MAT : MAT + 1]
    first = jnp.where(ordered[TYPE : TYPE + 1] == 0.0, 1.0, mat)
    tile_of = iota((TILES, 256), 1) // 8 == iota((TILES, 256), 0)
    low = jnp.min(jnp.where(tile_of, first, 1e3), axis=1, keepdims=True)
    high = jnp.max(jnp.where(tile_of, mat, 0.0), axis=1, keepdims=True)
    low = jnp.floor((low - 1.0) * 0.25)
    count = jnp.floor((jnp.floor((high - 1.0) * 0.25) - low) * 0.5) + 1.0
    before = (iota((TILES, TILES), 1) < iota((TILES, TILES), 0)).astype(F32)
    begin = dot(before, jnp.broadcast_to(count, (TILES, 384)))
    item = iota((TILES, 384), 1).astype(F32)
    mine = (begin <= item) & (item < begin + count)
    tile_id = iota((TILES, 384), 0).astype(F32)
    plan_v[0:1, :] = jnp.sum(jnp.where(mine, tile_id, 0.0), axis=0, keepdims=True).astype(jnp.int32)
    place_g = jnp.where(mine, low + 2.0 * (item - begin) - 16.0, 0.0)
    place_g = 16.0 + jnp.sum(place_g, axis=0, keepdims=True)
    plan_v[1:2, :] = place_g.astype(jnp.int32)
    items = jnp.sum(mine.astype(F32), axis=(0, 1), keepdims=True)
    plan_v[2:8, :] = jnp.broadcast_to(items, (6, 384)).astype(jnp.int32)
    return params


def fund_levels(params, world_ref, level):
    spread_o = spread()
    sigma = params[:, SIG : SIG + 1].reshape(16, 2, 8, 1)[:, 0].reshape(128, 1)
    total = jnp.zeros((128, 128), F32)
    for m in range(2):
        shock = dot01(world_ref[:, m, :], spread_o, ((0,), (0,)))
        total = total + (
            (DRIFT - 0.5 * sigma * sigma) / 12.0 + sigma * shock / math.sqrt(12.0)
        )
        level[m] = jnp.exp(total)


def build_tiles(first_tile, count, table, level, weight_t, dwt, rows_t, acc_t):
    fund = iota((128, 128), 0).astype(F32)

    def build(j, carry):
        where = 8 * lax.rem(j, 16) + iota((16, 128), 1) // 16
        rows = jnp.take_along_axis(table[j // 16], where, axis=1)

        def row(k):
            return rows[k : k + 1]

        share_sum = row(4) + row(5) + row(6) + row(7)
        wts = jnp.zeros((128, 128), F32)
        for k in range(4):
            wts = wts + jnp.where(fund == row(k), row(4 + k) / share_sum, 0.0)
        dwt[j] = wts * row(ACC)
        zero = jnp.zeros((16, 8, 128), F32)
        for m in range(2):
            one = (wts * level[m]).reshape(16, 8, 128)
            both = [one, zero] if m == 0 else [zero, one]
            both = jnp.stack(both, axis=1).reshape(256, 128)
            weight_t[j, :, 128 * m : 128 * m + 128] = both.astype(BF16)
        death = row(TYPE) == 0.0
        mat = row(MAT)
        log_keep = jnp.log(1.0 - row(MORT))
        rows_t[j, 0:1] = jnp.where(death, 1.0, mat)
        rows_t[j, 1:2] = mat
        rows_t[j, 2:3] = jnp.where(death, log_keep, 0.0) * LOG2E
        shift = jnp.where(death, jnp.log(row(MORT)) - log_keep, log_keep * mat)
        rows_t[j, 3:4] = shift * LOG2E
        rows_t[j, 4:5] = row(FEE) * -LOG2E
        rows_t[j, 5:6] = row(RATIO) * UNIT
        acc_t[pl.ds(j, 1), :] = row(ACC)
        return carry

    lax.fori_loop(first_tile, first_tile + count, build, 0, unroll=2)


def gather_kernel(
    shocks_ref,
    sigma_ref,
    index_ref,
    alloc_ref,
    kind_ref,
    mat_ref,
    ratio_ref,
    fee_ref,
    mort_ref,
    account_ref,
    world_ref,
    rate_ref,
    blocks_ref,
    weight_t,
    dwt,
    rows_t,
    acc_t,
    dates,
    plan_v,
    rank_ref,
    block_ref,
    table_ref,
    scratch,
    tables_ref,
    table,
    level,
    send,
    recv,
    own,
):
    me = lax.axis_index("outer")
    row, col = me // 4, me % 4

    def at(dy, dx):
        return ((row + dy) % 4) * 4 + (col + dx) % 4

    peers = [at(0, 1), at(0, 3), at(1, 0), at(3, 0), at(0, 2), at(2, 0)]
    barrier = pltpu.get_barrier_semaphore()
    for peer in peers:
        pl.semaphore_signal(barrier, inc=1, device_id={"outer": peer}, device_id_type=MESH)
    own_factor(
        me,
        shocks_ref,
        sigma_ref,
        index_ref,
        alloc_ref,
        kind_ref,
        mat_ref,
        ratio_ref,
        fee_ref,
        mort_ref,
        account_ref,
        block_ref,
        table_ref,
        scratch,
    )
    pl.semaphore_wait(barrier, len(peers))

    def post(number, peer, src, dst, sent=0):
        copy = pltpu.make_async_remote_copy(
            src_ref=src,
            dst_ref=dst,
            send_sem=send.at[sent],
            recv_sem=recv.at[number],
            device_id={"outer": peer},
            device_id_type=MESH,
        )
        copy.start()
        return copy

    def whole(ref, count, semaphore):
        view = ref.at[pl.ds(0, count)]
        return pltpu.make_async_copy(view, view, semaphore)

    numbers = iter(range(3, MESSAGES))

    def send_piece(peer, origin, first, count, mine=False, number=None):
        dst = blocks_ref.at[origin, pl.ds(first, count)]
        src = block_ref.at[pl.ds(first, count)] if mine else dst
        return post(next(numbers) if number is None else number, peer, src, dst)

    local = [
        pltpu.make_async_copy(table_ref, tables_ref.at[me], own.at[0]),
        pltpu.make_async_copy(block_ref, blocks_ref.at[me], own.at[1]),
    ]
    for copy in local:
        copy.start()

    for d in (1, 3, 2):
        post(0, at(0, d), table_ref, tables_ref.at[me], 1)

    def shift(color, first_step, second_step):
        return at(second_step, first_step) if color == 0 else at(first_step, second_step)

    near = []
    for color in range(2):
        q = 2 * color
        near.append([send_piece(shift(color, d, 0), me, q, 2, True) for d in (1, 3)])
    far = [send_piece(shift(color, 2, 0), me, 2 * color, 2, True) for color in range(2)]
    home = []
    for color in range(2):
        q = 2 * color
        home.append([send_piece(shift(color, 0, d), me, q, 2, True) for d in (1, 3)])

    date_tables(rate_ref, dates)
    whole(tables_ref, 3, recv.at[0]).wait()
    local[0].wait()
    line = tables_ref.at[pl.ds(row * 4, 4)]
    for d in (1, 3, 2):
        post(1, at(d, 0), line, line, 1)

    second = []

    def spread_second(color, offset):
        for way, d in enumerate((1, 3)):
            copy = send_piece(shift(color, 0, d), shift(color, offset, 0), 2 * color, 2)
            second.append((color, offset, way, copy))

    for side in range(2):
        for color in range(2):
            near[color][side].wait_recv()
            spread_second(color, 3 if side == 0 else 1)

    def hand_on(color, offset, way, copy):
        copy.wait_recv()
        behind, onward = (3, 1) if way == 0 else (1, 3)
        origin = shift(color, offset, behind)
        send_piece(shift(color, 0, onward), origin, 2 * color + way, 1, number=2)

    for color in range(2):
        far[color].wait_recv()
        spread_second(color, 2)
    for way in range(2):
        for color in range(2):
            hand_on(color, 0, way, home[color][way])
    whole(tables_ref, 12, recv.at[1]).wait()
    params = cohort_order(tables_ref, table, plan_v, rank_ref)
    fund_levels(params, world_ref, level)
    tiles = 0
    for n, entry in enumerate(second):
        more = (TILES * (n + 1) // 10) // 2 * 2 - tiles if n < 10 else 0
        if more:
            build_tiles(tiles, more, table, level, weight_t, dwt, rows_t, acc_t)
            tiles += more
        hand_on(*entry)
    whole(blocks_ref, 4, recv.at[2]).wait()
    local[1].wait()
    whole(blocks_ref, 15, send.at[0]).wait()
    whole(tables_ref, 15, send.at[1]).wait()


def gather_outer(shocks, sigma, index, alloc, rows, world, rate):
    vmem = pl.BlockSpec(memory_space=pltpu.VMEM)
    arguments = (shocks, sigma[None], index.T, alloc.T, *rows, world, rate.T)
    out_shape = (
        pltpu.VMEM((NOUT, 4, 16, 512), BF16),
        pltpu.VMEM((TILES, 256, 256), BF16),
        pltpu.VMEM((TILES, 128, 128), F32),
        pltpu.VMEM((TILES, 8, 128), F32),
        pltpu.VMEM((TILES, 128), F32),
        pltpu.VMEM((GROUPS + 2, 6, 8, 128), F32),
        pltpu.VMEM((8, 384), jnp.int32),
        pltpu.VMEM((8, 256), F32),
    )
    return pl.pallas_call(
        gather_kernel,
        out_shape=out_shape,
        in_specs=[vmem] * len(arguments),
        out_specs=(vmem,) * len(out_shape),
        scratch_shapes=[
            pltpu.VMEM((4, 16, 512), BF16),
            pltpu.VMEM((2, 128), F32),
            pltpu.VMEM((16, 128), F32),
            pltpu.VMEM((NOUT, 2, 128), F32),
            pltpu.VMEM((2, 16, 128), F32),
            pltpu.VMEM((2, 128, 128), F32),
            pltpu.SemaphoreType.DMA((2,)),
            pltpu.SemaphoreType.DMA((MESSAGES,)),
            pltpu.SemaphoreType.DMA((2,)),
        ],
        compiler_params=pltpu.CompilerParams(
            collective_id=0, has_side_effects=True, vmem_limit_bytes=24 << 20
        ),
        name="gather_outer",
    )(*in_hbm(*arguments))


def value_kernel(
    blocks_ref,
    weight_t,
    dwt,
    rows_t,
    acc_t,
    dates,
    plan_v,
    rank_ref,
    out_ref,
    fmat,
    fmat_t,
    plan,
    sums_t,
    sens,
    sums_in,
    kerns,
    sem,
):
    copy = pltpu.make_async_copy(plan_v, plan, sem)
    copy.start()
    step_in = iota((8, 128), 0) % 4
    for j in range(TILES):
        sens[j] = jnp.zeros((2, 128, 128), F32)
        sums_t[j] = jnp.zeros((4, 8, 128), F32)

    for g in range(GROUPS):
        cols = slice(128 * g, 128 * g + 128)
        part = blocks_ref[:, g // 4, :, 128 * (g % 4) : 128 * (g % 4) + 128]
        part = part.astype(F32).reshape(16, 2, 8, 128)
        for m in range(2):
            one = part[:, m].reshape(128, 128)
            fmat[m, :, cols] = one.astype(BF16)
        fmat_t[cols, :] = part.reshape(256, 128).T.astype(BF16)
    fmat[:, :, 2048:] = jnp.zeros((2, 128, 256), BF16)
    fmat_t[2048:, :] = jnp.zeros((256, 256), BF16)
    copy.wait()

    def raw(i, half):
        here = pl.ds(pl.multiple_of(plan[1, i] * 128, 128), 256)
        sums_in[half] = dot(fmat_t[here, :], weight_t[plan[0, i]])

    def group(j, g, half, slot):
        def wide(k):
            return jnp.broadcast_to(rows_t[j, k : k + 1], (8, 128))

        hz = (step_in + (4 * g + 1)).astype(F32)
        decay = lax.exp2(wide(2) * hz + wide(3))
        decay = jnp.where((hz >= wide(0)) & (hz <= wide(1)), decay, 0.0)
        fee_power = lax.exp2(wide(4) * hz)
        fee_decay = fee_power * decay
        strike = wide(5)
        part = slice(128 * slot, 128 * slot + 128)
        for m in range(2):
            growth = fee_power * dates[g, 3 * m + 2]
            y = sums_in[half, part, 128 * m : 128 * m + 128].reshape(16, 8, 128) * growth
            up = lax.exp2(strike - y)
            more = 1.0 + up
            slope = up / more
            some = jnp.concatenate(
                [up[0:4] + up[4:8] + up[8:12], up[12:14] + up[14:16]], axis=0
            )
            many = jnp.concatenate(
                [more[0:4] * more[4:8] * more[8:12], more[12:14] * more[14:16]], axis=0
            )
            soft_sum = jnp.sum(jnp.where(some < 2.0**-12, some, jnp.log(many)), axis=0)
            kerns[half, m, part, :] = (fee_decay * slope).reshape(128, 128).astype(BF16)
            rho_sum = soft_sum + jnp.sum(slope * y, axis=0) * (1.0 / LOG2E)
            sums_t[j, 2 * m] += (decay * dates[g, 3 * m]) * soft_sum
            sums_t[j, 2 * m + 1] += (decay * dates[g, 3 * m + 1]) * rho_sum

    def flush(i, half):
        j = plan[0, i]
        here = pl.ds(pl.multiple_of(plan[1, i] * 128, 128), 256)
        for m in range(2):
            sens[j, m] += dot(fmat[m, :, here], kerns[half, m])

    def item_work(i, half):
        j, g = plan[0, i], plan[1, i]
        flush(jnp.maximum(i - 1, 0), 1 - half)
        raw(i + 1, 1 - half)
        group(j, g, half, 0)
        group(j, g + 1, half, 1)

    kerns[1] = jnp.zeros((2, 256, 128), BF16)
    raw(0, 0)

    def rounds(first, count, size):
        def work(n, carry):
            for k in range(size):
                item_work(first + size * n + k, k % 2)
            return carry

        lax.fori_loop(0, count, work, 0)

    items = plan[2, 0]
    full = items // UNROLL
    pairs = (items - UNROLL * full + 1) // 2
    rounds(0, full, UNROLL)
    rounds(UNROLL * full, pairs, 2)
    flush(UNROLL * full + 2 * pairs - 1, 1)

    def close(q, deltas):
        fresh = list(deltas)
        for k in range(4):
            j = 4 * q + k
            for m in range(2):
                fresh[m] = fresh[m] + dwt[j] * sens[j, m]
        return tuple(fresh)

    none = jnp.zeros((128, 128), F32)
    delta = lax.fori_loop(0, TILES // 4, close, (none, none))
    scale = acc_t[...] * (1.0 / 20.0 / 256.0)
    res_acc = []
    for n in range(4):
        value = jnp.sum(sums_t[:, n], axis=1)
        res_acc.append(value * (scale if n % 2 == 0 else -scale))

    rank_row = rank_ref[0:1, :]
    tile_row = jnp.floor(rank_row * 0.125)
    slot_row = rank_row - 8.0 * tile_row
    pick = (tile_row == iota((TILES, 256), 0).astype(F32)).astype(F32)
    keep = (slot_row == (iota((128, 256), 0) // 16).astype(F32)).astype(F32)
    for m in range(2):
        parts = []
        for n in range(2):
            lanes = dot01(res_acc[2 * m + n], pick, ((0,), (0,)))
            parts.append(jnp.sum((lanes * keep).reshape(8, 16, 256), axis=0))
        down = delta[m].T.reshape(8, 16, 128)
        parts.append(jnp.sum(down, axis=0) * (-1.0 / 256.0))
        line = jnp.concatenate(parts, axis=1)
        for o in range(16):
            for k in range(5):
                r = (o % 2) * 10 + m * 5 + k
                out_ref[o // 2, r : r + 1, :] = line[o : o + 1, 128 * k : 128 * k + 128]
    for b in range(NIN):
        out_ref[b, 20:SLAB, :] = jnp.zeros((SLAB - 20, 128), F32)


def revalue(*tables):
    vmem = pl.BlockSpec(memory_space=pltpu.VMEM)
    return pl.pallas_call(
        value_kernel,
        out_shape=pltpu.VMEM((NIN, SLAB, 128), F32),
        in_specs=[vmem] * len(tables),
        out_specs=vmem,
        scratch_shapes=[
            pltpu.VMEM((2, 128, 2304), BF16),
            pltpu.VMEM((2304, 256), BF16),
            pltpu.SMEM((8, 384), jnp.int32),
            pltpu.VMEM((TILES, 4, 8, 128), F32),
            pltpu.VMEM((TILES, 2, 128, 128), F32),
            pltpu.VMEM((2, 256, 256), F32),
            pltpu.VMEM((2, 2, 256, 128), BF16),
            pltpu.SemaphoreType.DMA(()),
        ],
        compiler_params=pltpu.CompilerParams(vmem_limit_bytes=32 << 20),
        name="revalue",
    )(*in_vmem(*tables))


def scatter_kernel(slabs_ref, inbox, send, recv, own):
    me = lax.axis_index("inner")
    barrier = pltpu.get_barrier_semaphore()
    for d in range(1, NIN):
        pl.semaphore_signal(
            barrier, inc=1, device_id={"inner": lax.rem(me + d, NIN)}, device_id_type=MESH
        )
    local = pltpu.make_async_copy(slabs_ref.at[me], inbox.at[0], own)
    local.start()
    pl.semaphore_wait(barrier, NIN - 1)
    for d in (4, 3, 5, 2, 6, 7, 1):
        peer = lax.rem(me + d, NIN)
        pltpu.make_async_remote_copy(
            src_ref=slabs_ref.at[peer],
            dst_ref=inbox.at[d],
            send_sem=send,
            recv_sem=recv,
            device_id={"inner": peer},
            device_id_type=MESH,
        ).start()
    local.wait()
    view = inbox.at[pl.ds(0, NIN - 1)]
    pltpu.make_async_copy(view, view, recv).wait()
    pltpu.make_async_copy(view, view, send).wait()


def total_kernel(inbox_ref, res_ref, rho_ref, del_ref):
    total = inbox_ref[0]
    for d in range(1, NIN):
        total = total + inbox_ref[d]
    for o in range(2):
        for m in range(2):
            r = o * 10 + m * 5
            for k in range(2):
                lanes = slice(128 * k, 128 * k + 128)
                res_ref[o, m : m + 1, lanes] = total[r + k : r + k + 1]
                rho_ref[o, m : m + 1, lanes] = total[r + 2 + k : r + 3 + k]
            del_ref[o, m : m + 1, :] = total[r + 4 : r + 5]


def scatter_inner(slabs):
    vmem = pl.BlockSpec(memory_space=pltpu.VMEM)
    inbox = pl.pallas_call(
        scatter_kernel,
        out_shape=pltpu.VMEM((NIN, SLAB, 128), F32),
        in_specs=[vmem],
        out_specs=vmem,
        scratch_shapes=[
            pltpu.SemaphoreType.DMA(()),
            pltpu.SemaphoreType.DMA(()),
            pltpu.SemaphoreType.DMA(()),
        ],
        compiler_params=pltpu.CompilerParams(
            collective_id=1, has_side_effects=True, vmem_limit_bytes=8 << 20
        ),
        name="scatter_inner",
    )(*in_vmem(slabs))
    return pl.pallas_call(
        total_kernel,
        out_shape=(
            jax.ShapeDtypeStruct((2, 2, 256), F32),
            jax.ShapeDtypeStruct((2, 2, 256), F32),
            jax.ShapeDtypeStruct((2, 2, 128), F32),
        ),
        in_specs=[vmem],
        out_specs=(vmem, vmem, vmem),
        compiler_params=pltpu.CompilerParams(vmem_limit_bytes=8 << 20),
        name="total_inner",
    )(*in_vmem(inbox))


def shards(
    world_shocks,
    short_rate,
    inner_shocks,
    fund_volatility,
    fund_index,
    allocation,
    guarantee_type,
    maturity,
    guarantee_ratio,
    fee_rate,
    mortality,
    account,
):
    kinds = (guarantee_type, maturity, guarantee_ratio, fee_rate, mortality, account)
    rows = [value[None] for value in kinds]
    slabs = revalue(
        *gather_outer(
            inner_shocks,
            fund_volatility,
            fund_index,
            allocation,
            rows,
            world_shocks,
            short_rate,
        )
    )
    return scatter_inner(slabs)


def solution(mesh):
    return jax.shard_map(
        shards,
        mesh=mesh,
        in_specs=(
            P("outer", None, None),
            P("outer", None),
            P(None, "outer", "inner"),
            P("outer"),
            P("outer", None),
            P("outer", None),
            P("outer"),
            P("outer"),
            P("outer"),
            P("outer"),
            P("outer"),
            P("outer"),
        ),
        out_specs=(
            P(("outer", "inner"), None, None),
            P(("outer", "inner"), None, None),
            P(("outer", "inner"), None, None),
        ),
        check_vma=False,
    )
```

```python
import functools
import math

import jax
import jax.numpy as jnp
from jax import lax
from jax.experimental import pallas as pl
from jax.experimental.pallas import tpu as pltpu
from jax.sharding import PartitionSpec as P

MESH = pl.DeviceIdType.MESH
HIGHEST = lax.Precision.HIGHEST
F32, BF16 = jnp.float32, jnp.bfloat16

STEPS = 64
DRIFT = 0.06
SMOOTH = 0.05
NOUT = 16
NIN = 8
TILES = 32
GROUPS = 16
TYPE, MAT, RATIO, FEE, MORT, ACC, SIG, KEY = 8, 9, 10, 11, 12, 13, 14, 15
SLAB = 24
MESSAGES = 25
UNROLL = 12
LOG2E = 1.0 / math.log(2.0)
UNIT = LOG2E / SMOOTH


def dot(a, b, dims=((1,), (0,)), precision=None):
    return lax.dot_general(
        a, b, (dims, ((), ())), precision=precision, preferred_element_type=F32
    )


def in_vmem(*arrays):
    return [pltpu.with_memory_space_constraint(array, pltpu.VMEM) for array in arrays]


def in_hbm(*arrays):
    return [pltpu.with_memory_space_constraint(array, pltpu.HBM) for array in arrays]


def dot01(a, b, dims=((1,), (0,)), parts=3):
    b = b.astype(BF16)
    total = None
    for _ in range(parts):
        top = a.astype(BF16)
        a = a - top.astype(F32)
        one = dot(top, b, dims)
        total = one if total is None else total + one
    return total


def iota(shape, dim):
    return lax.broadcasted_iota(jnp.int32, shape, dim)


def own_factor(
    me,
    shocks_ref,
    sigma_ref,
    index_ref,
    alloc_ref,
    kind_ref,
    mat_ref,
    ratio_ref,
    fee_ref,
    mort_ref,
    acc_ref,
    out_ref,
    table_ref,
    scratch,
):
    sigma_row = sigma_ref[...]
    mat = mat_ref[...].astype(F32)
    number = (iota((1, 16), 1) + 16 * me).astype(F32)
    key = jnp.where(kind_ref[...] == 0, 128.0 - mat, 256.0 + mat) * 256.0 + number
    scratch[...] = jnp.zeros((16, 128), F32)
    scratch[0:4, 0:16] = index_ref[...].astype(F32)
    scratch[4:8, 0:16] = alloc_ref[...]
    scratch[TYPE : TYPE + 1, 0:16] = kind_ref[...].astype(F32)
    scratch[MAT : MAT + 1, 0:16] = mat
    scratch[RATIO : RATIO + 1, 0:16] = ratio_ref[...]
    scratch[FEE : FEE + 1, 0:16] = fee_ref[...]
    scratch[MORT : MORT + 1, 0:16] = mort_ref[...]
    scratch[ACC : ACC + 1, 0:16] = acc_ref[...]
    scratch[SIG : SIG + 1, 0:8] = sigma_row
    scratch[KEY : KEY + 1, 0:16] = key
    for r in range(2):
        line = scratch[8 * r : 8 * r + 1, :]
        for k in range(1, 8):
            line = line + pltpu.roll(scratch[8 * r + k : 8 * r + k + 1, :], 16 * k, 1)
        table_ref[r : r + 1, :] = line

    rows = jnp.concatenate(
        [shocks_ref[m, :, 128 * j : 128 * j + 128] for m in range(2) for j in range(16)],
        axis=0,
    )
    src, dst = iota((128, 128), 0), iota((128, 128), 1)
    upper = (src // 64 == dst // 64) & (src <= dst)
    running = dot01(rows, upper.astype(F32))
    same = iota((8, 8), 0) == iota((8, 8), 1)
    sigma = jnp.sum(jnp.where(same, sigma_row, 0.0), axis=1, keepdims=True)
    sigma = jnp.broadcast_to(sigma[None], (32, 8, 1)).reshape(256, 1)
    horizon = (iota((1, 128), 1) % 64 + 1).astype(F32)
    factor = jnp.exp(-0.5 * sigma * sigma * horizon + sigma * running)
    lane = iota((8, 128), 1)
    months = []
    for m in range(2):
        regs = [factor[(m * 16 + j) * 8 : (m * 16 + j) * 8 + 8] for j in range(16)]
        for bit in range(4):
            low = (lane // (4 << bit)) % 2 == 0
            step = 4 << bit
            fresh = list(regs)
            for j in range(16):
                if j >> bit & 1:
                    continue
                k = j | 1 << bit
                a, b = regs[j], regs[k]
                fresh[j] = jnp.where(low, a, pltpu.roll(b, step, 1))
                fresh[k] = jnp.where(low, pltpu.roll(a, 128 - step, 1), b)
            regs = fresh
        months.append(regs)
    for g in range(16):
        both = jnp.concatenate([months[0][g], months[1][g]], axis=0)
        out_ref[g // 4, :, 128 * (g % 4) : 128 * (g % 4) + 128] = both.astype(BF16)


def spread():
    return (iota((16, 128), 1) % 16 == iota((16, 128), 0)).astype(F32)


def date_tables(rate_ref, dates):
    rate_col = rate_ref[...].T
    rates = []
    for m in range(2):
        rate = jnp.sum(rate_col[:, m : m + 1] * spread(), axis=0, keepdims=True)
        rates.append(jnp.broadcast_to(rate, (8, 128)))
    step_in = iota((8, 128), 0) % 4
    for g in range(GROUPS + 2):
        hz = (step_in + (4 * g + 1)).astype(F32)
        for m in range(2):
            power = (LOG2E * rates[m]) * hz
            discount = lax.exp2(-power)
            dates[g, 3 * m] = discount
            dates[g, 3 * m + 1] = hz * discount
            dates[g, 3 * m + 2] = lax.exp2(power) * UNIT


def cohort_order(tables_ref, table, plan_v, rank_ref):
    lanes = iota((8, 128), 1)
    chosen = 16 * iota((8, 128), 0) + lanes % 16
    halves = []
    for h in range(2):
        pieces = []
        for r in range(2):
            piece = jnp.zeros((8, 128), F32)
            for s in range(8):
                line = jnp.broadcast_to(tables_ref[8 * h + s, r : r + 1, :], (8, 128))
                line = jnp.take_along_axis(line, chosen, axis=1)
                piece = jnp.where(lanes // 16 == s, line, piece)
            pieces.append(piece)
        halves.append(jnp.concatenate(pieces, axis=0))
    params_t = jnp.concatenate(halves, axis=1)
    params = params_t.T
    key_col, key_row = params[:, KEY : KEY + 1], params_t[KEY : KEY + 1]
    rank_col = jnp.sum((key_row < key_col).astype(F32), axis=1, keepdims=True)
    rank_row = jnp.sum((key_col < key_row).astype(F32), axis=0, keepdims=True)
    place = (rank_col == iota((256, 256), 1).astype(F32)).astype(F32)
    ordered = dot01(params_t, place)
    rank_ref[...] = jnp.broadcast_to(rank_row, (8, 256))
    table[0] = ordered[:, :128]
    table[1] = ordered[:, 128:]

    mat = ordered[MAT : MAT + 1]
    first = jnp.where(ordered[TYPE : TYPE + 1] == 0.0, 1.0, mat)
    tile_of = iota((TILES, 256), 1) // 8 == iota((TILES, 256), 0)
    low = jnp.min(jnp.where(tile_of, first, 1e3), axis=1, keepdims=True)
    high = jnp.max(jnp.where(tile_of, mat, 0.0), axis=1, keepdims=True)
    low = jnp.floor((low - 1.0) * 0.25)
    count = jnp.floor((jnp.floor((high - 1.0) * 0.25) - low) * 0.5) + 1.0
    before = (iota((TILES, TILES), 1) < iota((TILES, TILES), 0)).astype(F32)
    begin = dot(before, jnp.broadcast_to(count, (TILES, 384)))
    item = iota((TILES, 384), 1).astype(F32)
    mine = (begin <= item) & (item < begin + count)
    tile_id = iota((TILES, 384), 0).astype(F32)
    plan_v[0:1, :] = jnp.sum(jnp.where(mine, tile_id, 0.0), axis=0, keepdims=True).astype(jnp.int32)
    place_g = jnp.where(mine, low + 2.0 * (item - begin) - 16.0, 0.0)
    place_g = 16.0 + jnp.sum(place_g, axis=0, keepdims=True)
    plan_v[1:2, :] = place_g.astype(jnp.int32)
    items = jnp.sum(mine.astype(F32), axis=(0, 1), keepdims=True)
    plan_v[2:8, :] = jnp.broadcast_to(items, (6, 384)).astype(jnp.int32)
    return params


def fund_levels(params, world_ref, level):
    spread_o = spread()
    sigma = params[:, SIG : SIG + 1].reshape(16, 2, 8, 1)[:, 0].reshape(128, 1)
    total = jnp.zeros((128, 128), F32)
    for m in range(2):
        shock = dot01(world_ref[:, m, :], spread_o, ((0,), (0,)))
        total = total + (
            (DRIFT - 0.5 * sigma * sigma) / 12.0 + sigma * shock / math.sqrt(12.0)
        )
        level[m] = jnp.exp(total)


def build_tiles(first_tile, count, table, level, weight_t, dwt, rows_t, acc_t):
    fund = iota((128, 128), 0).astype(F32)

    def build(j, carry):
        where = 8 * lax.rem(j, 16) + iota((16, 128), 1) // 16
        rows = jnp.take_along_axis(table[j // 16], where, axis=1)

        def row(k):
            return rows[k : k + 1]

        share_sum = row(4) + row(5) + row(6) + row(7)
        wts = jnp.zeros((128, 128), F32)
        for k in range(4):
            wts = wts + jnp.where(fund == row(k), row(4 + k) / share_sum, 0.0)
        dwt[j] = wts * row(ACC)
        zero = jnp.zeros((16, 8, 128), F32)
        for m in range(2):
            one = (wts * level[m]).reshape(16, 8, 128)
            both = [one, zero] if m == 0 else [zero, one]
            both = jnp.stack(both, axis=1).reshape(256, 128)
            weight_t[j, :, 128 * m : 128 * m + 128] = both.astype(BF16)
        death = row(TYPE) == 0.0
        mat = row(MAT)
        log_keep = jnp.log(1.0 - row(MORT))
        rows_t[j, 0:1] = jnp.where(death, 1.0, mat)
        rows_t[j, 1:2] = mat
        rows_t[j, 2:3] = jnp.where(death, log_keep, 0.0) * LOG2E
        shift = jnp.where(death, jnp.log(row(MORT)) - log_keep, log_keep * mat)
        rows_t[j, 3:4] = shift * LOG2E
        rows_t[j, 4:5] = row(FEE) * -LOG2E
        rows_t[j, 5:6] = row(RATIO) * UNIT
        acc_t[pl.ds(j, 1), :] = row(ACC)
        return carry

    lax.fori_loop(first_tile, first_tile + count, build, 0, unroll=2)


def gather_kernel(
    shocks_ref,
    sigma_ref,
    index_ref,
    alloc_ref,
    kind_ref,
    mat_ref,
    ratio_ref,
    fee_ref,
    mort_ref,
    account_ref,
    world_ref,
    rate_ref,
    blocks_ref,
    weight_t,
    dwt,
    rows_t,
    acc_t,
    dates,
    plan_v,
    rank_ref,
    block_ref,
    table_ref,
    scratch,
    tables_ref,
    table,
    level,
    send,
    recv,
    own,
):
    me = lax.axis_index("outer")
    row, col = me // 4, me % 4

    def at(dy, dx):
        return ((row + dy) % 4) * 4 + (col + dx) % 4

    peers = [at(0, 1), at(0, 3), at(1, 0), at(3, 0), at(0, 2), at(2, 0)]
    barrier = pltpu.get_barrier_semaphore()
    for peer in peers:
        pl.semaphore_signal(barrier, inc=1, device_id={"outer": peer}, device_id_type=MESH)
    own_factor(
        me,
        shocks_ref,
        sigma_ref,
        index_ref,
        alloc_ref,
        kind_ref,
        mat_ref,
        ratio_ref,
        fee_ref,
        mort_ref,
        account_ref,
        block_ref,
        table_ref,
        scratch,
    )
    pl.semaphore_wait(barrier, len(peers))

    def post(number, peer, src, dst, sent=0):
        copy = pltpu.make_async_remote_copy(
            src_ref=src,
            dst_ref=dst,
            send_sem=send.at[sent],
            recv_sem=recv.at[number],
            device_id={"outer": peer},
            device_id_type=MESH,
        )
        copy.start()
        return copy

    def whole(ref, count, semaphore):
        view = ref.at[pl.ds(0, count)]
        return pltpu.make_async_copy(view, view, semaphore)

    numbers = iter(range(3, MESSAGES))

    def send_piece(peer, origin, first, count, mine=False, number=None):
        dst = blocks_ref.at[origin, pl.ds(first, count)]
        src = block_ref.at[pl.ds(first, count)] if mine else dst
        return post(next(numbers) if number is None else number, peer, src, dst)

    local = [
        pltpu.make_async_copy(table_ref, tables_ref.at[me], own.at[0]),
        pltpu.make_async_copy(block_ref, blocks_ref.at[me], own.at[1]),
    ]
    for copy in local:
        copy.start()

    for d in (1, 3, 2):
        post(0, at(0, d), table_ref, tables_ref.at[me], 1)

    def shift(color, first_step, second_step):
        return at(second_step, first_step) if color == 0 else at(first_step, second_step)

    near = []
    for color in range(2):
        q = 2 * color
        near.append([send_piece(shift(color, d, 0), me, q, 2, True) for d in (1, 3)])
    far = [send_piece(shift(color, 2, 0), me, 2 * color, 2, True) for color in range(2)]
    home = []
    for color in range(2):
        q = 2 * color
        home.append([send_piece(shift(color, 0, d), me, q, 2, True) for d in (1, 3)])

    date_tables(rate_ref, dates)
    whole(tables_ref, 3, recv.at[0]).wait()
    local[0].wait()
    line = tables_ref.at[pl.ds(row * 4, 4)]
    for d in (1, 3, 2):
        post(1, at(d, 0), line, line, 1)

    second = []

    def spread_second(color, offset):
        for way, d in enumerate((1, 3)):
            copy = send_piece(shift(color, 0, d), shift(color, offset, 0), 2 * color, 2)
            second.append((color, offset, way, copy))

    for side in range(2):
        for color in range(2):
            near[color][side].wait_recv()
            spread_second(color, 3 if side == 0 else 1)

    def hand_on(color, offset, way, copy):
        copy.wait_recv()
        behind, onward = (3, 1) if way == 0 else (1, 3)
        origin = shift(color, offset, behind)
        send_piece(shift(color, 0, onward), origin, 2 * color + way, 1, number=2)

    for color in range(2):
        far[color].wait_recv()
        spread_second(color, 2)
    for way in range(2):
        for color in range(2):
            hand_on(color, 0, way, home[color][way])
    whole(tables_ref, 12, recv.at[1]).wait()
    params = cohort_order(tables_ref, table, plan_v, rank_ref)
    fund_levels(params, world_ref, level)
    tiles = 0
    for n, entry in enumerate(second):
        more = (TILES * (n + 1) // 10) // 2 * 2 - tiles if n < 10 else 0
        if more:
            build_tiles(tiles, more, table, level, weight_t, dwt, rows_t, acc_t)
            tiles += more
        hand_on(*entry)
    whole(blocks_ref, 4, recv.at[2]).wait()
    local[1].wait()
    whole(blocks_ref, 15, send.at[0]).wait()
    whole(tables_ref, 15, send.at[1]).wait()


def gather_outer(shocks, sigma, index, alloc, rows, world, rate):
    vmem = pl.BlockSpec(memory_space=pltpu.VMEM)
    arguments = (shocks, sigma[None], index.T, alloc.T, *rows, world, rate.T)
    out_shape = (
        pltpu.VMEM((NOUT, 4, 16, 512), BF16),
        pltpu.VMEM((TILES, 256, 256), BF16),
        pltpu.VMEM((TILES, 128, 128), F32),
        pltpu.VMEM((TILES, 8, 128), F32),
        pltpu.VMEM((TILES, 128), F32),
        pltpu.VMEM((GROUPS + 2, 6, 8, 128), F32),
        pltpu.VMEM((8, 384), jnp.int32),
        pltpu.VMEM((8, 256), F32),
    )
    return pl.pallas_call(
        gather_kernel,
        out_shape=out_shape,
        in_specs=[vmem] * len(arguments),
        out_specs=(vmem,) * len(out_shape),
        scratch_shapes=[
            pltpu.VMEM((4, 16, 512), BF16),
            pltpu.VMEM((2, 128), F32),
            pltpu.VMEM((16, 128), F32),
            pltpu.VMEM((NOUT, 2, 128), F32),
            pltpu.VMEM((2, 16, 128), F32),
            pltpu.VMEM((2, 128, 128), F32),
            pltpu.SemaphoreType.DMA((2,)),
            pltpu.SemaphoreType.DMA((MESSAGES,)),
            pltpu.SemaphoreType.DMA((2,)),
        ],
        compiler_params=pltpu.CompilerParams(
            collective_id=0, has_side_effects=True, vmem_limit_bytes=24 << 20
        ),
        name="gather_outer",
    )(*in_hbm(*arguments))


def value_kernel(
    blocks_ref,
    weight_t,
    dwt,
    rows_t,
    acc_t,
    dates,
    plan_v,
    rank_ref,
    out_ref,
    fmat,
    fmat_t,
    plan,
    sums_t,
    sens,
    sums_in,
    kerns,
    sem,
):
    copy = pltpu.make_async_copy(plan_v, plan, sem)
    copy.start()
    step_in = iota((8, 128), 0) % 4
    for j in range(TILES):
        sens[j] = jnp.zeros((2, 128, 128), F32)
        sums_t[j] = jnp.zeros((4, 8, 128), F32)

    for g in range(GROUPS):
        cols = slice(128 * g, 128 * g + 128)
        part = blocks_ref[:, g // 4, :, 128 * (g % 4) : 128 * (g % 4) + 128]
        part = part.astype(F32).reshape(16, 2, 8, 128)
        for m in range(2):
            one = part[:, m].reshape(128, 128)
            fmat[m, :, cols] = one.astype(BF16)
        fmat_t[cols, :] = part.reshape(256, 128).T.astype(BF16)
    fmat[:, :, 2048:] = jnp.zeros((2, 128, 256), BF16)
    fmat_t[2048:, :] = jnp.zeros((256, 256), BF16)
    copy.wait()

    def raw(i, half):
        here = pl.ds(pl.multiple_of(plan[1, i] * 128, 128), 256)
        sums_in[half] = dot(fmat_t[here, :], weight_t[plan[0, i]])

    def group(j, g, half, slot):
        def wide(k):
            return jnp.broadcast_to(rows_t[j, k : k + 1], (8, 128))

        hz = (step_in + (4 * g + 1)).astype(F32)
        decay = lax.exp2(wide(2) * hz + wide(3))
        decay = jnp.where((hz >= wide(0)) & (hz <= wide(1)), decay, 0.0)
        fee_power = lax.exp2(wide(4) * hz)
        fee_decay = fee_power * decay
        strike = wide(5)
        part = slice(128 * slot, 128 * slot + 128)
        for m in range(2):
            growth = fee_power * dates[g, 3 * m + 2]
            y = sums_in[half, part, 128 * m : 128 * m + 128].reshape(16, 8, 128) * growth
            up = lax.exp2(strike - y)
            more = 1.0 + up
            slope = up / more
            some = jnp.concatenate(
                [up[0:4] + up[4:8] + up[8:12], up[12:14] + up[14:16]], axis=0
            )
            many = jnp.concatenate(
                [more[0:4] * more[4:8] * more[8:12], more[12:14] * more[14:16]], axis=0
            )
            soft_sum = jnp.sum(jnp.where(some < 2.0**-12, some, jnp.log(many)), axis=0)
            kerns[half, m, part, :] = (fee_decay * slope).reshape(128, 128).astype(BF16)
            rho_sum = soft_sum + jnp.sum(slope * y, axis=0) * (1.0 / LOG2E)
            sums_t[j, 2 * m] += (decay * dates[g, 3 * m]) * soft_sum
            sums_t[j, 2 * m + 1] += (decay * dates[g, 3 * m + 1]) * rho_sum

    def flush(i, half):
        j = plan[0, i]
        here = pl.ds(pl.multiple_of(plan[1, i] * 128, 128), 256)
        for m in range(2):
            sens[j, m] += dot(fmat[m, :, here], kerns[half, m])

    def item_work(i, half):
        j, g = plan[0, i], plan[1, i]
        flush(jnp.maximum(i - 1, 0), 1 - half)
        raw(i + 1, 1 - half)
        group(j, g, half, 0)
        group(j, g + 1, half, 1)

    kerns[1] = jnp.zeros((2, 256, 128), BF16)
    raw(0, 0)

    def rounds(first, count, size):
        def work(n, carry):
            for k in range(size):
                item_work(first + size * n + k, k % 2)
            return carry

        lax.fori_loop(0, count, work, 0)

    items = plan[2, 0]
    full = items // UNROLL
    pairs = (items - UNROLL * full + 1) // 2
    rounds(0, full, UNROLL)
    rounds(UNROLL * full, pairs, 2)
    flush(UNROLL * full + 2 * pairs - 1, 1)

    def close(q, deltas):
        fresh = list(deltas)
        for k in range(4):
            j = 4 * q + k
            for m in range(2):
                fresh[m] = fresh[m] + dwt[j] * sens[j, m]
        return tuple(fresh)

    none = jnp.zeros((128, 128), F32)
    delta = lax.fori_loop(0, TILES // 4, close, (none, none))
    scale = acc_t[...] * (1.0 / 20.0 / 256.0)
    res_acc = []
    for n in range(4):
        value = jnp.sum(sums_t[:, n], axis=1)
        res_acc.append(value * (scale if n % 2 == 0 else -scale))

    rank_row = rank_ref[0:1, :]
    tile_row = jnp.floor(rank_row * 0.125)
    slot_row = rank_row - 8.0 * tile_row
    pick = (tile_row == iota((TILES, 256), 0).astype(F32)).astype(F32)
    keep = (slot_row == (iota((128, 256), 0) // 16).astype(F32)).astype(F32)
    for m in range(2):
        parts = []
        for n in range(2):
            lanes = dot01(res_acc[2 * m + n], pick, ((0,), (0,)), parts=2)
            parts.append(jnp.sum((lanes * keep).reshape(8, 16, 256), axis=0))
        down = delta[m].T.reshape(8, 16, 128)
        parts.append(jnp.sum(down, axis=0) * (-1.0 / 256.0))
        line = jnp.concatenate(parts, axis=1)
        for o in range(16):
            for k in range(5):
                r = (o % 2) * 10 + m * 5 + k
                out_ref[o // 2, r : r + 1, :] = line[o : o + 1, 128 * k : 128 * k + 128]
    for b in range(NIN):
        out_ref[b, 20:SLAB, :] = jnp.zeros((SLAB - 20, 128), F32)


def revalue(*tables):
    vmem = pl.BlockSpec(memory_space=pltpu.VMEM)
    return pl.pallas_call(
        value_kernel,
        out_shape=pltpu.VMEM((NIN, SLAB, 128), F32),
        in_specs=[vmem] * len(tables),
        out_specs=vmem,
        scratch_shapes=[
            pltpu.VMEM((2, 128, 2304), BF16),
            pltpu.VMEM((2304, 256), BF16),
            pltpu.SMEM((8, 384), jnp.int32),
            pltpu.VMEM((TILES, 4, 8, 128), F32),
            pltpu.VMEM((TILES, 2, 128, 128), F32),
            pltpu.VMEM((2, 256, 256), F32),
            pltpu.VMEM((2, 2, 256, 128), BF16),
            pltpu.SemaphoreType.DMA(()),
        ],
        compiler_params=pltpu.CompilerParams(vmem_limit_bytes=32 << 20),
        name="revalue",
    )(*in_vmem(*tables))


def scatter_kernel(slabs_ref, inbox, send, recv, own):
    me = lax.axis_index("inner")
    barrier = pltpu.get_barrier_semaphore()
    for d in range(1, NIN):
        pl.semaphore_signal(
            barrier, inc=1, device_id={"inner": lax.rem(me + d, NIN)}, device_id_type=MESH
        )
    local = pltpu.make_async_copy(slabs_ref.at[me], inbox.at[0], own)
    local.start()
    pl.semaphore_wait(barrier, NIN - 1)
    for d in (4, 3, 5, 2, 6, 7, 1):
        peer = lax.rem(me + d, NIN)
        pltpu.make_async_remote_copy(
            src_ref=slabs_ref.at[peer],
            dst_ref=inbox.at[d],
            send_sem=send,
            recv_sem=recv,
            device_id={"inner": peer},
            device_id_type=MESH,
        ).start()
    local.wait()
    view = inbox.at[pl.ds(0, NIN - 1)]
    pltpu.make_async_copy(view, view, recv).wait()
    pltpu.make_async_copy(view, view, send).wait()


def total_kernel(inbox_ref, res_ref, rho_ref, del_ref):
    total = inbox_ref[0]
    for d in range(1, NIN):
        total = total + inbox_ref[d]
    for o in range(2):
        for m in range(2):
            r = o * 10 + m * 5
            for k in range(2):
                lanes = slice(128 * k, 128 * k + 128)
                res_ref[o, m : m + 1, lanes] = total[r + k : r + k + 1]
                rho_ref[o, m : m + 1, lanes] = total[r + 2 + k : r + 3 + k]
            del_ref[o, m : m + 1, :] = total[r + 4 : r + 5]


def scatter_inner(slabs):
    vmem = pl.BlockSpec(memory_space=pltpu.VMEM)
    inbox = pl.pallas_call(
        scatter_kernel,
        out_shape=pltpu.VMEM((NIN, SLAB, 128), F32),
        in_specs=[vmem],
        out_specs=vmem,
        scratch_shapes=[
            pltpu.SemaphoreType.DMA(()),
            pltpu.SemaphoreType.DMA(()),
            pltpu.SemaphoreType.DMA(()),
        ],
        compiler_params=pltpu.CompilerParams(
            collective_id=1, has_side_effects=True, vmem_limit_bytes=8 << 20
        ),
        name="scatter_inner",
    )(*in_vmem(slabs))
    return pl.pallas_call(
        total_kernel,
        out_shape=(
            jax.ShapeDtypeStruct((2, 2, 256), F32),
            jax.ShapeDtypeStruct((2, 2, 256), F32),
            jax.ShapeDtypeStruct((2, 2, 128), F32),
        ),
        in_specs=[vmem],
        out_specs=(vmem, vmem, vmem),
        compiler_params=pltpu.CompilerParams(vmem_limit_bytes=8 << 20),
        name="total_inner",
    )(*in_vmem(inbox))


def shards(
    world_shocks,
    short_rate,
    inner_shocks,
    fund_volatility,
    fund_index,
    allocation,
    guarantee_type,
    maturity,
    guarantee_ratio,
    fee_rate,
    mortality,
    account,
):
    kinds = (guarantee_type, maturity, guarantee_ratio, fee_rate, mortality, account)
    rows = [value[None] for value in kinds]
    slabs = revalue(
        *gather_outer(
            inner_shocks,
            fund_volatility,
            fund_index,
            allocation,
            rows,
            world_shocks,
            short_rate,
        )
    )
    return scatter_inner(slabs)


def solution(mesh):
    return jax.shard_map(
        shards,
        mesh=mesh,
        in_specs=(
            P("outer", None, None),
            P("outer", None),
            P(None, "outer", "inner"),
            P("outer"),
            P("outer", None),
            P("outer", None),
            P("outer"),
            P("outer"),
            P("outer"),
            P("outer"),
            P("outer"),
            P("outer"),
        ),
        out_specs=(
            P(("outer", "inner"), None, None),
            P(("outer", "inner"), None, None),
            P(("outer", "inner"), None, None),
        ),
        check_vma=False,
    )
```
